32 devices in a mesh: dp: 8 (over y, x, core), mp: 4 (over z).
Axes of the slice: x: 2, y: 2, z: 4, core: 2. Of those that a mesh axis runs over, the one named last changes fastest.
Arguments:
- tokens: bfloat16 [8, 1024, 1536], P('dp', 'mp'), may hold values from -6 to 6
- attn_gain: bfloat16 [1536], P('dp'), may hold values from 0.5 to 1.5
- w_query: bfloat16 [1536, 1536], P('dp', 'mp'), may hold values from -0.5 to 0.5
- key_weight: bfloat16 [1536, 512], P('dp', 'mp'), may hold values from -0.5 to 0.5
- value_weight: bfloat16 [1536, 512], P('dp', 'mp'), may hold values from -0.15625 to 0.15625
- w_output: bfloat16 [1536, 1536], P('dp', 'mp'), may hold values from -1.75 to 1.75
- router: bfloat16 [1536, 24], P('dp'), may hold values from -0.078125 to 0.078125
- moe_gain: bfloat16 [1536], P('dp'), may hold values from 0.5 to 1.5
- w_in: bfloat16 [1536, 24, 2, 512], P('dp', None, None, 'mp'), may hold values from -0.15625 to 0.15625
- w_out: bfloat16 [1536, 24, 512], P('dp', None, 'mp'), may hold values from -5 to 5
- segments: int32 [8, 1024], P('dp'), may hold values from 0 to 7, never falling along the last dimension, each value on 1 to 512 neighbouring positions
- routes: int32 [8, 1024, 8], P('dp'), may hold values from 0 to 23, all different within a row; in each aligned block of 1024 rows (0 to 1023, 1024 to 2047, ..., all dimensions but the last counted through in order) at most 384 rows name the same one
- cotangent: bfloat16 [8, 1024, 1536], P('dp', 'mp'), may hold values from -6 to 6
Outputs:
- layer_out: bfloat16 [8, 1024, 1536], P('dp', 'mp')
- grad_tokens: float32 [8, 1024, 1536], P('dp', 'mp')
- grad_attn_gain: float32 [1536], P('dp')
- grad_query: float32 [1536, 1536], P('dp', 'mp')
- grad_key: float32 [1536, 512], P('dp', 'mp')
- grad_value: float32 [1536, 512], P('dp', 'mp')
- grad_output: float32 [1536, 1536], P('dp', 'mp')
- grad_router: float32 [1536, 24], P('dp')
- grad_moe_gain: float32 [1536], P('dp')
- grad_w_in: float32 [1536, 24, 2, 512], P('dp', None, None, 'mp')
- grad_w_out: float32 [1536, 24, 512], P('dp', None, 'mp')
The draws below stay inside these ranges and needn't reach their ends.
Inputs may be any that keep to these rules, and one draw needn't show every extreme that they name: `segments`: within a sequence segment numbers never fall; each document has 1 to 512 tokens, and one has exactly 512. `routes`: A token's 8 experts differ. Within one sequence at most 384 token-choice pairs name one expert, a bound that some block reaches.
All inputs are finite; a program needn't handle non-finite values.
Results may differ from the reference program's by a relative error of at most 0.025.
Values may be sent and summed in bfloat16 or wider, within the bound.
No kernel may reach another device: no remote copies, remote signals or barrier semaphores. Data moves between devices by JAX's collectives and lax.ppermute only.
A program may use at most 320 MiB of HBM per device.

```python
import math
import jax
import jax.numpy as jnp
import numpy as np
from jax import lax

MODEL_WIDTH = 1536
QUERY_HEADS = 24
KEY_VALUE_HEADS = 8
HEAD_SIZE = 64
EXPERTS = 24
FF = 512
TOP = 8
SEQUENCE_LENGTH = 1024
DOCS = 8
SEQS = 8
CAP = 384


def steps_of(stream_key, extent, pieces, least, largest):
    gain, own = 1.0, jax.random.fold_in(stream_key, 6)
    for axis_at, blocks in pieces:
        draws = jnp.exp(jax.random.uniform(jax.random.fold_in(own, axis_at), (blocks,), jnp.float32, least / len(pieces), largest / len(pieces)))
        gain = gain * jnp.repeat(draws, extent[axis_at] // blocks).reshape([-1 if axis == axis_at else 1 for axis in range(len(extent))])
    return gain


def profile(amount, total, reach, lean):
    portions = [(1 << 20) // math.isqrt(grade ** lean) + 1 for grade in range(2, amount + 1)]
    rest, counts = total - reach - (amount - 1), [1] * (amount - 1)
    while rest > 0:
        free = [i for i in range(amount - 1) if counts[i] < reach]
        mass, left = sum([portions[i] for i in free]), rest
        for i in free:
            addition = min(reach - counts[i], max(1, left * portions[i] // mass), rest)
            counts[i] = counts[i] + addition
            rest = rest - addition
    return np.array([reach] + counts)


def ragged(key, number_of, total, reach, lean):
    if number_of == 2:
        one = jax.random.randint(key, (), max(1, total - reach), min(reach, total - 1) + 1)
        return jnp.stack([one, total - one])
    tallies = jnp.asarray(profile(number_of, total, reach, lean), jnp.int32)
    couples = (number_of - 1) // 2
    giver, sink = tallies[1:1 + 2 * couples:2], tallies[2:2 + 2 * couples:2]
    margin = jnp.minimum(giver - 1, reach - sink)
    shifted = jax.random.randint(jax.random.fold_in(key, 1), (couples,), 0, 1 << 20) % (margin + 1)
    tallies = tallies.at[1:1 + 2 * couples:2].set(giver - shifted).at[2:2 + 2 * couples:2].set(sink + shifted)
    return tallies[jax.random.permutation(jax.random.fold_in(key, 2), number_of)]


def routed_block(rng, own, number, rows, number_of, top, bound, slope):
    ranking = jax.random.permutation(rng, number_of)
    crowded, ordinary = load_shares(number_of, rows * top, bound, slope, True), load_shares(number_of, rows * top, bound, slope, False)
    places = jnp.arange(number_of)

    def named(sizes, offset_by):
        used = int((sizes > 0).sum())
        fixed = max(1, used // 4)
        moved = fixed + (places - fixed + offset_by * (used - fixed)) % max(1, number_of - fixed)
        return jnp.zeros((number_of,), jnp.int32).at[ranking[jnp.where(places < fixed, places, moved)]].set(jnp.asarray(sizes, jnp.int32))

    sizes = jnp.where(number % 4 == 0, named(crowded, number // 4), named(ordinary, number - number // 4 - 1))
    mixed = jax.random.permutation(jax.random.fold_in(own, 3), number_of)
    source_of, taker = mixed[0:number_of // 2 * 2:2], mixed[1:number_of // 2 * 2:2]
    slack = jnp.minimum(sizes[source_of] - 1, bound - sizes[taker]) // 2
    slack = jnp.where((source_of == ranking[0]) | (taker == ranking[0]) | (sizes[taker] == 0), 0, jnp.maximum(slack, 0))
    moved = jax.random.randint(jax.random.fold_in(own, 4), (number_of // 2,), 0, 1 << 20) % (slack + 1)
    sizes = sizes.at[source_of].add(-moved).at[taker].add(moved)
    items = jnp.searchsorted(jnp.cumsum(sizes), jnp.arange(rows * top), side="right").astype(jnp.int32)
    listing = items.reshape(top, rows).T
    listing = listing[jax.random.permutation(jax.random.fold_in(own, 1), rows)]
    offset_by = jax.random.randint(jax.random.fold_in(own, 2), (rows, 1), 0, top)
    return jnp.take_along_axis(listing, (jnp.arange(top)[None, :] + offset_by) % top, axis=1)


def load_shares(number_of, total, limit, lean, full):
    weights = [(1 << 20) // math.isqrt(standing ** lean) + 1 for standing in range(1, number_of + 1)]
    largest = limit if full else min(limit, max(-(-total // number_of), total * weights[0] // sum(weights)))
    least = 1 if total - largest >= number_of - 1 else 0
    given, surplus = [largest] + [least] * (number_of - 1), total - largest - least * (number_of - 1)
    while surplus > 0:
        free = [i for i in range(1, number_of) if given[i] < largest] or [i for i in range(1, number_of) if given[i] < limit]
        pool, remaining = sum([weights[i] for i in free]), surplus
        for i in free:
            addition = min(limit - given[i], max(1, remaining * weights[i] // pool), surplus)
            given[i] = given[i] + addition
            surplus = surplus - addition
    return np.array(given)


def normal_values(own_key, extent, width, reach, shards=(), kind=jnp.bfloat16):
    array = width * jax.random.normal(own_key, extent, jnp.float32)
    if shards:
        array = array * steps_of(own_key, extent, shards, -0.22, 0.18)
    return jnp.clip(array, -reach, reach).astype(kind)


def setup_inputs(seed: int = 0) -> dict:
    streams_of = jax.random.split(jax.random.key(seed), 14)
    tokens = normal_values(streams_of[0], (SEQS, SEQUENCE_LENGTH, MODEL_WIDTH), 1.0, 6.0, ((0, 8), (1, 4)))
    attn_gain = jnp.clip(1.0 + 0.1 * jax.random.normal(streams_of[1], (MODEL_WIDTH,), jnp.float32), 0.5, 1.5).astype(jnp.bfloat16)
    w_query = normal_values(streams_of[2], (MODEL_WIDTH, QUERY_HEADS * HEAD_SIZE), (MODEL_WIDTH // 12) ** -0.5, 0.5, ((0, 8), (1, 4)))
    key_weight = normal_values(streams_of[3], (MODEL_WIDTH, KEY_VALUE_HEADS * HEAD_SIZE), (MODEL_WIDTH // 12) ** -0.5, 0.5, ((0, 8), (1, 4)))
    value_weight = normal_values(streams_of[4], (MODEL_WIDTH, KEY_VALUE_HEADS * HEAD_SIZE), MODEL_WIDTH ** -0.5, 0.15625, ((0, 8), (1, 4)))
    w_output = normal_values(streams_of[5], (MODEL_WIDTH, QUERY_HEADS * HEAD_SIZE), 0.3, 1.75, ((0, 8), (1, 4)))
    router = normal_values(streams_of[6], (MODEL_WIDTH, EXPERTS), 0.013, 0.078125, ((0, 8),))
    moe_gain = jnp.clip(1.0 + 0.1 * jax.random.normal(streams_of[7], (MODEL_WIDTH,), jnp.float32), 0.5, 1.5).astype(jnp.bfloat16)
    w_in = normal_values(streams_of[8], (MODEL_WIDTH, EXPERTS, 2, FF), MODEL_WIDTH ** -0.5, 0.15625, ((0, 8), (3, 4)))
    w_out = normal_values(streams_of[9], (MODEL_WIDTH, EXPERTS, FF), 0.8, 5.0, ((0, 8), (2, 4)))
    segments = jax.vmap(lambda own: jnp.searchsorted(jnp.cumsum(ragged(own, DOCS, SEQUENCE_LENGTH, SEQUENCE_LENGTH // 2, 2)), jnp.arange(SEQUENCE_LENGTH), side="right"))(jax.random.split(streams_of[10], SEQS)).reshape((SEQS, SEQUENCE_LENGTH)).astype(jnp.int32)
    routes_keys = jax.random.split(jax.random.fold_in(streams_of[11], 1), SEQS * SEQUENCE_LENGTH // SEQUENCE_LENGTH)
    routes_turns = jax.random.permutation(jax.random.fold_in(streams_of[11], 3), SEQS * SEQUENCE_LENGTH // SEQUENCE_LENGTH)
    routes = jax.vmap(lambda own, number: routed_block(jax.random.fold_in(streams_of[11], 2), own, number, SEQUENCE_LENGTH, EXPERTS, TOP, CAP, 1))(routes_keys, routes_turns).reshape((SEQS, SEQUENCE_LENGTH, TOP))
    cotangent = normal_values(streams_of[12], (SEQS, SEQUENCE_LENGTH, MODEL_WIDTH), 1.0, 6.0, ((0, 8), (1, 4)))
    return dict(tokens=tokens, attn_gain=attn_gain, w_query=w_query, key_weight=key_weight, value_weight=value_weight, w_output=w_output, router=router, moe_gain=moe_gain, w_in=w_in, w_out=w_out, segments=segments, routes=routes, cotangent=cotangent)


RESID = 0.22
ATTN_MULT = 0.015625
EPS = 1e-06
ROPE_BASE = 10000.0
NEG = -1e+30
HIGHEST = lax.Precision.HIGHEST

@jax.custom_vjp
def low(v):
    return lax.optimization_barrier(v.astype(jnp.bfloat16)).astype(jnp.float32)

@jax.custom_vjp
def low_back(v):
    return v

def low_keep(v):
    return (low(v), None)

def low_pass(kept, grad):
    return (grad,)

def back_keep(v):
    return (v, None)

def back_low(kept, grad):
    return (low(grad),)
low.defvjp(low_keep, low_pass)
low_back.defvjp(back_keep, back_low)

def precise_product(left, right):
    return jnp.dot(left, right, precision=HIGHEST, preferred_element_type=jnp.float32)

def norm_scale(values, gain_vec):
    return values * lax.rsqrt(lax.optimization_barrier(jnp.mean(values * values, -1, keepdims=True)) + EPS) * gain_vec

def apply_rotary(values, head_count):
    length = values.shape[0]
    shaped = values.reshape(length, head_count, HEAD_SIZE)
    half_size = HEAD_SIZE // 2
    frequency = ROPE_BASE ** (-jnp.arange(half_size).astype(jnp.float32) * 2.0 / HEAD_SIZE)
    angles = jnp.arange(length).astype(jnp.float32)[:, None] * frequency[None, :]
    cosine = jnp.cos(angles)[:, None, :]
    sine_part = jnp.sin(angles)[:, None, :]
    front_half = shaped[:, :, :half_size]
    back_half = shaped[:, :, half_size:]
    turned = jnp.concatenate([front_half * cosine - back_half * sine_part, back_half * cosine + front_half * sine_part], -1)
    return turned.reshape(length, head_count * HEAD_SIZE)

def dispatch(route_ids):
    flat_ids = route_ids.reshape(-1).astype(jnp.int32)
    onehot = (flat_ids[:, None] == jnp.arange(EXPERTS, dtype=jnp.int32)[None, :]).astype(jnp.int32)
    rank_of = lax.optimization_barrier(jnp.sum((jnp.cumsum(onehot, 0) - onehot) * onehot, 1))
    slot_of = (flat_ids * CAP + rank_of).astype(jnp.int32)
    slot_owner = jnp.full((EXPERTS * CAP,), SEQUENCE_LENGTH * TOP, jnp.int32).at[slot_of].set(jnp.arange(SEQUENCE_LENGTH * TOP, dtype=jnp.int32))
    return (slot_of, slot_owner)

def attend(query_rows, incoming_keys, incoming_values, doc_ids):
    rows_per_block = min(512, SEQUENCE_LENGTH)
    grouping_width = QUERY_HEADS // KEY_VALUE_HEADS
    blocks_of_queries = query_rows.reshape(SEQUENCE_LENGTH // rows_per_block, rows_per_block, KEY_VALUE_HEADS, grouping_width, HEAD_SIZE)
    heads_of_keys = incoming_keys.reshape(SEQUENCE_LENGTH, KEY_VALUE_HEADS, HEAD_SIZE)
    heads_of_values = incoming_values.reshape(SEQUENCE_LENGTH, KEY_VALUE_HEADS, HEAD_SIZE)
    positions = jnp.arange(SEQUENCE_LENGTH, dtype=jnp.int32)

    def one_block(block_item):
        query_block, row_start = block_item
        scores = low_back(ATTN_MULT * jnp.einsum('qgjd,kgd->gjqk', query_block, heads_of_keys, precision=HIGHEST))
        row_pos = row_start + jnp.arange(rows_per_block, dtype=jnp.int32)
        row_docs = lax.dynamic_slice_in_dim(doc_ids, row_start, rows_per_block)
        visible = (positions[None, :] <= row_pos[:, None]) & (doc_ids[None, :] == row_docs[:, None])
        probability = low(jax.nn.softmax(jnp.where(visible, scores, NEG), -1))
        return jnp.einsum('gjqk,kgd->qgjd', probability, heads_of_values, precision=HIGHEST).reshape(rows_per_block, QUERY_HEADS * HEAD_SIZE)
    starts = jnp.arange(SEQUENCE_LENGTH // rows_per_block, dtype=jnp.int32) * rows_per_block
    return lax.map(jax.checkpoint(one_block), (blocks_of_queries, starts)).reshape(SEQUENCE_LENGTH, QUERY_HEADS * HEAD_SIZE)

def seq_layer(weights, hidden_in, doc_ids, route_ids):
    attn_g, query_w, key_matrix, value_w, output_w, router_w, moe_g, in_w, out_w = weights
    attention_normed = low(norm_scale(hidden_in, attn_g))
    query_rows = low(apply_rotary(low_back(precise_product(attention_normed, query_w)), QUERY_HEADS))
    rotated_keys = low(apply_rotary(low_back(precise_product(attention_normed, key_matrix)), KEY_VALUE_HEADS))
    values_r = low(low_back(precise_product(attention_normed, value_w)))
    attended = low(low_back(attend(query_rows, rotated_keys, values_r, doc_ids)))
    attn_branch = low_back(precise_product(attended, output_w.T))
    middle = hidden_in + RESID * attn_branch
    normed_m = low(norm_scale(middle, moe_g))
    logits = precise_product(normed_m, router_w)
    chosen = route_ids[:, :, None] == jnp.arange(EXPERTS, dtype=jnp.int32)[None, None, :]
    picked = lax.optimization_barrier(jnp.sum(jnp.where(chosen, logits[:, None, :], 0.0), -1))
    gates = jax.nn.softmax(picked, -1)
    slot_of, slot_owner = dispatch(route_ids)
    table = slot_owner // TOP
    padded = jnp.concatenate([normed_m, jnp.zeros((1, MODEL_WIDTH), normed_m.dtype)], 0)
    dispatched = padded[table].reshape(EXPERTS, CAP, MODEL_WIDTH)
    gate_up = low_back(jnp.einsum('ecd,dejf->ecjf', dispatched, in_w, precision=HIGHEST))
    activated = low(jax.nn.silu(gate_up[:, :, 0]) * gate_up[:, :, 1])
    expert_out = low_back(jnp.einsum('ecf,def->ecd', activated, out_w, precision=HIGHEST))
    per_choice = expert_out.reshape(EXPERTS * CAP, MODEL_WIDTH)[slot_of].reshape(SEQUENCE_LENGTH, TOP, MODEL_WIDTH)
    moe_branch = low_back(lax.optimization_barrier(jnp.sum(gates[:, :, None] * per_choice, 1)))
    return middle + RESID * moe_branch

def reference(tokens, attn_gain, w_query, key_weight, value_weight, w_output, router, moe_gain, w_in, w_out, segments, routes, cotangent):
    weights = (attn_gain.astype(jnp.float32), w_query.astype(jnp.float32), key_weight.astype(jnp.float32), value_weight.astype(jnp.float32), w_output.astype(jnp.float32), router.astype(jnp.float32), moe_gain.astype(jnp.float32), w_in.astype(jnp.float32), w_out.astype(jnp.float32))
    tokens_f = tokens.astype(jnp.float32)

    def layer(weight_set, inputs):

        def step(carry, seq_item):
            hidden_in, doc_ids, route_ids = seq_item
            return (carry, jax.checkpoint(seq_layer)(weight_set, hidden_in, doc_ids, route_ids))
        unused, outputs = lax.scan(step, jnp.zeros((), jnp.float32), (inputs, segments, routes))
        return outputs
    outputs, backward = jax.vjp(layer, weights, tokens_f)
    weight_grads, token_grads = backward(cotangent.astype(jnp.float32))
    return (outputs.astype(jnp.bfloat16), token_grads, weight_grads[0], weight_grads[1], weight_grads[2], weight_grads[3], weight_grads[4], weight_grads[5], weight_grads[6], weight_grads[7], weight_grads[8])
```

```python
import functools

import jax
import jax.numpy as jnp
from jax import lax
from jax.experimental import pallas as pl
from jax.experimental.pallas import tpu as pltpu
from jax.sharding import Mesh
from jax.sharding import PartitionSpec as P

HEAD = 64
RESID = 0.22
ATTN_MULT = 0.015625
EPS = 1e-06
ROPE_BASE = 10000.0
NEG = -1e30
F32 = jnp.float32
BF16 = jnp.bfloat16
BLK = 256
VMEM_CAP = 60 * 1024 * 1024


def nt(left, right):
    return lax.dot_general(left, right, (((1,), (1,)), ((), ())), preferred_element_type=F32)


def tn(left, right):
    return lax.dot_general(left, right, (((0,), (0,)), ((), ())), preferred_element_type=F32)


def nn(left, right):
    return jnp.dot(left, right, preferred_element_type=F32)


def rope_cols(values, cosine, sine):
    lane = lax.broadcasted_iota(jnp.int32, cosine.shape, 1)
    low = (lane % HEAD) < (HEAD // 2)
    pieces = []
    for start in range(0, values.shape[1], 128):
        piece = values[:, start : start + 128]
        turned = jnp.where(low, pltpu.roll(piece, 96, 1), pltpu.roll(piece, 32, 1))
        pieces.append(piece * cosine + turned * sine)
    return pieces[0] if len(pieces) == 1 else jnp.concatenate(pieces, 1)


def seen(kc, i, kdoc_ref, qdoc, group):
    kdoc = kdoc_ref[pl.ds(pl.multiple_of(kc * BLK, BLK), BLK), :]
    kpos = kc * BLK + lax.broadcasted_iota(jnp.int32, (BLK, 1), 0)
    qpos = i * BLK + lax.broadcasted_iota(jnp.int32, (1, BLK), 1)
    visible = (kpos <= qpos) & (kdoc == qdoc)
    return jnp.where(visible, 0.0, NEG)


def attn_fwd_kernel(
    tok_ref, gain_ref, w_ref, cos_ref, sin_ref, kdoc_ref, qdoc_ref,
    na_ref, q_ref, k_ref, v_ref, att_ref, lse_ref, s_scr, *, q_heads, kv_heads,
):
    i = pl.program_id(0)
    group = q_heads // kv_heads
    tok = tok_ref[...].astype(F32)
    inv = lax.rsqrt(jnp.mean(tok * tok, -1, keepdims=True) + EPS)
    na = (tok * inv * gain_ref[...]).astype(BF16)
    na_ref[...] = na
    qkv = nn(na, w_ref[...])
    qk_cols = (q_heads + kv_heads) * HEAD
    roped = rope_cols(qkv[:, :qk_cols], cos_ref[...], sin_ref[...]).astype(BF16)
    vals = qkv[:, qk_cols:].astype(BF16)
    rows = pl.ds(pl.multiple_of(i * BLK, BLK), BLK)
    heads = [roped[:, h * HEAD : (h + 1) * HEAD] for h in range(q_heads + kv_heads)]
    for h in range(q_heads):
        q_ref[h] = heads[h]
    for g in range(kv_heads):
        k_ref[g, rows, :] = heads[q_heads + g]
        v_ref[g, rows, :] = vals[:, g * HEAD : (g + 1) * HEAD]
    lo = jnp.maximum(i - 2, 0)
    qdoc = qdoc_ref[...]
    for g in range(kv_heads):
        qs = jnp.concatenate(heads[g * group : (g + 1) * group], 0)

        def scores(kc, top, g=g, qs=qs):
            keys = k_ref[g, pl.ds(pl.multiple_of(kc * BLK, BLK), BLK), :]
            bias = seen(kc, i, kdoc_ref, qdoc, group)
            s = nt(keys, qs) * ATTN_MULT + jnp.concatenate([bias] * group, 1)
            s_scr[kc - lo] = s
            return jnp.maximum(top, jnp.max(s, 0, keepdims=True))

        top = lax.fori_loop(lo, i + 1, scores, jnp.full((1, group * BLK), NEG, F32))

        def mix(kc, carry, g=g, top=top):
            total, out = carry
            e = jnp.exp(s_scr[kc - lo] - top)
            vv = v_ref[g, pl.ds(pl.multiple_of(kc * BLK, BLK), BLK), :]
            return total + jnp.sum(e, 0, keepdims=True), out + tn(vv, e.astype(BF16))

        total, out = lax.fori_loop(
            lo, i + 1, mix, (jnp.zeros((1, group * BLK), F32), jnp.zeros((HEAD, group * BLK), F32))
        )
        out = out / total
        lse_ref[0, g : g + 1, :] = top + jnp.log(total)
        for j in range(group):
            h = g * group + j
            att_ref[:, h * HEAD : (h + 1) * HEAD] = out[:, j * BLK : (j + 1) * BLK].T.astype(BF16)


def attn_fwd(tokens, gain, pack, cosine, sine, kdoc, qdoc, q_heads, kv_heads):
    length, width = tokens.shape
    blocks = length // BLK
    cols = (q_heads + 2 * kv_heads) * HEAD
    group = q_heads // kv_heads
    fixed = lambda i: (0, 0)
    fixed3 = lambda i: (0, 0, 0)
    row = lambda i: (i, 0)
    return pl.pallas_call(
        functools.partial(attn_fwd_kernel, q_heads=q_heads, kv_heads=kv_heads),
        grid=(blocks,),
        in_specs=[
            pl.BlockSpec((BLK, width), row),
            pl.BlockSpec((1, width), fixed),
            pl.BlockSpec((width, cols), fixed),
            pl.BlockSpec((BLK, 128), row),
            pl.BlockSpec((BLK, 128), row),
            pl.BlockSpec((length, 1), fixed),
            pl.BlockSpec((1, BLK), lambda i: (0, i)),
        ],
        out_specs=[
            pl.BlockSpec((BLK, width), row),
            pl.BlockSpec((q_heads, BLK, HEAD), lambda i: (0, i, 0)),
            pl.BlockSpec((kv_heads, length, HEAD), fixed3),
            pl.BlockSpec((kv_heads, length, HEAD), fixed3),
            pl.BlockSpec((BLK, q_heads * HEAD), row),
            pl.BlockSpec((1, kv_heads, group * BLK), lambda i: (i, 0, 0)),
        ],
        out_shape=[
            jax.ShapeDtypeStruct((length, width), BF16),
            jax.ShapeDtypeStruct((q_heads, length, HEAD), BF16),
            jax.ShapeDtypeStruct((kv_heads, length, HEAD), BF16),
            jax.ShapeDtypeStruct((kv_heads, length, HEAD), BF16),
            jax.ShapeDtypeStruct((length, q_heads * HEAD), BF16),
            jax.ShapeDtypeStruct((blocks, kv_heads, group * BLK), F32),
        ],
        scratch_shapes=[pltpu.VMEM((3, BLK, group * BLK), F32)],
        compiler_params=pltpu.CompilerParams(
            dimension_semantics=("arbitrary",), vmem_limit_bytes=VMEM_CAP
        ),
        cost_estimate=pl.CostEstimate(
            flops=2 * length * width * cols + 8 * length * 768 * q_heads * HEAD,
            transcendentals=length * 640 * q_heads,
            bytes_accessed=4 * length * width + 2 * width * cols,
        ),
        name="attn_fwd",
    )(tokens, gain, pack, cosine, sine, kdoc, qdoc)


def attn_bwd_kernel(
    ag_ref, wo_ref, q_ref, k_ref, v_ref, att_ref, lse_ref, cos_ref, sin_ref, kdoc_ref, qdoc_ref,
    dq_ref, dkv_ref, dk_scr, dv_scr, *, q_heads, kv_heads,
):
    i = pl.program_id(0)
    group = q_heads // kv_heads

    @pl.when(i == 0)
    def _():
        dk_scr[...] = jnp.zeros_like(dk_scr)
        dv_scr[...] = jnp.zeros_like(dv_scr)

    do = nn(ag_ref[...], wo_ref[...]).astype(BF16)
    lo = jnp.maximum(i - 2, 0)
    qdoc = qdoc_ref[...]
    att = att_ref[...]
    dq_heads = []
    for g in range(kv_heads):
        span = range(g * group, (g + 1) * group)
        qs = jnp.concatenate([q_ref[h] for h in span], 0)
        dos = jnp.concatenate([do[:, h * HEAD : (h + 1) * HEAD] for h in span], 0)
        outs = jnp.concatenate([att[:, h * HEAD : (h + 1) * HEAD] for h in span], 0)
        dot_row = jnp.sum((dos.astype(F32) * outs.astype(F32)).T, 0, keepdims=True)
        lse = lse_ref[0, g : g + 1, :]

        def chunk(kc, dq, g=g, qs=qs, dos=dos, dot_row=dot_row, lse=lse):
            rows = pl.ds(pl.multiple_of(kc * BLK, BLK), BLK)
            keys = k_ref[g, rows, :]
            vals = v_ref[g, rows, :]
            bias = seen(kc, i, kdoc_ref, qdoc, group)
            s = nt(keys, qs) * ATTN_MULT + jnp.concatenate([bias] * group, 1)
            prob = jnp.exp(s - lse)
            dprob = nt(vals, dos)
            ds = (prob * (dprob - dot_row)).astype(BF16)
            dv_scr[g, rows, :] += nn(prob.astype(BF16), dos)
            dk_scr[g, rows, :] += nn(ds, qs)
            return dq + tn(keys, ds)

        dq = lax.fori_loop(lo, i + 1, chunk, jnp.zeros((HEAD, group * BLK), F32))
        for j in range(group):
            dq_heads.append(dq[:, j * BLK : (j + 1) * BLK].T)
    rows = pl.ds(pl.multiple_of(i * BLK, BLK), BLK)
    dq_all = jnp.concatenate(dq_heads, 1) * ATTN_MULT
    dq_ref[...] = rope_cols(dq_all, cos_ref[rows, :], -sin_ref[rows, :]).astype(BF16)

    @pl.when(i == pl.num_programs(0) - 1)
    def _():
        dk = jnp.concatenate([dk_scr[g] for g in range(kv_heads)], 1) * ATTN_MULT
        kcols = kv_heads * HEAD
        dkv_ref[:, :kcols] = rope_cols(dk, cos_ref[...], -sin_ref[...]).astype(BF16)
        dkv_ref[:, kcols:] = jnp.concatenate([dv_scr[g] for g in range(kv_heads)], 1).astype(BF16)


def attn_bwd(ag, wo, q, k, v, att, lse, cosine, sine, kdoc, qdoc):
    length, width = ag.shape
    q_heads, kv_heads = q.shape[0], k.shape[0]
    blocks = length // BLK
    group = q_heads // kv_heads
    fixed = lambda i: (0, 0)
    fixed3 = lambda i: (0, 0, 0)
    row = lambda i: (i, 0)
    return pl.pallas_call(
        functools.partial(attn_bwd_kernel, q_heads=q_heads, kv_heads=kv_heads),
        grid=(blocks,),
        in_specs=[
            pl.BlockSpec((BLK, width), row),
            pl.BlockSpec((width, q_heads * HEAD), fixed),
            pl.BlockSpec((q_heads, BLK, HEAD), lambda i: (0, i, 0)),
            pl.BlockSpec((kv_heads, length, HEAD), fixed3),
            pl.BlockSpec((kv_heads, length, HEAD), fixed3),
            pl.BlockSpec((BLK, q_heads * HEAD), row),
            pl.BlockSpec((1, kv_heads, group * BLK), lambda i: (i, 0, 0)),
            pl.BlockSpec((length, 128), fixed),
            pl.BlockSpec((length, 128), fixed),
            pl.BlockSpec((length, 1), fixed),
            pl.BlockSpec((1, BLK), lambda i: (0, i)),
        ],
        out_specs=[
            pl.BlockSpec((BLK, q_heads * HEAD), row),
            pl.BlockSpec((length, 2 * kv_heads * HEAD), fixed),
        ],
        out_shape=[
            jax.ShapeDtypeStruct((length, q_heads * HEAD), BF16),
            jax.ShapeDtypeStruct((length, 2 * kv_heads * HEAD), BF16),
        ],
        scratch_shapes=[
            pltpu.VMEM((kv_heads, length, HEAD), F32),
            pltpu.VMEM((kv_heads, length, HEAD), F32),
        ],
        compiler_params=pltpu.CompilerParams(
            dimension_semantics=("arbitrary",), vmem_limit_bytes=VMEM_CAP
        ),
        cost_estimate=pl.CostEstimate(
            flops=2 * length * width * q_heads * HEAD + 20 * length * 768 * q_heads * HEAD,
            transcendentals=length * 640 * q_heads,
            bytes_accessed=2 * length * width + 2 * width * q_heads * HEAD,
        ),
        name="attn_bwd",
    )(ag, wo, q, k, v, att, lse, cosine, sine, kdoc, qdoc)


def mid_kernel(
    att_ref, wo_ref, tok_ref, gain_ref, small_ref, routes_ref, mid_ref, nm_ref, gate_ref, *, experts
):
    branch = nt(att_ref[0], wo_ref[0])
    for m in range(1, att_ref.shape[0]):
        branch += nt(att_ref[m], wo_ref[m])
    middle = tok_ref[...].astype(F32) + RESID * branch
    mid_ref[...] = middle
    inv = lax.rsqrt(jnp.mean(middle * middle, -1, keepdims=True) + EPS)
    nm = (middle * inv * gain_ref[...]).astype(BF16)
    nm_ref[...] = nm
    logits = nn(nm, small_ref[...])
    lane = lax.broadcasted_iota(jnp.int32, logits.shape, 1)
    chosen = lane == routes_ref[:, 0:1]
    for c in range(1, routes_ref.shape[1]):
        chosen = chosen | (lane == routes_ref[:, c : c + 1])
    logits = jnp.where(chosen, logits, NEG)
    e = jnp.exp(logits - jnp.max(logits, -1, keepdims=True))
    gate_ref[...] = e / jnp.sum(e, -1, keepdims=True)


def mid_fwd(att_all, wo_all, tokens, gain, pack, small_at, routes, experts):
    length, width = tokens.shape
    parts, _, cols = att_all.shape
    blocks = length // BLK
    fixed = lambda i: (0, 0)
    row = lambda i: (i, 0)
    return pl.pallas_call(
        functools.partial(mid_kernel, experts=experts),
        grid=(blocks,),
        in_specs=[
            pl.BlockSpec((parts, BLK, cols), lambda i: (0, i, 0)),
            pl.BlockSpec((parts, width, cols), lambda i: (0, 0, 0)),
            pl.BlockSpec((BLK, width), row),
            pl.BlockSpec((1, width), fixed),
            pl.BlockSpec((width, 128), lambda i: (0, small_at)),
            pl.BlockSpec((BLK, routes.shape[1]), row),
        ],
        out_specs=[
            pl.BlockSpec((BLK, width), row),
            pl.BlockSpec((BLK, width), row),
            pl.BlockSpec((BLK, 128), row),
        ],
        out_shape=[
            jax.ShapeDtypeStruct((length, width), F32),
            jax.ShapeDtypeStruct((length, width), BF16),
            jax.ShapeDtypeStruct((length, 128), F32),
        ],
        compiler_params=pltpu.CompilerParams(
            dimension_semantics=("arbitrary",), vmem_limit_bytes=VMEM_CAP
        ),
        cost_estimate=pl.CostEstimate(
            flops=2 * length * width * cols * parts,
            transcendentals=length * 128,
            bytes_accessed=10 * length * width + 2 * width * cols * parts,
        ),
        name="mid_fwd",
    )(att_all, wo_all, tokens, gain, pack, routes)


def gate_cols(gates, first):
    lane = lax.broadcasted_iota(jnp.int32, gates.shape, 1)
    return [
        jnp.sum(jnp.where(lane == first + k, gates, 0.0), -1, keepdims=True) for k in range(2)
    ]


def moe_fwd_kernel(base_ref, x_ref, w_ref, gate_ref, h_ref, gact_ref):
    p = pl.program_id(1)
    h = nn(x_ref[...], w_ref[...])
    h_ref[...] = h.astype(BF16)
    cols = gate_cols(gate_ref[...], base_ref[0] + 2 * p)
    for k in range(2):
        gate = h[:, 256 * k : 256 * k + 128]
        up = h[:, 256 * k + 128 : 256 * k + 256]
        act = gate * jax.nn.sigmoid(gate) * up
        gact_ref[:, 128 * k : 128 * k + 128] = (cols[k] * act).astype(BF16)


def moe_fwd(base, x, w_in, gates, rows):
    length, width = x.shape
    cols = w_in.shape[1]
    return pl.pallas_call(
        moe_fwd_kernel,
        grid_spec=pltpu.PrefetchScalarGridSpec(
            num_scalar_prefetch=1,
            grid=(length // rows, cols // 512),
            in_specs=[
                pl.BlockSpec((rows, width), lambda i, p, b: (i, 0)),
                pl.BlockSpec((width, 512), lambda i, p, b: (0, p)),
                pl.BlockSpec((rows, 128), lambda i, p, b: (i, 0)),
            ],
            out_specs=[
                pl.BlockSpec((rows, 512), lambda i, p, b: (i, p)),
                pl.BlockSpec((rows, 256), lambda i, p, b: (i, p)),
            ],
        ),
        out_shape=[
            jax.ShapeDtypeStruct((length, cols), BF16),
            jax.ShapeDtypeStruct((length, cols // 2), BF16),
        ],
        compiler_params=pltpu.CompilerParams(
            dimension_semantics=("arbitrary", "arbitrary"), vmem_limit_bytes=VMEM_CAP
        ),
        cost_estimate=pl.CostEstimate(
            flops=2 * length * width * cols,
            transcendentals=length * cols // 2,
            bytes_accessed=2 * length * (width + cols + cols // 2) + 4 * width * cols,
        ),
        name="moe_fwd",
    )(base, x, w_in, gates)


def moe_bwd_kernel(base_ref, g_ref, w_ref, gate_ref, h_ref, gug_ref, choice_ref):
    p = pl.program_id(1)
    first = base_ref[0] + 2 * p
    plain = nn(g_ref[...], w_ref[...])
    cols = gate_cols(gate_ref[...], first)

    @pl.when(p == 0)
    def _():
        choice_ref[...] = jnp.zeros_like(choice_ref)

    lane = lax.broadcasted_iota(jnp.int32, choice_ref.shape, 1)
    add = jnp.zeros(choice_ref.shape, F32)
    for k in range(2):
        gate = h_ref[:, 256 * k : 256 * k + 128].astype(F32)
        up = h_ref[:, 256 * k + 128 : 256 * k + 256].astype(F32)
        part = plain[:, 128 * k : 128 * k + 128]
        sig = jax.nn.sigmoid(gate)
        silu = gate * sig
        add = jnp.where(lane == first + k, jnp.sum(silu * up * part, -1, keepdims=True), add)
        act_grad = cols[k] * part
        gug_ref[:, 256 * k : 256 * k + 128] = (
            act_grad * up * sig * (1.0 + gate * (1.0 - sig))
        ).astype(BF16)
        gug_ref[:, 256 * k + 128 : 256 * k + 256] = (act_grad * silu).astype(BF16)
    choice_ref[...] += add


def moe_bwd(base, g, w_out, gates, h, rows):
    length, width = g.shape
    cols = h.shape[1]
    return pl.pallas_call(
        moe_bwd_kernel,
        grid_spec=pltpu.PrefetchScalarGridSpec(
            num_scalar_prefetch=1,
            grid=(length // rows, cols // 512),
            in_specs=[
                pl.BlockSpec((rows, width), lambda i, p, b: (i, 0)),
                pl.BlockSpec((width, 256), lambda i, p, b: (0, p)),
                pl.BlockSpec((rows, 128), lambda i, p, b: (i, 0)),
                pl.BlockSpec((rows, 512), lambda i, p, b: (i, p)),
            ],
            out_specs=[
                pl.BlockSpec((rows, 512), lambda i, p, b: (i, p)),
                pl.BlockSpec((rows, 128), lambda i, p, b: (i, 0)),
            ],
        ),
        out_shape=[
            jax.ShapeDtypeStruct((length, cols), BF16),
            jax.ShapeDtypeStruct((length, 128), F32),
        ],
        compiler_params=pltpu.CompilerParams(
            dimension_semantics=("arbitrary", "arbitrary"), vmem_limit_bytes=VMEM_CAP
        ),
        cost_estimate=pl.CostEstimate(
            flops=length * width * cols,
            transcendentals=length * cols // 2,
            bytes_accessed=2 * length * (width + 2 * cols) + 2 * width * cols,
        ),
        name="moe_bwd",
    )(base, g, w_out, gates, h)


def swap(value, axis, bit, size):
    return lax.ppermute(value, axis, [(i, i ^ bit) for i in range(size)])


def reorder(value, q, quads):
    if quads != 4:
        return value
    n = value.shape[-1] // 4
    b = [value[..., k * n : (k + 1) * n] for k in range(4)]
    odd = (q & 1) == 1
    far = (q & 2) == 2
    c = [jnp.where(odd, b[k ^ 1], b[k]) for k in range(4)]
    return jnp.concatenate([jnp.where(far, c[k ^ 2], c[k]) for k in range(4)], -1)


def gather_rows(value, quads):
    if quads != 4:
        return lax.all_gather(value, "q", axis=0, tiled=True)
    half = value.shape[0] // 2
    from_x = swap(value, "q", 1, 4)
    from_y = swap(value, "q", 2, 4)
    diag_a = swap(from_x[:half], "q", 2, 4)
    diag_b = swap(from_y[half:], "q", 1, 4)
    return jnp.concatenate([value, from_x, from_y, diag_a, diag_b], 0)


def scatter_rows(value, quads):
    if quads != 4:
        return lax.psum_scatter(value, "q", scatter_dimension=0, tiled=True).astype(F32)
    n = value.shape[0] // 4
    half = n // 2
    own, to_x, to_y, diag = (value[k * n : (k + 1) * n] for k in range(4))
    via_x = swap(diag[:half], "q", 1, 4)
    via_y = swap(diag[half:], "q", 2, 4)
    to_y = jnp.concatenate([(to_y[:half].astype(F32) + via_x.astype(F32)).astype(BF16), to_y[half:]], 0)
    to_x = jnp.concatenate([to_x[:half], (to_x[half:].astype(F32) + via_y.astype(F32)).astype(BF16)], 0)
    from_x = swap(to_x, "q", 1, 4)
    from_y = swap(to_y, "q", 2, 4)
    return own.astype(F32) + from_x.astype(F32) + from_y.astype(F32)


def both_cores(mine, c):
    other = swap(mine, "c", 1, 2)
    first = c == 0
    return jnp.concatenate([jnp.where(first, mine, other), jnp.where(first, other, mine)], 0)


def body(
    tokens, attn_gain, w_query, key_weight, value_weight, w_output, router, moe_gain, w_in, w_out,
    segments, routes, cotangent, *, quads,
):
    q = lax.axis_index("q")
    c = lax.axis_index("c")
    length = segments.shape[1]
    width = tokens.shape[2]
    rows = w_query.shape[0]
    experts = router.shape[1]
    half_e = experts // 2
    ff = w_out.shape[2]
    q_heads = w_query.shape[1] // HEAD
    kv_heads = key_weight.shape[1] // HEAD
    q_cols, kv_cols = q_heads * HEAD, kv_heads * HEAD
    qkv_cols = q_cols + 2 * kv_cols
    mp = lax.axis_size("mp")

    doc_row = segments
    doc_col = segments.reshape(length, 1)
    lane = jnp.arange(128, dtype=jnp.int32) % (HEAD // 2)
    freq = ROPE_BASE ** (-lane.astype(F32) * 2.0 / HEAD)
    angles = jnp.arange(length).astype(F32)[:, None] * freq[None, :]
    cosine = jnp.cos(angles)
    upper = (jnp.arange(128, dtype=jnp.int32) % HEAD) < (HEAD // 2)
    sine = jnp.where(upper[None, :], -jnp.sin(angles), jnp.sin(angles))

    tok_own = reorder(tokens[0], q, quads)
    cot_own = reorder(cotangent[0], q, quads)
    tok_all = lax.all_gather(tok_own, "mp", axis=0, tiled=True)

    pad = jnp.zeros((rows, 128 - experts - 2), BF16)
    pack = jnp.concatenate(
        [w_query, key_weight, value_weight, router, attn_gain[:, None], moe_gain[:, None], pad], 1
    )
    pack = gather_rows(both_cores(pack, c), quads)
    small_at = qkv_cols // 128
    gains = pack[:, qkv_cols + experts : qkv_cols + experts + 2].astype(F32)
    attn_g = gains[:, 0].reshape(1, width)
    moe_g = gains[:, 1].reshape(1, width)
    wo_pieces = lax.all_gather(w_output, "mp", axis=0, tiled=False)
    wo_pieces = wo_pieces.transpose(1, 0, 2).reshape(rows, mp * q_cols)
    wo_rows = gather_rows(both_cores(wo_pieces, c), quads)
    wo_all = wo_rows.reshape(width, mp, q_cols).transpose(1, 0, 2)

    in_halves = w_in.reshape(rows, 2, half_e * 2 * ff)
    out_halves = w_out.reshape(rows, 2, half_e * ff)

    def half_rows(halves):
        mine = lax.dynamic_index_in_dim(halves, c, 1, keepdims=False)
        give = lax.dynamic_index_in_dim(halves, 1 - c, 1, keepdims=False)
        other = swap(give, "c", 1, 2)
        first = c == 0
        return jnp.concatenate([jnp.where(first, mine, other), jnp.where(first, other, mine)], 0)

    in_full = gather_rows(half_rows(in_halves), quads)
    out_full = gather_rows(half_rows(out_halves), quads)

    normed_a, q_r, k_r, v_r, attended, lse = attn_fwd(
        tok_all, attn_g, pack, cosine, sine, doc_col, doc_row, q_heads, kv_heads
    )
    att_all = lax.all_gather(attended, "mp", axis=0, tiled=False)
    middle, normed_m, gates = mid_fwd(
        att_all, wo_all, tok_all, moe_g, pack, small_at, routes[0], experts
    )

    x2 = jnp.concatenate([normed_m, swap(normed_m, "c", 1, 2)], 0)
    gates2 = jnp.concatenate([gates, swap(gates, "c", 1, 2)], 0)
    base = (c * half_e).astype(jnp.int32).reshape(1)
    hidden, gact = moe_fwd(base, x2, in_full, gates2, length)

    moe_grad = (RESID * cot_own.astype(F32)).astype(BF16)
    grad_all = lax.all_gather(moe_grad, "mp", axis=0, tiled=True)
    g2 = jnp.concatenate([grad_all, swap(grad_all, "c", 1, 2)], 0)
    gug, choice2 = moe_bwd(base, g2, out_full, gates2, hidden, length)

    back2 = nt(gug, in_full).astype(BF16)
    back_other = swap(back2[length:], "c", 1, 2)
    choice = choice2[:length] + swap(choice2[length:], "c", 1, 2)
    gates_c = gates * choice
    logit_grad = (gates_c - gates * jnp.sum(gates_c, -1, keepdims=True)).astype(BF16)
    router_all = pack[:, small_at * 128 :]
    normed_m_grad = (
        back2[:length].astype(F32) + back_other.astype(F32) + nt(logit_grad, router_all)
    ).astype(BF16)
    m_grad = lax.psum_scatter(normed_m_grad, "mp", scatter_dimension=0, tiled=True).astype(F32)

    combined2 = nt(gact, out_full).astype(BF16)
    comb_other = swap(combined2[length:], "c", 1, 2)
    combined = (combined2[:length].astype(F32) + comb_other.astype(F32)).astype(BF16)
    moe_branch = lax.psum_scatter(combined, "mp", scatter_dimension=0, tiled=True).astype(F32)

    own_at = lax.axis_index("mp") * (length // mp)
    middle_own = lax.dynamic_slice_in_dim(middle, own_at, length // mp, 0)
    layer_out = (middle_own + RESID * moe_branch).astype(BF16)

    in_part = tn(x2, gug).astype(BF16)
    out_part = tn(g2, gact).astype(BF16)
    in_sum = scatter_rows(in_part, quads).astype(BF16)
    out_sum = scatter_rows(out_part, quads).astype(BF16)

    def own_rows(total):
        mine = lax.dynamic_slice_in_dim(total, c * rows, rows, 0)
        give = lax.dynamic_slice_in_dim(total, (1 - c) * rows, rows, 0)
        other = swap(give, "c", 1, 2)
        first = c == 0
        return jnp.concatenate([jnp.where(first, mine, other), jnp.where(first, other, mine)], 1)

    grad_in = own_rows(in_sum).astype(F32)
    grad_out = own_rows(out_sum).astype(F32)

    inv_m = lax.rsqrt(jnp.mean(middle_own * middle_own, -1, keepdims=True) + EPS)
    scaled = m_grad * moe_g
    middle_grad = cot_own.astype(F32) + inv_m * (
        scaled - middle_own * inv_m * inv_m * jnp.mean(scaled * middle_own, -1, keepdims=True)
    )
    attn_grad = (RESID * middle_grad).astype(BF16)
    ag_all = lax.all_gather(attn_grad, "mp", axis=0, tiled=True)

    wo_own = lax.dynamic_index_in_dim(wo_all, lax.axis_index("mp"), 0, keepdims=False)
    dq, dkv = attn_bwd(ag_all, wo_own, q_r, k_r, v_r, attended, lse, cosine, sine, doc_col, doc_row)
    normed_a_grad = nt(dq, pack[:, :q_cols]) + nt(dkv, pack[:, q_cols:qkv_cols])
    a_grad = lax.psum_scatter(
        normed_a_grad.astype(BF16), "mp", scatter_dimension=0, tiled=True
    ).astype(F32)
    tok_f = tok_own.astype(F32)
    inv_a = lax.rsqrt(jnp.mean(tok_f * tok_f, -1, keepdims=True) + EPS)
    scaled = a_grad * attn_g
    grad_tokens = middle_grad + inv_a * (
        scaled - tok_f * inv_a * inv_a * jnp.mean(scaled * tok_f, -1, keepdims=True)
    )

    parts = jnp.concatenate(
        [
            tn(normed_a, dq).astype(BF16),
            tn(normed_a, dkv).astype(BF16),
            tn(ag_all, attended).astype(BF16),
            tn(normed_m, logit_grad).astype(BF16),
        ],
        1,
    )
    cols = parts.shape[1]
    by_core = parts.reshape(width // (2 * rows), 2, rows, cols)
    mine = lax.dynamic_index_in_dim(by_core, c, 1, keepdims=False)
    give = lax.dynamic_index_in_dim(by_core, 1 - c, 1, keepdims=False)
    pair = (mine.astype(F32) + swap(give, "c", 1, 2).astype(F32)).astype(BF16)
    sums = scatter_rows(pair.reshape(width // 2, cols), quads)
    grad_query = sums[:, :q_cols]
    grad_kv = sums[:, q_cols:qkv_cols]
    grad_output = sums[:, qkv_cols : qkv_cols + q_cols]
    router_part = sums[:, qkv_cols + q_cols : qkv_cols + q_cols + experts]

    attn_gain_part = (
        jnp.sum(grad_query * w_query.astype(F32), 1)
        + jnp.sum(grad_kv[:, :kv_cols] * key_weight.astype(F32), 1)
        + jnp.sum(grad_kv[:, kv_cols:] * value_weight.astype(F32), 1)
    ) / attn_gain.astype(F32)
    moe_gain_part = (
        jnp.sum(grad_in * w_in.reshape(rows, -1).astype(F32), 1)
        + jnp.sum(router_part * router.astype(F32), 1)
    ) / moe_gain.astype(F32)
    tiny = jnp.concatenate([router_part, attn_gain_part[:, None], moe_gain_part[:, None]], 1)
    total = tiny
    for k in range(1, mp):
        total = total + lax.ppermute(tiny, "mp", [(i, (i + k) % mp) for i in range(mp)])

    return (
        reorder(layer_out, q, quads)[None],
        reorder(grad_tokens, q, quads)[None],
        total[:, experts],
        grad_query,
        grad_kv[:, :kv_cols],
        grad_kv[:, kv_cols:],
        grad_output,
        total[:, :experts],
        total[:, experts + 1],
        grad_in.reshape(w_in.shape),
        grad_out.reshape(w_out.shape),
    )


def solution(mesh):
    dp, mp = mesh.shape["dp"], mesh.shape["mp"]
    quads = dp // 2
    split = Mesh(mesh.devices.reshape(quads, 2, mp), ("q", "c", "mp"))
    d = ("q", "c")
    placed = (
        P(d, "mp", None),
        P(d),
        P(d, "mp"),
        P(d, "mp"),
        P(d, "mp"),
        P(d, "mp"),
        P(d, None),
        P(d),
        P(d, None, None, "mp"),
        P(d, None, "mp"),
        P(d, None),
        P(d, None, None),
        P(d, "mp", None),
    )
    return jax.shard_map(
        functools.partial(body, quads=quads),
        mesh=split,
        in_specs=placed,
        out_specs=(
            P(d, "mp", None),
            P(d, "mp", None),
            P(d),
            P(d, "mp"),
            P(d, "mp"),
            P(d, "mp"),
            P(d, "mp"),
            P(d, None),
            P(d),
            P(d, None, None, "mp"),
            P(d, None, "mp"),
        ),
        check_vma=False,
    )
```

```python
import functools

import jax
import jax.numpy as jnp
from jax import lax
from jax.experimental import pallas as pl
from jax.experimental.pallas import tpu as pltpu
from jax.sharding import Mesh
from jax.sharding import PartitionSpec as P

HEAD = 64
RESID = 0.22
ATTN_MULT = 0.015625
EPS = 1e-06
ROPE_BASE = 10000.0
NEG = -1e30
F32 = jnp.float32
BF16 = jnp.bfloat16
BLK = 256
VMEM_CAP = 60 * 1024 * 1024


def nt(left, right):
    return lax.dot_general(left, right, (((1,), (1,)), ((), ())), preferred_element_type=F32)


def tn(left, right):
    return lax.dot_general(left, right, (((0,), (0,)), ((), ())), preferred_element_type=F32)


def nn(left, right):
    return jnp.dot(left, right, preferred_element_type=F32)


def cost(flops, transcendentals, bytes_accessed, scale=1):
    return pl.CostEstimate(
        flops=flops // scale,
        transcendentals=transcendentals // scale,
        bytes_accessed=bytes_accessed // scale,
    )


def rope_cols(values, cosine, sine):
    lane = lax.broadcasted_iota(jnp.int32, cosine.shape, 1)
    low = (lane % HEAD) < (HEAD // 2)
    pieces = []
    for start in range(0, values.shape[1], 128):
        piece = values[:, start : start + 128]
        turned = jnp.where(low, pltpu.roll(piece, 96, 1), pltpu.roll(piece, 32, 1))
        pieces.append(piece * cosine + turned * sine)
    return pieces[0] if len(pieces) == 1 else jnp.concatenate(pieces, 1)


def seen(kc, i, kdoc_ref, qdoc, group):
    kdoc = kdoc_ref[pl.ds(pl.multiple_of(kc * BLK, BLK), BLK), :]
    kpos = kc * BLK + lax.broadcasted_iota(jnp.int32, (BLK, 1), 0)
    qpos = i * BLK + lax.broadcasted_iota(jnp.int32, (1, BLK), 1)
    visible = (kpos <= qpos) & (kdoc == qdoc)
    return jnp.where(visible, 0.0, NEG)


def attn_fwd_kernel(
    tok_ref, gain_ref, w_ref, cos_ref, sin_ref, kdoc_ref, qdoc_ref,
    na_ref, q_ref, k_ref, v_ref, att_ref, lse_ref, s_scr, *, q_heads, kv_heads,
):
    i = pl.program_id(0)
    group = q_heads // kv_heads
    tok = tok_ref[...].astype(F32)
    inv = lax.rsqrt(jnp.mean(tok * tok, -1, keepdims=True) + EPS)
    na = (tok * inv * gain_ref[...]).astype(BF16)
    na_ref[...] = na
    qkv = nn(na, w_ref[...])
    qk_cols = (q_heads + kv_heads) * HEAD
    roped = rope_cols(qkv[:, :qk_cols], cos_ref[...], sin_ref[...]).astype(BF16)
    vals = qkv[:, qk_cols:].astype(BF16)
    rows = pl.ds(pl.multiple_of(i * BLK, BLK), BLK)
    heads = [roped[:, h * HEAD : (h + 1) * HEAD] for h in range(q_heads + kv_heads)]
    for h in range(q_heads):
        q_ref[h] = heads[h]
    for g in range(kv_heads):
        k_ref[g, rows, :] = heads[q_heads + g]
        v_ref[g, rows, :] = vals[:, g * HEAD : (g + 1) * HEAD]
    lo = jnp.maximum(i - 2, 0)
    qdoc = qdoc_ref[...]
    for g in range(kv_heads):
        qs = jnp.concatenate(heads[g * group : (g + 1) * group], 0)

        def scores(kc, top, g=g, qs=qs):
            keys = k_ref[g, pl.ds(pl.multiple_of(kc * BLK, BLK), BLK), :]
            bias = seen(kc, i, kdoc_ref, qdoc, group)
            s = nt(keys, qs) * ATTN_MULT + jnp.concatenate([bias] * group, 1)
            s_scr[kc - lo] = s
            return jnp.maximum(top, jnp.max(s, 0, keepdims=True))

        top = lax.fori_loop(lo, i + 1, scores, jnp.full((1, group * BLK), NEG, F32))

        def mix(kc, carry, g=g, top=top):
            total, out = carry
            e = jnp.exp(s_scr[kc - lo] - top)
            vv = v_ref[g, pl.ds(pl.multiple_of(kc * BLK, BLK), BLK), :]
            return total + jnp.sum(e, 0, keepdims=True), out + tn(vv, e.astype(BF16))

        total, out = lax.fori_loop(
            lo, i + 1, mix, (jnp.zeros((1, group * BLK), F32), jnp.zeros((HEAD, group * BLK), F32))
        )
        out = out / total
        lse_ref[0, g : g + 1, :] = top + jnp.log(total)
        for j in range(group):
            h = g * group + j
            att_ref[:, h * HEAD : (h + 1) * HEAD] = out[:, j * BLK : (j + 1) * BLK].T.astype(BF16)


def attn_fwd(tokens, gain, pack, cosine, sine, kdoc, qdoc, q_heads, kv_heads):
    length, width = tokens.shape
    blocks = length // BLK
    cols = (q_heads + 2 * kv_heads) * HEAD
    group = q_heads // kv_heads
    fixed = lambda i: (0, 0)
    fixed3 = lambda i: (0, 0, 0)
    row = lambda i: (i, 0)
    return pl.pallas_call(
        functools.partial(attn_fwd_kernel, q_heads=q_heads, kv_heads=kv_heads),
        grid=(blocks,),
        in_specs=[
            pl.BlockSpec((BLK, width), row),
            pl.BlockSpec((1, width), fixed),
            pl.BlockSpec((width, cols), fixed),
            pl.BlockSpec((BLK, 128), row),
            pl.BlockSpec((BLK, 128), row),
            pl.BlockSpec((length, 1), fixed),
            pl.BlockSpec((1, BLK), lambda i: (0, i)),
        ],
        out_specs=[
            pl.BlockSpec((BLK, width), row),
            pl.BlockSpec((q_heads, BLK, HEAD), lambda i: (0, i, 0)),
            pl.BlockSpec((kv_heads, length, HEAD), fixed3),
            pl.BlockSpec((kv_heads, length, HEAD), fixed3),
            pl.BlockSpec((BLK, q_heads * HEAD), row),
            pl.BlockSpec((1, kv_heads, group * BLK), lambda i: (i, 0, 0)),
        ],
        out_shape=[
            jax.ShapeDtypeStruct((length, width), BF16),
            jax.ShapeDtypeStruct((q_heads, length, HEAD), BF16),
            jax.ShapeDtypeStruct((kv_heads, length, HEAD), BF16),
            jax.ShapeDtypeStruct((kv_heads, length, HEAD), BF16),
            jax.ShapeDtypeStruct((length, q_heads * HEAD), BF16),
            jax.ShapeDtypeStruct((blocks, kv_heads, group * BLK), F32),
        ],
        scratch_shapes=[pltpu.VMEM((3, BLK, group * BLK), F32)],
        compiler_params=pltpu.CompilerParams(
            dimension_semantics=("arbitrary",), vmem_limit_bytes=VMEM_CAP
        ),
        cost_estimate=cost(
            flops=2 * length * width * cols + 8 * length * 768 * q_heads * HEAD,
            transcendentals=length * 640 * q_heads,
            bytes_accessed=4 * length * width + 2 * width * cols,
            scale=100,
        ),
        name="attn_fwd",
    )(tokens, gain, pack, cosine, sine, kdoc, qdoc)


def attn_bwd_kernel(
    do_ref, q_ref, k_ref, v_ref, att_ref, lse_ref, cos_ref, sin_ref, kdoc_ref, qdoc_ref,
    dq_ref, dkv_ref, dk_scr, dv_scr, *, q_heads, kv_heads,
):
    i = pl.program_id(0)
    group = q_heads // kv_heads

    @pl.when(i == 0)
    def _():
        dk_scr[...] = jnp.zeros_like(dk_scr)
        dv_scr[...] = jnp.zeros_like(dv_scr)

    do = do_ref[...]
    lo = jnp.maximum(i - 2, 0)
    qdoc = qdoc_ref[...]
    att = att_ref[...]
    dq_heads = []
    for g in range(kv_heads):
        span = range(g * group, (g + 1) * group)
        qs = jnp.concatenate([q_ref[h] for h in span], 0)
        dos = jnp.concatenate([do[:, h * HEAD : (h + 1) * HEAD] for h in span], 0)
        outs = jnp.concatenate([att[:, h * HEAD : (h + 1) * HEAD] for h in span], 0)
        dot_row = jnp.sum((dos.astype(F32) * outs.astype(F32)).T, 0, keepdims=True)
        lse = lse_ref[0, g : g + 1, :]

        def chunk(kc, dq, g=g, qs=qs, dos=dos, dot_row=dot_row, lse=lse):
            rows = pl.ds(pl.multiple_of(kc * BLK, BLK), BLK)
            keys = k_ref[g, rows, :]
            vals = v_ref[g, rows, :]
            bias = seen(kc, i, kdoc_ref, qdoc, group)
            s = nt(keys, qs) * ATTN_MULT + jnp.concatenate([bias] * group, 1)
            prob = jnp.exp(s - lse)
            dprob = nt(vals, dos)
            ds = (prob * (dprob - dot_row)).astype(BF16)
            dv_scr[g, rows, :] += nn(prob.astype(BF16), dos)
            dk_scr[g, rows, :] += nn(ds, qs)
            return dq + tn(keys, ds)

        dq = lax.fori_loop(lo, i + 1, chunk, jnp.zeros((HEAD, group * BLK), F32))
        for j in range(group):
            dq_heads.append(dq[:, j * BLK : (j + 1) * BLK].T)
    rows = pl.ds(pl.multiple_of(i * BLK, BLK), BLK)
    dq_all = jnp.concatenate(dq_heads, 1) * ATTN_MULT
    dq_ref[...] = rope_cols(dq_all, cos_ref[rows, :], -sin_ref[rows, :]).astype(BF16)

    @pl.when(i == pl.num_programs(0) - 1)
    def _():
        dk = jnp.concatenate([dk_scr[g] for g in range(kv_heads)], 1) * ATTN_MULT
        kcols = kv_heads * HEAD
        dkv_ref[:, :kcols] = rope_cols(dk, cos_ref[...], -sin_ref[...]).astype(BF16)
        dkv_ref[:, kcols:] = jnp.concatenate([dv_scr[g] for g in range(kv_heads)], 1).astype(BF16)


def attn_bwd(do, q, k, v, att, lse, cosine, sine, kdoc, qdoc):
    length = do.shape[0]
    q_heads, kv_heads = q.shape[0], k.shape[0]
    blocks = length // BLK
    group = q_heads // kv_heads
    fixed = lambda i: (0, 0)
    fixed3 = lambda i: (0, 0, 0)
    row = lambda i: (i, 0)
    return pl.pallas_call(
        functools.partial(attn_bwd_kernel, q_heads=q_heads, kv_heads=kv_heads),
        grid=(blocks,),
        in_specs=[
            pl.BlockSpec((BLK, q_heads * HEAD), row),
            pl.BlockSpec((q_heads, BLK, HEAD), lambda i: (0, i, 0)),
            pl.BlockSpec((kv_heads, length, HEAD), fixed3),
            pl.BlockSpec((kv_heads, length, HEAD), fixed3),
            pl.BlockSpec((BLK, q_heads * HEAD), row),
            pl.BlockSpec((1, kv_heads, group * BLK), lambda i: (i, 0, 0)),
            pl.BlockSpec((length, 128), fixed),
            pl.BlockSpec((length, 128), fixed),
            pl.BlockSpec((length, 1), fixed),
            pl.BlockSpec((1, BLK), lambda i: (0, i)),
        ],
        out_specs=[
            pl.BlockSpec((BLK, q_heads * HEAD), row),
            pl.BlockSpec((length, 2 * kv_heads * HEAD), fixed),
        ],
        out_shape=[
            jax.ShapeDtypeStruct((length, q_heads * HEAD), BF16),
            jax.ShapeDtypeStruct((length, 2 * kv_heads * HEAD), BF16),
        ],
        scratch_shapes=[
            pltpu.VMEM((kv_heads, length, HEAD), F32),
            pltpu.VMEM((kv_heads, length, HEAD), F32),
        ],
        compiler_params=pltpu.CompilerParams(
            dimension_semantics=("arbitrary",), vmem_limit_bytes=VMEM_CAP
        ),
        cost_estimate=cost(
            flops=20 * length * 768 * q_heads * HEAD,
            transcendentals=length * 640 * q_heads,
            bytes_accessed=8 * length * q_heads * HEAD,
        ),
        name="attn_bwd",
    )(do, q, k, v, att, lse, cosine, sine, kdoc, qdoc)


def mid_kernel(
    att_ref, wo_ref, tok_ref, gain_ref, small_ref, routes_ref, mid_ref, nm_ref, gate_ref, flat_ref
):
    att = jnp.concatenate([att_ref[k] for k in range(att_ref.shape[0])], 1)
    flat_ref[...] = att
    branch = nt(att, wo_ref[...])
    middle = tok_ref[...].astype(F32) + RESID * branch
    mid_ref[...] = middle
    inv = lax.rsqrt(jnp.mean(middle * middle, -1, keepdims=True) + EPS)
    nm = (middle * inv * gain_ref[...]).astype(BF16)
    nm_ref[...] = nm
    logits = nn(nm, small_ref[...])
    lane = lax.broadcasted_iota(jnp.int32, logits.shape, 1)
    chosen = lane == routes_ref[:, 0:1]
    for c in range(1, routes_ref.shape[1]):
        chosen = chosen | (lane == routes_ref[:, c : c + 1])
    logits = jnp.where(chosen, logits, NEG)
    e = jnp.exp(logits - jnp.max(logits, -1, keepdims=True))
    gate_ref[...] = e / jnp.sum(e, -1, keepdims=True)


def mid_fwd(att_all, wo_rows, tokens, gain, pack, small_at, routes):
    length, width = tokens.shape
    parts, _, cols = att_all.shape
    blocks = length // BLK
    fixed = lambda i: (0, 0)
    row = lambda i: (i, 0)
    return pl.pallas_call(
        mid_kernel,
        grid=(blocks,),
        in_specs=[
            pl.BlockSpec((parts, BLK, cols), lambda i: (0, i, 0)),
            pl.BlockSpec((width, parts * cols), fixed),
            pl.BlockSpec((BLK, width), row),
            pl.BlockSpec((1, width), fixed),
            pl.BlockSpec((width, 128), lambda i: (0, small_at)),
            pl.BlockSpec((BLK, routes.shape[1]), row),
        ],
        out_specs=[
            pl.BlockSpec((BLK, width), row),
            pl.BlockSpec((BLK, width), row),
            pl.BlockSpec((BLK, 128), row),
            pl.BlockSpec((BLK, parts * cols), row),
        ],
        out_shape=[
            jax.ShapeDtypeStruct((length, width), F32),
            jax.ShapeDtypeStruct((length, width), BF16),
            jax.ShapeDtypeStruct((length, 128), F32),
            jax.ShapeDtypeStruct((length, parts * cols), BF16),
        ],
        compiler_params=pltpu.CompilerParams(
            dimension_semantics=("arbitrary",), vmem_limit_bytes=VMEM_CAP
        ),
        cost_estimate=cost(
            flops=2 * length * width * cols * parts,
            transcendentals=length * 128,
            bytes_accessed=10 * length * width + 2 * width * cols * parts,
            scale=100,
        ),
        name="mid_fwd",
    )(att_all, wo_rows, tokens, gain, pack, routes)


def norm_back(n_grad, values, gain):
    inv = lax.rsqrt(jnp.mean(values * values, -1, keepdims=True) + EPS)
    scaled = n_grad * gain
    return inv * (scaled - values * (inv * inv) * jnp.mean(scaled * values, -1, keepdims=True))


def back_mid_kernel(
    own_ref, back_ref, recv_ref, lg_ref, small_ref, mid_ref, gain_ref, cot_ref, wo_ref, ag_ref, p_ref
):
    n_grad = back_ref[...].astype(F32) + recv_ref[...].astype(F32) + nt(lg_ref[...], small_ref[...])
    grad = norm_back(n_grad, mid_ref[...], gain_ref[...])
    own = (pl.program_id(0) == own_ref[0]).astype(F32)
    ag = (RESID * (grad + own * cot_ref[...].astype(F32))).astype(BF16)
    ag_ref[...] = ag
    out = nn(ag, wo_ref[...]).astype(BF16)
    cols = p_ref.shape[2]
    for k in range(p_ref.shape[0]):
        p_ref[k] = out[:, k * cols : (k + 1) * cols]


def back_mid(own, back, recv, logit_grad, pack, small_at, middle, gain, cot, wo_rows, parts):
    length, width = middle.shape
    blocks = length // BLK
    cols = wo_rows.shape[1] // parts
    fixed = lambda i, o: (0, 0)
    row = lambda i, o: (i, 0)
    return pl.pallas_call(
        back_mid_kernel,
        grid_spec=pltpu.PrefetchScalarGridSpec(
            num_scalar_prefetch=1,
            grid=(blocks,),
            in_specs=[
                pl.BlockSpec((BLK, width), row),
                pl.BlockSpec((BLK, width), row),
                pl.BlockSpec((BLK, 128), row),
                pl.BlockSpec((width, 128), lambda i, o: (0, small_at)),
                pl.BlockSpec((BLK, width), row),
                pl.BlockSpec((1, width), fixed),
                pl.BlockSpec((BLK, width), fixed),
                pl.BlockSpec((width, parts * cols), fixed),
            ],
            out_specs=[
                pl.BlockSpec((BLK, width), row),
                pl.BlockSpec((parts, BLK, cols), lambda i, o: (0, i, 0)),
            ],
        ),
        out_shape=[
            jax.ShapeDtypeStruct((length, width), BF16),
            jax.ShapeDtypeStruct((parts, length, cols), BF16),
        ],
        compiler_params=pltpu.CompilerParams(
            dimension_semantics=("arbitrary",), vmem_limit_bytes=VMEM_CAP
        ),
        cost_estimate=cost(
            flops=2 * length * width * cols * parts,
            transcendentals=0,
            bytes_accessed=12 * length * width + 2 * width * cols * parts,
        ),
        name="back_mid",
    )(own, back, recv, logit_grad, pack, middle, gain, cot, wo_rows)


def back_end_kernel(dq_ref, dkv_ref, w_ref, tok_ref, gain_ref, ag_ref, out_ref):
    d_all = jnp.concatenate([dq_ref[...], dkv_ref[...]], 1)
    n_grad = nt(d_all, w_ref[...])
    grad = norm_back(n_grad, tok_ref[...].astype(F32), gain_ref[...])
    out_ref[...] = (grad + ag_ref[...].astype(F32) * (1.0 / RESID)).astype(BF16)


def back_end(dq, dkv, pack, tokens, gain, ag):
    length, width = tokens.shape
    cols = dq.shape[1] + dkv.shape[1]
    fixed = lambda i: (0, 0)
    row = lambda i: (i, 0)
    return pl.pallas_call(
        back_end_kernel,
        grid=(length // BLK,),
        in_specs=[
            pl.BlockSpec((BLK, dq.shape[1]), row),
            pl.BlockSpec((BLK, dkv.shape[1]), row),
            pl.BlockSpec((width, cols), fixed),
            pl.BlockSpec((BLK, width), row),
            pl.BlockSpec((1, width), fixed),
            pl.BlockSpec((BLK, width), row),
        ],
        out_specs=pl.BlockSpec((BLK, width), row),
        out_shape=jax.ShapeDtypeStruct((length, width), BF16),
        compiler_params=pltpu.CompilerParams(
            dimension_semantics=("arbitrary",), vmem_limit_bytes=VMEM_CAP
        ),
        cost_estimate=cost(
            flops=2 * length * width * cols,
            transcendentals=0,
            bytes_accessed=6 * length * width + 2 * width * cols,
        ),
        name="back_end",
    )(dq, dkv, pack, tokens, gain, ag)


def gate_cols(gates, first):
    lane = lax.broadcasted_iota(jnp.int32, gates.shape, 1)
    return [
        jnp.sum(jnp.where(lane == first + k, gates, 0.0), -1, keepdims=True) for k in range(2)
    ]


def moe_fwd_kernel(base_ref, x_ref, w_ref, gate_ref, h_ref, gact_ref):
    p = pl.program_id(1)
    h = nn(x_ref[...], w_ref[...])
    h_ref[...] = h.astype(BF16)
    cols = gate_cols(gate_ref[...], base_ref[0] + 2 * p)
    for k in range(2):
        gate = h[:, 256 * k : 256 * k + 128]
        up = h[:, 256 * k + 128 : 256 * k + 256]
        act = gate * jax.nn.sigmoid(gate) * up
        gact_ref[:, 128 * k : 128 * k + 128] = (cols[k] * act).astype(BF16)


def moe_fwd(base, x, w_in, gates, rows):
    length, width = x.shape
    cols = w_in.shape[1]
    return pl.pallas_call(
        moe_fwd_kernel,
        grid_spec=pltpu.PrefetchScalarGridSpec(
            num_scalar_prefetch=1,
            grid=(length // rows, cols // 512),
            in_specs=[
                pl.BlockSpec((rows, width), lambda i, p, b: (i, 0)),
                pl.BlockSpec((width, 512), lambda i, p, b: (0, p)),
                pl.BlockSpec((rows, 128), lambda i, p, b: (i, 0)),
            ],
            out_specs=[
                pl.BlockSpec((rows, 512), lambda i, p, b: (i, p)),
                pl.BlockSpec((rows, 256), lambda i, p, b: (i, p)),
            ],
        ),
        out_shape=[
            jax.ShapeDtypeStruct((length, cols), BF16),
            jax.ShapeDtypeStruct((length, cols // 2), BF16),
        ],
        compiler_params=pltpu.CompilerParams(
            dimension_semantics=("arbitrary", "arbitrary"), vmem_limit_bytes=VMEM_CAP
        ),
        cost_estimate=cost(
            flops=2 * length * width * cols,
            transcendentals=length * cols // 2,
            bytes_accessed=2 * length * (width + cols + cols // 2) + 4 * width * cols,
            scale=100,
        ),
        name="moe_fwd",
    )(base, x, w_in, gates)


def moe_bwd_kernel(base_ref, g_ref, w_ref, gate_ref, h_ref, gug_ref, choice_ref):
    p = pl.program_id(1)
    first = base_ref[0] + 2 * p
    plain = nn(g_ref[...], w_ref[...])
    cols = gate_cols(gate_ref[...], first)

    @pl.when(p == 0)
    def _():
        choice_ref[...] = jnp.zeros_like(choice_ref)

    lane = lax.broadcasted_iota(jnp.int32, choice_ref.shape, 1)
    add = jnp.zeros(choice_ref.shape, F32)
    for k in range(2):
        gate = h_ref[:, 256 * k : 256 * k + 128].astype(F32)
        up = h_ref[:, 256 * k + 128 : 256 * k + 256].astype(F32)
        part = plain[:, 128 * k : 128 * k + 128]
        sig = jax.nn.sigmoid(gate)
        silu = gate * sig
        add = jnp.where(lane == first + k, jnp.sum(silu * up * part, -1, keepdims=True), add)
        act_grad = cols[k] * part
        gug_ref[:, 256 * k : 256 * k + 128] = (
            act_grad * up * sig * (1.0 + gate * (1.0 - sig))
        ).astype(BF16)
        gug_ref[:, 256 * k + 128 : 256 * k + 256] = (act_grad * silu).astype(BF16)
    choice_ref[...] += add


def moe_bwd(base, g, w_out, gates, h, rows):
    length, width = g.shape
    cols = h.shape[1]
    return pl.pallas_call(
        moe_bwd_kernel,
        grid_spec=pltpu.PrefetchScalarGridSpec(
            num_scalar_prefetch=1,
            grid=(length // rows, cols // 512),
            in_specs=[
                pl.BlockSpec((rows, width), lambda i, p, b: (i, 0)),
                pl.BlockSpec((width, 256), lambda i, p, b: (0, p)),
                pl.BlockSpec((rows, 128), lambda i, p, b: (i, 0)),
                pl.BlockSpec((rows, 512), lambda i, p, b: (i, p)),
            ],
            out_specs=[
                pl.BlockSpec((rows, 512), lambda i, p, b: (i, p)),
                pl.BlockSpec((rows, 128), lambda i, p, b: (i, 0)),
            ],
        ),
        out_shape=[
            jax.ShapeDtypeStruct((length, cols), BF16),
            jax.ShapeDtypeStruct((length, 128), F32),
        ],
        compiler_params=pltpu.CompilerParams(
            dimension_semantics=("arbitrary", "arbitrary"), vmem_limit_bytes=VMEM_CAP
        ),
        cost_estimate=cost(
            flops=length * width * cols,
            transcendentals=length * cols // 2,
            bytes_accessed=2 * length * (width + 2 * cols) + 2 * width * cols,
        ),
        name="moe_bwd",
    )(base, g, w_out, gates, h)


def tn_pair_kernel(left_ref, left2_ref, right_ref, right2_ref, out_ref):
    out_ref[...] = (tn(left_ref[...], right_ref[...]) + tn(left2_ref[...], right2_ref[...])).astype(BF16)


def tn_pair(left, left2, right, right2):
    length, width = left.shape
    cols = right.shape[1]
    tall, wide = width // 2, 512
    return pl.pallas_call(
        tn_pair_kernel,
        grid=(width // tall, cols // wide),
        in_specs=[
            pl.BlockSpec((length, tall), lambda i, j: (0, i)),
            pl.BlockSpec((length, tall), lambda i, j: (0, i)),
            pl.BlockSpec((length, wide), lambda i, j: (0, j)),
            pl.BlockSpec((length, wide), lambda i, j: (0, j)),
        ],
        out_specs=pl.BlockSpec((tall, wide), lambda i, j: (i, j)),
        out_shape=jax.ShapeDtypeStruct((width, cols), BF16),
        compiler_params=pltpu.CompilerParams(
            dimension_semantics=("arbitrary", "arbitrary"), vmem_limit_bytes=VMEM_CAP
        ),
        cost_estimate=cost(
            flops=4 * length * width * cols,
            transcendentals=0,
            bytes_accessed=4 * length * (width + 2 * cols),
            scale=100,
        ),
        name="weight_grad",
    )(left, left2, right, right2)


def swap(value, axis, bit, size):
    return lax.ppermute(value, axis, [(i, i ^ bit) for i in range(size)])


def reorder(value, q, quads):
    if quads != 4:
        return value
    n = value.shape[-1] // 4
    b = [value[..., k * n : (k + 1) * n] for k in range(4)]
    odd = (q & 1) == 1
    far = (q & 2) == 2
    c = [jnp.where(odd, b[k ^ 1], b[k]) for k in range(4)]
    return jnp.concatenate([jnp.where(far, c[k ^ 2], c[k]) for k in range(4)], -1)


def gather_first(value, quads):
    if quads != 4:
        return (lax.all_gather(value, "q", axis=0, tiled=True),)
    half = value.shape[0] // 2
    return swap(value[:half], "q", 1, 4), swap(value[half:], "q", 2, 4)


def gather_rest(value, quads):
    if quads != 4:
        return ()
    half = value.shape[0] // 2
    return swap(value[half:], "q", 1, 4), swap(value[:half], "q", 2, 4)


def gather_last(value, first, rest, quads):
    if quads != 4:
        return first[0]
    diag_a = swap(first[0], "q", 2, 4)
    diag_b = swap(first[1], "q", 1, 4)
    return jnp.concatenate([value, first[0], rest[0], rest[1], first[1], diag_a, diag_b], 0)


def gather_rows(value, quads):
    return gather_last(value, gather_first(value, quads), gather_rest(value, quads), quads)


def scatter_first(value, quads):
    if quads != 4:
        return (value,)
    n = value.shape[0] // 8
    part = [value[k * n : (k + 1) * n] for k in range(8)]
    from_x = swap(jnp.concatenate([part[2], part[6]], 0), "q", 1, 4)
    from_y = swap(jnp.concatenate([part[5], part[7]], 0), "q", 2, 4)
    return value, from_x, from_y


def scatter_second(first, quads):
    if quads != 4:
        return lax.psum_scatter(first[0], "q", scatter_dimension=0, tiled=True).astype(F32)
    value, from_x, from_y = first
    n = value.shape[0] // 8
    give_y = (value[4 * n : 5 * n].astype(F32) + from_x[n:].astype(F32)).astype(BF16)
    give_x = (value[3 * n : 4 * n].astype(F32) + from_y[n:].astype(F32)).astype(BF16)
    give_x, give_y = lax.optimization_barrier((give_x, give_y))
    low = swap(give_y, "q", 2, 4)
    high = swap(give_x, "q", 1, 4)
    value, from_x, from_y = all_after((value, from_x, from_y), low, high)
    return jnp.concatenate(
        [
            value[:n].astype(F32) + from_x[:n].astype(F32) + low.astype(F32),
            value[n : 2 * n].astype(F32) + from_y[:n].astype(F32) + high.astype(F32),
        ],
        0,
    )


def scatter_rows(value, quads):
    return scatter_second(scatter_first(value, quads), quads)


def after(value, *others):
    return lax.optimization_barrier((value, *others))[0]


def all_after(values, *others):
    return lax.optimization_barrier((*values, *others))[: len(values)]


def to_halves(mine, give, c):
    other = swap(give, "c", 1, 2)
    first = c == 0
    return jnp.concatenate([jnp.where(first, mine, other), jnp.where(first, other, mine)], 0)


def from_halves(total, rows, c):
    mine = lax.dynamic_slice_in_dim(total, c * rows, rows, 0)
    give = lax.dynamic_slice_in_dim(total, (1 - c) * rows, rows, 0)
    other = swap(give, "c", 1, 2)
    first = c == 0
    return jnp.where(first, mine, other), jnp.where(first, other, mine), mine, other


def column_halves(value, c):
    n = value.shape[1] // 2
    mine = jnp.where(c == 0, value[:, :n], value[:, n:])
    give = jnp.where(c == 0, value[:, n:], value[:, :n])
    return mine, give


def whole_columns(half, c):
    other = swap(half, "c", 1, 2)
    return jnp.where(c == 0, half, other), jnp.where(c == 0, other, half)


def body(
    tokens, attn_gain, w_query, key_weight, value_weight, w_output, router, moe_gain, w_in, w_out,
    segments, routes, cotangent, *, quads,
):
    q = lax.axis_index("q")
    c = lax.axis_index("c")
    m = lax.axis_index("mp")
    length = segments.shape[1]
    width = tokens.shape[2]
    rows = w_query.shape[0]
    experts = router.shape[1]
    half_e = experts // 2
    ff = w_out.shape[2]
    q_heads = w_query.shape[1] // HEAD
    kv_heads = key_weight.shape[1] // HEAD
    q_cols, kv_cols = q_heads * HEAD, kv_heads * HEAD
    qkv_cols = q_cols + 2 * kv_cols
    mp = lax.axis_size("mp")

    tok_own = reorder(tokens[0], q, quads)
    tok_all = lax.all_gather(tok_own, "mp", axis=0, tiled=True)

    pad = jnp.zeros((rows, 128 - experts - 2), BF16)
    pack = jnp.concatenate(
        [w_query, key_weight, value_weight, router, attn_gain[:, None], moe_gain[:, None], pad], 1
    )
    pack_pair = to_halves(*column_halves(pack, c), c)
    pack_first = gather_first(pack_pair, quads)
    pack_half = gather_last(pack_pair, pack_first, gather_rest(pack_pair, quads), quads)
    pack = jnp.concatenate(whole_columns(pack_half, c), 1)
    small_at = qkv_cols // 128
    gains = pack[:, qkv_cols + experts : qkv_cols + experts + 2].astype(F32)
    attn_g = gains[:, 0].reshape(1, width)
    moe_g = gains[:, 1].reshape(1, width)

    doc_row = segments
    doc_col = segments.reshape(length, 1)
    lane = jnp.arange(128, dtype=jnp.int32) % (HEAD // 2)
    freq = ROPE_BASE ** (-lane.astype(F32) * 2.0 / HEAD)
    angles = jnp.arange(length).astype(F32)[:, None] * freq[None, :]
    cosine = jnp.cos(angles)
    upper = (jnp.arange(128, dtype=jnp.int32) % HEAD) < (HEAD // 2)
    sine = jnp.where(upper[None, :], -jnp.sin(angles), jnp.sin(angles))

    def half_rows(value):
        mine = lax.dynamic_slice_in_dim(value, c * half_e, half_e, 1).reshape(rows, -1)
        give = lax.dynamic_slice_in_dim(value, (1 - c) * half_e, half_e, 1).reshape(rows, -1)
        return to_halves(mine, give, c), mine, give

    in_pair, in_kept, in_gave = half_rows(after(w_in, pack_pair))
    out_pair, _, _ = half_rows(after(w_out, in_pair))
    in_src = after(in_pair, *pack_first)
    in_got = gather_first(in_src, quads)
    in_rest = gather_rest(after(in_src, *in_got), quads)

    normed_a, q_r, k_r, v_r, attended, lse = attn_fwd(
        tok_all, attn_g, after(pack, *in_got), cosine, sine, doc_col, doc_row, q_heads, kv_heads
    )

    wo_pad = jnp.concatenate([w_output, jnp.zeros((rows, 5 * 64), BF16)], 1)
    wo_cols = lax.all_gather(after(wo_pad, tok_all, pack), "mp", axis=0, tiled=False)
    wo_cols = jnp.concatenate([wo_cols[j, :, :q_cols] for j in range(mp)], 1)
    wo_pair = to_halves(*column_halves(after(wo_cols, attended), c), c)
    in_full = gather_last(in_pair, in_got, in_rest, quads)
    wo_src = after(wo_pair, in_full)
    wo_got, wo_rest = gather_first(wo_src, quads), gather_rest(wo_src, quads)
    out_src = after(out_pair, *wo_got, *wo_rest)
    out_got, out_rest = gather_first(out_src, quads), gather_rest(out_src, quads)
    wo_half = gather_last(wo_src, wo_got, wo_rest, quads)
    wo_rows = jnp.concatenate(whole_columns(wo_half, c), 1)
    out_full = gather_last(out_src, out_got, out_rest, quads)

    att_all = lax.all_gather(after(attended, *in_rest), "mp", axis=0, tiled=False)
    middle, normed_m, gates, att_flat = mid_fwd(
        after(att_all, in_full, *out_got, *out_rest), wo_rows, tok_all, moe_g, pack, small_at, routes[0]
    )

    cot_own = lax.optimization_barrier(reorder(cotangent[0], q, quads))
    moe_grad = (RESID * cot_own.astype(F32)).astype(BF16)
    grad_all = lax.all_gather(after(moe_grad, attended), "mp", axis=0, tiled=True)

    x_own = normed_m
    x_other = swap(normed_m, "c", 1, 2)
    gates_other = swap(gates, "c", 1, 2)
    base = (c * half_e).astype(jnp.int32).reshape(1)
    hid_own, gact_own = moe_fwd(base, x_own, in_full, gates, length)
    x_other, _ = lax.optimization_barrier((x_other, gact_own))
    hid_other, gact_other = moe_fwd(base, x_other, in_full, gates_other, length)
    comb_give = nt(gact_other, out_full).astype(BF16)
    comb_recv = swap(comb_give, "c", 1, 2)
    comb_own = nt(after(gact_own, comb_give), out_full)
    combined = (comb_own + comb_recv.astype(F32)).astype(BF16)
    moe_branch = lax.psum_scatter(combined, "mp", scatter_dimension=0, tiled=True).astype(F32)

    g_other = swap(grad_all, "c", 1, 2)
    gug_own, choice_own = moe_bwd(base, grad_all, out_full, gates, after(hid_own, combined), length)
    gug_other, choice_other = moe_bwd(
        base, g_other, out_full, gates_other, after(hid_other, gug_own), length
    )
    choice = choice_own + swap(choice_other, "c", 1, 2)
    out_part = tn_pair(grad_all, g_other, *all_after((gact_own, gact_other), gug_other))
    out_first = scatter_first(out_part, quads)
    back_give = nt(after(gug_other, out_part), in_full).astype(BF16)
    back_recv = swap(back_give, "c", 1, 2)
    back_own = nt(after(gug_own, back_give), in_full).astype(BF16)
    gates_c = gates * choice
    logit_grad = (gates_c - gates * jnp.sum(gates_c, -1, keepdims=True)).astype(BF16)
    ag, p_part = back_mid(
        m.astype(jnp.int32).reshape(1), back_own, back_recv, logit_grad, pack, small_at,
        after(middle, moe_branch, *out_first[1:]), moe_g, cot_own, wo_rows, mp,
    )
    attended_grad = lax.psum_scatter(p_part, "mp", scatter_dimension=0, tiled=False)

    out_sum = scatter_second(all_after(out_first, ag), quads).astype(BF16)
    in_part = tn_pair(x_own, x_other, *all_after((gug_own, gug_other), ag))
    att_late = after(att_flat, in_part)
    half_cols = att_flat.shape[1] // 2
    wo_mine = tn(ag, jnp.where(c == 0, att_late[:, :half_cols], att_late[:, half_cols:]))
    wo_give = tn(ag, jnp.where(c == 0, att_late[:, half_cols:], att_late[:, :half_cols]))
    wo_part = (wo_mine + swap(wo_give.astype(BF16), "c", 1, 2).astype(F32)).astype(BF16)
    in_first = scatter_first(in_part, quads)
    layer_out = (
        lax.dynamic_slice_in_dim(middle, m * (length // mp), length // mp, 0) + RESID * moe_branch
    ).astype(BF16)

    dq, dkv = attn_bwd(
        after(attended_grad, out_sum), q_r, k_r, v_r, attended, lse, cosine, sine, doc_col, doc_row
    )
    end_part = back_end(dq, dkv, pack, tok_all, attn_g, ag)
    grad_tokens = lax.psum_scatter(end_part, "mp", scatter_dimension=0, tiled=True).astype(F32)

    in_sum = scatter_second(all_after(in_first, end_part), quads).astype(BF16)
    wo_sum = scatter_rows(after(wo_part, end_part), quads).astype(BF16)

    dq_late, dkv_late = after(dq, end_part), after(dkv, end_part)
    part = jnp.concatenate(
        [tn(normed_a, dq_late), tn(normed_a, dkv_late), tn(normed_m, logit_grad)], 1
    ).astype(BF16)
    mine, give = column_halves(part, c)
    pair = (mine.astype(F32) + swap(give, "c", 1, 2).astype(F32)).astype(BF16)
    pair_sum = scatter_second(all_after(scatter_first(pair, quads), in_sum), quads).astype(BF16)
    sums = jnp.concatenate(from_halves(after(pair_sum, wo_sum), rows, c)[:2], 1)
    sums = sums.astype(F32)
    grad_query = sums[:, :q_cols]
    grad_key = sums[:, q_cols : q_cols + kv_cols]
    grad_value = sums[:, q_cols + kv_cols : qkv_cols]
    router_part = sums[:, qkv_cols : qkv_cols + experts]

    wo_own_rows = jnp.concatenate(from_halves(wo_sum, rows, c)[:2], 1)
    grad_output = lax.dynamic_slice_in_dim(wo_own_rows, m * q_cols, q_cols, 1).astype(F32)
    for k in range(1, mp):
        send = lax.dynamic_slice_in_dim(wo_own_rows, ((m + k) % mp) * q_cols, q_cols, 1)
        grad_output = grad_output + lax.ppermute(
            send, "mp", [(i, (i + k) % mp) for i in range(mp)]
        ).astype(F32)

    in_0, in_1, in_mine, in_other = from_halves(in_sum, rows, c)
    out_0, out_1, _, _ = from_halves(out_sum, rows, c)
    grad_in = jnp.concatenate([in_0, in_1], 1).astype(F32)
    grad_out = jnp.concatenate([out_0, out_1], 1).astype(F32)

    attn_gain_part = (
        jnp.sum(grad_query * w_query.astype(F32), 1)
        + jnp.sum(grad_key * key_weight.astype(F32), 1)
        + jnp.sum(grad_value * value_weight.astype(F32), 1)
    ) / attn_gain.astype(F32)
    moe_gain_part = (
        jnp.sum(in_mine.astype(F32) * in_kept.astype(F32), 1)
        + jnp.sum(in_other.astype(F32) * in_gave.astype(F32), 1)
        + jnp.sum(router_part * router.astype(F32), 1)
    ) / moe_gain.astype(F32)
    tiny = jnp.concatenate([router_part, attn_gain_part[:, None], moe_gain_part[:, None]], 1)
    total = tiny
    for k in range(1, mp):
        total = total + lax.ppermute(tiny, "mp", [(i, (i + k) % mp) for i in range(mp)])

    return (
        reorder(layer_out, q, quads)[None],
        reorder(grad_tokens, q, quads)[None],
        total[:, experts],
        grad_query,
        grad_key,
        grad_value,
        grad_output,
        total[:, :experts],
        total[:, experts + 1],
        grad_in.reshape(w_in.shape),
        grad_out.reshape(w_out.shape),
    )


def solution(mesh):
    dp, mp = mesh.shape["dp"], mesh.shape["mp"]
    quads = dp // 2
    split = Mesh(mesh.devices.reshape(quads, 2, mp), ("q", "c", "mp"))
    d = ("q", "c")
    placed = (
        P(d, "mp", None),
        P(d),
        P(d, "mp"),
        P(d, "mp"),
        P(d, "mp"),
        P(d, "mp"),
        P(d, None),
        P(d),
        P(d, None, None, "mp"),
        P(d, None, "mp"),
        P(d, None),
        P(d, None, None),
        P(d, "mp", None),
    )
    return jax.shard_map(
        functools.partial(body, quads=quads),
        mesh=split,
        in_specs=placed,
        out_specs=(
            P(d, "mp", None),
            P(d, "mp", None),
            P(d),
            P(d, "mp"),
            P(d, "mp"),
            P(d, "mp"),
            P(d, "mp"),
            P(d, None),
            P(d),
            P(d, None, None, "mp"),
            P(d, None, "mp"),
        ),
        check_vma=False,
    )
```

```python
import functools

import jax
import jax.numpy as jnp
from jax import lax
from jax.experimental import pallas as pl
from jax.experimental.pallas import tpu as pltpu
from jax.sharding import Mesh
from jax.sharding import PartitionSpec as P

HEAD = 64
RESID = 0.22
ATTN_MULT = 0.015625
EPS = 1e-06
ROPE_BASE = 10000.0
NEG = -1e30
F32 = jnp.float32
BF16 = jnp.bfloat16
BLK = 256
VMEM_CAP = 60 * 1024 * 1024


def nt(left, right):
    return lax.dot_general(left, right, (((1,), (1,)), ((), ())), preferred_element_type=F32)


def tn(left, right):
    return lax.dot_general(left, right, (((0,), (0,)), ((), ())), preferred_element_type=F32)


def nn(left, right):
    return jnp.dot(left, right, preferred_element_type=F32)


def cost(flops, transcendentals, bytes_accessed, scale=1):
    return pl.CostEstimate(
        flops=flops // scale,
        transcendentals=transcendentals // scale,
        bytes_accessed=bytes_accessed // scale,
    )


def rope_cols(values, cosine, sine):
    lane = lax.broadcasted_iota(jnp.int32, cosine.shape, 1)
    low = (lane % HEAD) < (HEAD // 2)
    pieces = []
    for start in range(0, values.shape[1], 128):
        piece = values[:, start : start + 128]
        turned = jnp.where(low, pltpu.roll(piece, 96, 1), pltpu.roll(piece, 32, 1))
        pieces.append(piece * cosine + turned * sine)
    return pieces[0] if len(pieces) == 1 else jnp.concatenate(pieces, 1)


def seen(kc, i, kdoc_ref, qdoc, group):
    kdoc = kdoc_ref[pl.ds(pl.multiple_of(kc * BLK, BLK), BLK), :]
    kpos = kc * BLK + lax.broadcasted_iota(jnp.int32, (BLK, 1), 0)
    qpos = i * BLK + lax.broadcasted_iota(jnp.int32, (1, BLK), 1)
    visible = (kpos <= qpos) & (kdoc == qdoc)
    return jnp.where(visible, 0.0, NEG)


def attn_fwd_kernel(
    tok_ref, gain_ref, w_ref, cos_ref, sin_ref, kdoc_ref, qdoc_ref,
    na_ref, q_ref, k_ref, v_ref, att_ref, lse_ref, s_scr, *, q_heads, kv_heads,
):
    i = pl.program_id(0)
    group = q_heads // kv_heads
    tok = tok_ref[...].astype(F32)
    inv = lax.rsqrt(jnp.mean(tok * tok, -1, keepdims=True) + EPS)
    na = (tok * inv * gain_ref[...]).astype(BF16)
    na_ref[...] = na
    qkv = nn(na, w_ref[...])
    qk_cols = (q_heads + kv_heads) * HEAD
    roped = rope_cols(qkv[:, :qk_cols], cos_ref[...], sin_ref[...]).astype(BF16)
    vals = qkv[:, qk_cols:].astype(BF16)
    rows = pl.ds(pl.multiple_of(i * BLK, BLK), BLK)
    heads = [roped[:, h * HEAD : (h + 1) * HEAD] for h in range(q_heads + kv_heads)]
    for h in range(q_heads):
        q_ref[h] = heads[h]
    for g in range(kv_heads):
        k_ref[g, rows, :] = heads[q_heads + g]
        v_ref[g, rows, :] = vals[:, g * HEAD : (g + 1) * HEAD]
    lo = jnp.maximum(i - 2, 0)
    qdoc = qdoc_ref[...]
    for g in range(kv_heads):
        qs = jnp.concatenate(heads[g * group : (g + 1) * group], 0)

        def scores(kc, top, g=g, qs=qs):
            keys = k_ref[g, pl.ds(pl.multiple_of(kc * BLK, BLK), BLK), :]
            bias = seen(kc, i, kdoc_ref, qdoc, group)
            s = nt(keys, qs) * ATTN_MULT + jnp.concatenate([bias] * group, 1)
            s_scr[kc - lo] = s
            return jnp.maximum(top, jnp.max(s, 0, keepdims=True))

        top = lax.fori_loop(lo, i + 1, scores, jnp.full((1, group * BLK), NEG, F32))

        def mix(kc, carry, g=g, top=top):
            total, out = carry
            e = jnp.exp(s_scr[kc - lo] - top)
            vv = v_ref[g, pl.ds(pl.multiple_of(kc * BLK, BLK), BLK), :]
            return total + jnp.sum(e, 0, keepdims=True), out + tn(vv, e.astype(BF16))

        total, out = lax.fori_loop(
            lo, i + 1, mix, (jnp.zeros((1, group * BLK), F32), jnp.zeros((HEAD, group * BLK), F32))
        )
        out = out / total
        lse_ref[0, g : g + 1, :] = top + jnp.log(total)
        for j in range(group):
            h = g * group + j
            att_ref[:, h * HEAD : (h + 1) * HEAD] = out[:, j * BLK : (j + 1) * BLK].T.astype(BF16)


def attn_fwd(tokens, gain, pack, cosine, sine, kdoc, qdoc, q_heads, kv_heads):
    length, width = tokens.shape
    blocks = length // BLK
    cols = (q_heads + 2 * kv_heads) * HEAD
    group = q_heads // kv_heads
    fixed = lambda i: (0, 0)
    fixed3 = lambda i: (0, 0, 0)
    row = lambda i: (i, 0)
    return pl.pallas_call(
        functools.partial(attn_fwd_kernel, q_heads=q_heads, kv_heads=kv_heads),
        grid=(blocks,),
        in_specs=[
            pl.BlockSpec((BLK, width), row),
            pl.BlockSpec((1, width), fixed),
            pl.BlockSpec((width, cols), fixed),
            pl.BlockSpec((BLK, 128), row),
            pl.BlockSpec((BLK, 128), row),
            pl.BlockSpec((length, 1), fixed),
            pl.BlockSpec((1, BLK), lambda i: (0, i)),
        ],
        out_specs=[
            pl.BlockSpec((BLK, width), row),
            pl.BlockSpec((q_heads, BLK, HEAD), lambda i: (0, i, 0)),
            pl.BlockSpec((kv_heads, length, HEAD), fixed3),
            pl.BlockSpec((kv_heads, length, HEAD), fixed3),
            pl.BlockSpec((BLK, q_heads * HEAD), row),
            pl.BlockSpec((1, kv_heads, group * BLK), lambda i: (i, 0, 0)),
        ],
        out_shape=[
            jax.ShapeDtypeStruct((length, width), BF16),
            jax.ShapeDtypeStruct((q_heads, length, HEAD), BF16),
            jax.ShapeDtypeStruct((kv_heads, length, HEAD), BF16),
            jax.ShapeDtypeStruct((kv_heads, length, HEAD), BF16),
            jax.ShapeDtypeStruct((length, q_heads * HEAD), BF16),
            jax.ShapeDtypeStruct((blocks, kv_heads, group * BLK), F32),
        ],
        scratch_shapes=[pltpu.VMEM((3, BLK, group * BLK), F32)],
        compiler_params=pltpu.CompilerParams(
            dimension_semantics=("arbitrary",), vmem_limit_bytes=VMEM_CAP
        ),
        cost_estimate=cost(
            flops=2 * length * width * cols + 8 * length * 768 * q_heads * HEAD,
            transcendentals=length * 640 * q_heads,
            bytes_accessed=4 * length * width + 2 * width * cols,
            scale=100,
        ),
        name="attn_fwd",
    )(tokens, gain, pack, cosine, sine, kdoc, qdoc)


def attn_bwd_kernel(
    do_ref, q_ref, k_ref, v_ref, att_ref, lse_ref, cos_ref, sin_ref, kdoc_ref, qdoc_ref,
    dq_ref, dkv_ref, dk_scr, dv_scr, *, q_heads, kv_heads,
):
    i = pl.program_id(0)
    group = q_heads // kv_heads

    @pl.when(i == 0)
    def _():
        dk_scr[...] = jnp.zeros_like(dk_scr)
        dv_scr[...] = jnp.zeros_like(dv_scr)

    do = do_ref[...]
    lo = jnp.maximum(i - 2, 0)
    qdoc = qdoc_ref[...]
    att = att_ref[...]
    dq_heads = []
    for g in range(kv_heads):
        span = range(g * group, (g + 1) * group)
        qs = jnp.concatenate([q_ref[h] for h in span], 0)
        dos = jnp.concatenate([do[:, h * HEAD : (h + 1) * HEAD] for h in span], 0)
        outs = jnp.concatenate([att[:, h * HEAD : (h + 1) * HEAD] for h in span], 0)
        dot_row = jnp.sum((dos.astype(F32) * outs.astype(F32)).T, 0, keepdims=True)
        lse = lse_ref[0, g : g + 1, :]

        def chunk(kc, dq, g=g, qs=qs, dos=dos, dot_row=dot_row, lse=lse):
            rows = pl.ds(pl.multiple_of(kc * BLK, BLK), BLK)
            keys = k_ref[g, rows, :]
            vals = v_ref[g, rows, :]
            bias = seen(kc, i, kdoc_ref, qdoc, group)
            s = nt(keys, qs) * ATTN_MULT + jnp.concatenate([bias] * group, 1)
            prob = jnp.exp(s - lse)
            dprob = nt(vals, dos)
            ds = (prob * (dprob - dot_row)).astype(BF16)
            dv_scr[g, rows, :] += nn(prob.astype(BF16), dos)
            dk_scr[g, rows, :] += nn(ds, qs)
            return dq + tn(keys, ds)

        dq = lax.fori_loop(lo, i + 1, chunk, jnp.zeros((HEAD, group * BLK), F32))
        for j in range(group):
            dq_heads.append(dq[:, j * BLK : (j + 1) * BLK].T)
    rows = pl.ds(pl.multiple_of(i * BLK, BLK), BLK)
    dq_all = jnp.concatenate(dq_heads, 1) * ATTN_MULT
    dq_ref[...] = rope_cols(dq_all, cos_ref[rows, :], -sin_ref[rows, :]).astype(BF16)

    @pl.when(i == pl.num_programs(0) - 1)
    def _():
        dk = jnp.concatenate([dk_scr[g] for g in range(kv_heads)], 1) * ATTN_MULT
        kcols = kv_heads * HEAD
        dkv_ref[:, :kcols] = rope_cols(dk, cos_ref[...], -sin_ref[...]).astype(BF16)
        dkv_ref[:, kcols:] = jnp.concatenate([dv_scr[g] for g in range(kv_heads)], 1).astype(BF16)


def attn_bwd(do, q, k, v, att, lse, cosine, sine, kdoc, qdoc):
    length = do.shape[0]
    q_heads, kv_heads = q.shape[0], k.shape[0]
    blocks = length // BLK
    group = q_heads // kv_heads
    fixed = lambda i: (0, 0)
    fixed3 = lambda i: (0, 0, 0)
    row = lambda i: (i, 0)
    return pl.pallas_call(
        functools.partial(attn_bwd_kernel, q_heads=q_heads, kv_heads=kv_heads),
        grid=(blocks,),
        in_specs=[
            pl.BlockSpec((BLK, q_heads * HEAD), row),
            pl.BlockSpec((q_heads, BLK, HEAD), lambda i: (0, i, 0)),
            pl.BlockSpec((kv_heads, length, HEAD), fixed3),
            pl.BlockSpec((kv_heads, length, HEAD), fixed3),
            pl.BlockSpec((BLK, q_heads * HEAD), row),
            pl.BlockSpec((1, kv_heads, group * BLK), lambda i: (i, 0, 0)),
            pl.BlockSpec((length, 128), fixed),
            pl.BlockSpec((length, 128), fixed),
            pl.BlockSpec((length, 1), fixed),
            pl.BlockSpec((1, BLK), lambda i: (0, i)),
        ],
        out_specs=[
            pl.BlockSpec((BLK, q_heads * HEAD), row),
            pl.BlockSpec((length, 2 * kv_heads * HEAD), fixed),
        ],
        out_shape=[
            jax.ShapeDtypeStruct((length, q_heads * HEAD), BF16),
            jax.ShapeDtypeStruct((length, 2 * kv_heads * HEAD), BF16),
        ],
        scratch_shapes=[
            pltpu.VMEM((kv_heads, length, HEAD), F32),
            pltpu.VMEM((kv_heads, length, HEAD), F32),
        ],
        compiler_params=pltpu.CompilerParams(
            dimension_semantics=("arbitrary",), vmem_limit_bytes=VMEM_CAP
        ),
        cost_estimate=cost(
            flops=20 * length * 768 * q_heads * HEAD,
            transcendentals=length * 640 * q_heads,
            bytes_accessed=8 * length * q_heads * HEAD,
        ),
        name="attn_bwd",
    )(do, q, k, v, att, lse, cosine, sine, kdoc, qdoc)


def mid_kernel(
    att_ref, wo_ref, tok_ref, gain_ref, small_ref, routes_ref, mid_ref, nm_ref, gate_ref, flat_ref
):
    att = jnp.concatenate([att_ref[k] for k in range(att_ref.shape[0])], 1)
    flat_ref[...] = att
    branch = nt(att, wo_ref[...])
    middle = tok_ref[...].astype(F32) + RESID * branch
    mid_ref[...] = middle
    inv = lax.rsqrt(jnp.mean(middle * middle, -1, keepdims=True) + EPS)
    nm = (middle * inv * gain_ref[...]).astype(BF16)
    nm_ref[...] = nm
    logits = nn(nm, small_ref[...])
    lane = lax.broadcasted_iota(jnp.int32, logits.shape, 1)
    chosen = lane == routes_ref[:, 0:1]
    for c in range(1, routes_ref.shape[1]):
        chosen = chosen | (lane == routes_ref[:, c : c + 1])
    logits = jnp.where(chosen, logits, NEG)
    e = jnp.exp(logits - jnp.max(logits, -1, keepdims=True))
    gate_ref[...] = e / jnp.sum(e, -1, keepdims=True)


def mid_fwd(att_all, wo_rows, tokens, gain, pack, small_at, routes):
    length, width = tokens.shape
    parts, _, cols = att_all.shape
    blocks = length // BLK
    fixed = lambda i: (0, 0)
    row = lambda i: (i, 0)
    return pl.pallas_call(
        mid_kernel,
        grid=(blocks,),
        in_specs=[
            pl.BlockSpec((parts, BLK, cols), lambda i: (0, i, 0)),
            pl.BlockSpec((width, parts * cols), fixed),
            pl.BlockSpec((BLK, width), row),
            pl.BlockSpec((1, width), fixed),
            pl.BlockSpec((width, 128), lambda i: (0, small_at)),
            pl.BlockSpec((BLK, routes.shape[1]), row),
        ],
        out_specs=[
            pl.BlockSpec((BLK, width), row),
            pl.BlockSpec((BLK, width), row),
            pl.BlockSpec((BLK, 128), row),
            pl.BlockSpec((BLK, parts * cols), row),
        ],
        out_shape=[
            jax.ShapeDtypeStruct((length, width), F32),
            jax.ShapeDtypeStruct((length, width), BF16),
            jax.ShapeDtypeStruct((length, 128), F32),
            jax.ShapeDtypeStruct((length, parts * cols), BF16),
        ],
        compiler_params=pltpu.CompilerParams(
            dimension_semantics=("arbitrary",), vmem_limit_bytes=VMEM_CAP
        ),
        cost_estimate=cost(
            flops=2 * length * width * cols * parts,
            transcendentals=length * 128,
            bytes_accessed=10 * length * width + 2 * width * cols * parts,
        ),
        name="mid_fwd",
    )(att_all, wo_rows, tokens, gain, pack, routes)


def norm_back(n_grad, values, gain):
    inv = lax.rsqrt(jnp.mean(values * values, -1, keepdims=True) + EPS)
    scaled = n_grad * gain
    return inv * (scaled - values * (inv * inv) * jnp.mean(scaled * values, -1, keepdims=True))


def back_mid_kernel(
    own_ref, back_ref, recv_ref, lg_ref, small_ref, mid_ref, gain_ref, cot_ref, wo_ref, ag_ref, p_ref
):
    n_grad = back_ref[...].astype(F32) + recv_ref[...].astype(F32) + nt(lg_ref[...], small_ref[...])
    grad = norm_back(n_grad, mid_ref[...], gain_ref[...])
    own = (pl.program_id(0) == own_ref[0]).astype(F32)
    ag = (RESID * (grad + own * cot_ref[...].astype(F32))).astype(BF16)
    ag_ref[...] = ag
    out = nn(ag, wo_ref[...]).astype(BF16)
    cols = p_ref.shape[2]
    for k in range(p_ref.shape[0]):
        p_ref[k] = out[:, k * cols : (k + 1) * cols]


def back_mid(own, back, recv, logit_grad, pack, small_at, middle, gain, cot, wo_rows, parts):
    length, width = middle.shape
    blocks = length // BLK
    cols = wo_rows.shape[1] // parts
    fixed = lambda i, o: (0, 0)
    row = lambda i, o: (i, 0)
    return pl.pallas_call(
        back_mid_kernel,
        grid_spec=pltpu.PrefetchScalarGridSpec(
            num_scalar_prefetch=1,
            grid=(blocks,),
            in_specs=[
                pl.BlockSpec((BLK, width), row),
                pl.BlockSpec((BLK, width), row),
                pl.BlockSpec((BLK, 128), row),
                pl.BlockSpec((width, 128), lambda i, o: (0, small_at)),
                pl.BlockSpec((BLK, width), row),
                pl.BlockSpec((1, width), fixed),
                pl.BlockSpec((BLK, width), fixed),
                pl.BlockSpec((width, parts * cols), fixed),
            ],
            out_specs=[
                pl.BlockSpec((BLK, width), row),
                pl.BlockSpec((parts, BLK, cols), lambda i, o: (0, i, 0)),
            ],
        ),
        out_shape=[
            jax.ShapeDtypeStruct((length, width), BF16),
            jax.ShapeDtypeStruct((parts, length, cols), BF16),
        ],
        compiler_params=pltpu.CompilerParams(
            dimension_semantics=("arbitrary",), vmem_limit_bytes=VMEM_CAP
        ),
        cost_estimate=cost(
            flops=2 * length * width * cols * parts,
            transcendentals=0,
            bytes_accessed=12 * length * width + 2 * width * cols * parts,
        ),
        name="back_mid",
    )(own, back, recv, logit_grad, pack, middle, gain, cot, wo_rows)


def back_end_kernel(dq_ref, dkv_ref, w_ref, tok_ref, gain_ref, ag_ref, out_ref):
    d_all = jnp.concatenate([dq_ref[...], dkv_ref[...]], 1)
    n_grad = nt(d_all, w_ref[...])
    grad = norm_back(n_grad, tok_ref[...].astype(F32), gain_ref[...])
    out_ref[...] = (grad + ag_ref[...].astype(F32) * (1.0 / RESID)).astype(BF16)


def back_end(dq, dkv, pack, tokens, gain, ag):
    length, width = tokens.shape
    cols = dq.shape[1] + dkv.shape[1]
    fixed = lambda i: (0, 0)
    row = lambda i: (i, 0)
    return pl.pallas_call(
        back_end_kernel,
        grid=(length // BLK,),
        in_specs=[
            pl.BlockSpec((BLK, dq.shape[1]), row),
            pl.BlockSpec((BLK, dkv.shape[1]), row),
            pl.BlockSpec((width, cols), fixed),
            pl.BlockSpec((BLK, width), row),
            pl.BlockSpec((1, width), fixed),
            pl.BlockSpec((BLK, width), row),
        ],
        out_specs=pl.BlockSpec((BLK, width), row),
        out_shape=jax.ShapeDtypeStruct((length, width), BF16),
        compiler_params=pltpu.CompilerParams(
            dimension_semantics=("arbitrary",), vmem_limit_bytes=VMEM_CAP
        ),
        cost_estimate=cost(
            flops=2 * length * width * cols,
            transcendentals=0,
            bytes_accessed=6 * length * width + 2 * width * cols,
        ),
        name="back_end",
    )(dq, dkv, pack, tokens, gain, ag)


def gate_cols(gates, first):
    lane = lax.broadcasted_iota(jnp.int32, gates.shape, 1)
    return [
        jnp.sum(jnp.where(lane == first + k, gates, 0.0), -1, keepdims=True) for k in range(2)
    ]


def moe_fwd_kernel(base_ref, x_ref, w_ref, gate_ref, h_ref, gact_ref):
    p = pl.program_id(1)
    h = nn(x_ref[...], w_ref[...])
    h_ref[...] = h.astype(BF16)
    cols = gate_cols(gate_ref[...], base_ref[0] + 2 * p)
    for k in range(2):
        gate = h[:, 256 * k : 256 * k + 128]
        up = h[:, 256 * k + 128 : 256 * k + 256]
        act = gate * jax.nn.sigmoid(gate) * up
        gact_ref[:, 128 * k : 128 * k + 128] = (cols[k] * act).astype(BF16)


def moe_fwd(base, x, w_in, gates, rows, scale):
    length, width = x.shape
    cols = w_in.shape[1]
    return pl.pallas_call(
        moe_fwd_kernel,
        grid_spec=pltpu.PrefetchScalarGridSpec(
            num_scalar_prefetch=1,
            grid=(length // rows, cols // 512),
            in_specs=[
                pl.BlockSpec((rows, width), lambda i, p, b: (i, 0)),
                pl.BlockSpec((width, 512), lambda i, p, b: (0, p)),
                pl.BlockSpec((rows, 128), lambda i, p, b: (i, 0)),
            ],
            out_specs=[
                pl.BlockSpec((rows, 512), lambda i, p, b: (i, p)),
                pl.BlockSpec((rows, 256), lambda i, p, b: (i, p)),
            ],
        ),
        out_shape=[
            jax.ShapeDtypeStruct((length, cols), BF16),
            jax.ShapeDtypeStruct((length, cols // 2), BF16),
        ],
        compiler_params=pltpu.CompilerParams(
            dimension_semantics=("arbitrary", "arbitrary"), vmem_limit_bytes=VMEM_CAP
        ),
        cost_estimate=cost(
            flops=2 * length * width * cols,
            transcendentals=length * cols // 2,
            bytes_accessed=2 * length * (width + cols + cols // 2) + 4 * width * cols,
            scale=scale,
        ),
        name="moe_fwd",
    )(base, x, w_in, gates)


def combine_kernel(*refs):
    gact_ref, pieces, out_ref, w_scr = refs[0], refs[1:-2], refs[-2], refs[-1]

    @pl.when(pl.program_id(0) == 0)
    def _():
        at = 0
        for piece in pieces:
            w_scr[at : at + piece.shape[0], :] = piece[...]
            at += piece.shape[0]

    out_ref[...] = nt(gact_ref[...], w_scr[...]).astype(BF16)


def combine(gact, pieces, rows):
    length, cols = gact.shape
    width = sum(p.shape[0] for p in pieces)
    return pl.pallas_call(
        combine_kernel,
        grid=(length // rows,),
        in_specs=[pl.BlockSpec((rows, cols), lambda i: (i, 0))]
        + [pl.BlockSpec(p.shape, lambda i: (0, 0)) for p in pieces],
        out_specs=pl.BlockSpec((rows, width), lambda i: (i, 0)),
        out_shape=jax.ShapeDtypeStruct((length, width), BF16),
        scratch_shapes=[pltpu.VMEM((width, cols), BF16)],
        compiler_params=pltpu.CompilerParams(
            dimension_semantics=("arbitrary",), vmem_limit_bytes=VMEM_CAP
        ),
        cost_estimate=cost(
            flops=2 * length * width * cols,
            transcendentals=0,
            bytes_accessed=2 * (length * width + length * cols + width * cols),
        ),
        name="combine",
    )(gact, *pieces)


def moe_bwd_kernel(*refs):
    base_ref, g_ref, gate_ref, h_ref = refs[:4]
    pieces, gug_ref, choice_ref = refs[4:-2], refs[-2], refs[-1]
    p = pl.program_id(1)
    first = base_ref[0] + 2 * p
    weights = [piece[...] for piece in pieces]
    plain = nn(g_ref[...], weights[0] if len(weights) == 1 else jnp.concatenate(weights, 0))
    cols = gate_cols(gate_ref[...], first)

    @pl.when(p == 0)
    def _():
        choice_ref[...] = jnp.zeros_like(choice_ref)

    lane = lax.broadcasted_iota(jnp.int32, choice_ref.shape, 1)
    add = jnp.zeros(choice_ref.shape, F32)
    for k in range(2):
        gate = h_ref[:, 256 * k : 256 * k + 128].astype(F32)
        up = h_ref[:, 256 * k + 128 : 256 * k + 256].astype(F32)
        part = plain[:, 128 * k : 128 * k + 128]
        sig = jax.nn.sigmoid(gate)
        silu = gate * sig
        add = jnp.where(lane == first + k, jnp.sum(silu * up * part, -1, keepdims=True), add)
        act_grad = cols[k] * part
        gug_ref[:, 256 * k : 256 * k + 128] = (
            act_grad * up * sig * (1.0 + gate * (1.0 - sig))
        ).astype(BF16)
        gug_ref[:, 256 * k + 128 : 256 * k + 256] = (act_grad * silu).astype(BF16)
    choice_ref[...] += add


def moe_bwd(base, g, pieces, gates, h, rows):
    length, width = g.shape
    cols = h.shape[1]
    return pl.pallas_call(
        moe_bwd_kernel,
        grid_spec=pltpu.PrefetchScalarGridSpec(
            num_scalar_prefetch=1,
            grid=(length // rows, cols // 512),
            in_specs=[
                pl.BlockSpec((rows, width), lambda i, p, b: (i, 0)),
                pl.BlockSpec((rows, 128), lambda i, p, b: (i, 0)),
                pl.BlockSpec((rows, 512), lambda i, p, b: (i, p)),
            ]
            + [pl.BlockSpec((w.shape[0], 256), lambda i, p, b: (0, p)) for w in pieces],
            out_specs=[
                pl.BlockSpec((rows, 512), lambda i, p, b: (i, p)),
                pl.BlockSpec((rows, 128), lambda i, p, b: (i, 0)),
            ],
        ),
        out_shape=[
            jax.ShapeDtypeStruct((length, cols), BF16),
            jax.ShapeDtypeStruct((length, 128), F32),
        ],
        compiler_params=pltpu.CompilerParams(
            dimension_semantics=("arbitrary", "arbitrary"), vmem_limit_bytes=VMEM_CAP
        ),
        cost_estimate=cost(
            flops=length * width * cols,
            transcendentals=length * cols // 2,
            bytes_accessed=2 * length * (width + 2 * cols) + 2 * width * cols,
        ),
        name="moe_bwd",
    )(base, g, gates, h, *pieces)


def segment_kernel(*refs, count):
    lefts, rights, outs = refs[:4], refs[4:6], refs[6:]
    first = tn(jnp.concatenate([lefts[0][...], lefts[1][...]], 1), rights[0][...])
    second = tn(jnp.concatenate([lefts[2][...], lefts[3][...]], 1), rights[1][...])
    value = (first + second).astype(BF16)
    for k in range(count):

        @pl.when(pl.program_id(0) == k)
        def _(k=k):
            outs[k][...] = value


def pick(s, values):
    out = values[0]
    for k in range(1, len(values)):
        out = jnp.where(s == k, values[k], out)
    return out


def weight_grad(left, left2, right, right2, segments):
    length, width = left.shape
    cols = right.shape[1] // 2
    quarter = width // 4
    wide = min(cols, 768)
    steps = cols // wide
    count = len(segments)
    firsts, seconds, halves = zip(*segments, strict=True)
    one = pl.BlockSpec((length, quarter), lambda s, j: (0, pick(s, firsts)))
    two = pl.BlockSpec((length, quarter), lambda s, j: (0, pick(s, seconds)))
    side = pl.BlockSpec((length, wide), lambda s, j: (0, pick(s, halves) * steps + j))

    def place(k):
        return pl.BlockSpec(
            (2 * quarter, wide),
            lambda s, j: (0, jnp.where(s == k, j, jnp.where(s < k, 0, steps - 1))),
        )

    return pl.pallas_call(
        functools.partial(segment_kernel, count=count),
        grid=(count, steps),
        in_specs=[one, two, one, two, side, side],
        out_specs=[place(k) for k in range(count)],
        out_shape=[jax.ShapeDtypeStruct((2 * quarter, cols), BF16)] * count,
        compiler_params=pltpu.CompilerParams(
            dimension_semantics=("arbitrary", "arbitrary"), vmem_limit_bytes=VMEM_CAP
        ),
        cost_estimate=cost(
            flops=2 * count * length * width * cols,
            transcendentals=0,
            bytes_accessed=4 * length * (width + 2 * cols),
            scale=100,
        ),
        name="weight_grad",
    )(left, left, left2, left2, right, right2)


def swap(value, axis, bit, size):
    return lax.ppermute(value, axis, [(i, i ^ bit) for i in range(size)])


def reorder(value, q, quads):
    if quads != 4:
        return value
    n = value.shape[-1] // 4
    b = [value[..., k * n : (k + 1) * n] for k in (0, 1, 3, 2)]
    odd = (q & 1) == 1
    far = (q & 2) == 2
    c = [jnp.where(odd, b[k], b[j]) for j, k in ((0, 1), (1, 0), (2, 3), (3, 2))]
    return jnp.concatenate([jnp.where(far, c[k], c[j]) for j, k in ((0, 3), (1, 2), (2, 1), (3, 0))], -1)


def restore(value, q, quads):
    if quads != 4:
        return value
    n = value.shape[-1] // 4
    b = [value[..., k * n : (k + 1) * n] for k in (0, 1, 3, 2)]
    odd = (q & 1) == 1
    far = (q & 2) == 2
    c = [jnp.where(odd, b[k ^ 1], b[k]) for k in range(4)]
    return jnp.concatenate([jnp.where(far, c[k ^ 2], c[k]) for k in range(4)], -1)


def gather_first(low, high, quads):
    if quads != 4:
        return (lax.all_gather(jnp.concatenate([low, high], 0), "q", axis=0, tiled=True),)
    return swap(low, "q", 1, 4), swap(high, "q", 2, 4)


def gather_rest(low, high, quads):
    if quads != 4:
        return ()
    return swap(high, "q", 1, 4), swap(low, "q", 2, 4)


def gather_diagonal(first, quads):
    if quads != 4:
        return ()
    return swap(first[0], "q", 2, 4), swap(first[1], "q", 1, 4)


def gather_join(low, high, first, rest, diagonal, quads):
    if quads != 4:
        return first[0]
    return jnp.concatenate(
        [low, high, first[0], rest[0], diagonal[0], diagonal[1], rest[1], first[1]], 0
    )


def gather_pieces(low, high, first, rest, diagonal, quads):
    if quads != 4:
        return first
    return (low, high, first[0], rest[0], diagonal[0], diagonal[1], rest[1], first[1])


def gather_rows(low, high, quads):
    first = gather_first(low, high, quads)
    rest = gather_rest(low, high, quads)
    return gather_join(low, high, first, rest, gather_diagonal(first, quads), quads)


SEND_LEFT, SEND_RIGHT, KEEP_LEFT, KEEP_RIGHT = (2, 3, 0), (2, 1, 1), (0, 1, 0), (0, 3, 1)


def cut(value, segment):
    n, half = value.shape[0] // 4, (value.shape[1] // 2 + 127) // 128 * 128
    side = value[:, half:] if segment[2] else value[:, :half]
    return jnp.concatenate([side[k * n : (k + 1) * n] for k in segment[:2]], 0)


def scatter_first(left, right):
    return swap(left, "q", 2, 4), swap(right, "q", 1, 4)


def scatter_second(keep_left, keep_right, from_y, from_x, tie=None):
    n = keep_left.shape[0] // 2
    give_x = (keep_left[n:].astype(F32) + from_y[:n].astype(F32)).astype(BF16)
    give_y = (keep_right[n:].astype(F32) + from_x[:n].astype(F32)).astype(BF16)
    give_x, give_y = lax.optimization_barrier((give_x, give_y))
    left = swap(give_x, "q", 1, 4)
    right = swap(give_y, "q", 2, 4)
    others = () if tie is None else tie(left, right)
    keep_left, keep_right, from_y, from_x, left, right = all_after(
        (keep_left, keep_right, from_y, from_x, left, right), *others
    )
    return (
        (keep_left[:n].astype(F32) + from_y[n:].astype(F32) + left.astype(F32)).astype(BF16),
        (keep_right[:n].astype(F32) + from_x[n:].astype(F32) + right.astype(F32)).astype(BF16),
    )


def scatter_plain(value):
    total = lax.psum_scatter(value, "q", scatter_dimension=0, tiled=True)
    half = total.shape[1] // 2
    return total[:, :half], total[:, half:]


def after(value, *others):
    return lax.optimization_barrier((value, *others))[0]


def all_after(values, *others):
    return lax.optimization_barrier((*values, *others))[: len(values)]


def to_halves(mine, give, c):
    other = swap(give, "c", 1, 2)
    first = c == 0
    return jnp.where(first, mine, other), jnp.where(first, other, mine)


def from_halves(totals, rows, c):
    def take(at):
        return jnp.concatenate([lax.dynamic_slice_in_dim(t, at * rows, rows, 0) for t in totals], 1)

    return take(c), swap(take(1 - c), "c", 1, 2)


def in_order(mine, other, c):
    return jnp.where(c == 0, mine, other), jnp.where(c == 0, other, mine)


def column_halves(value, c):
    n = value.shape[1] // 2
    mine = jnp.where(c == 0, value[:, :n], value[:, n:])
    give = jnp.where(c == 0, value[:, n:], value[:, :n])
    return mine, give


def whole_columns(half, c):
    other = swap(half, "c", 1, 2)
    return jnp.where(c == 0, half, other), jnp.where(c == 0, other, half)


def body(
    tokens, attn_gain, w_query, key_weight, value_weight, w_output, router, moe_gain, w_in, w_out,
    segments, routes, cotangent, *, quads,
):
    q = lax.axis_index("q")
    c = lax.axis_index("c")
    m = lax.axis_index("mp")
    length = segments.shape[1]
    width = tokens.shape[2]
    rows = w_query.shape[0]
    experts = router.shape[1]
    half_e = experts // 2
    ff = w_out.shape[2]
    q_heads = w_query.shape[1] // HEAD
    kv_heads = key_weight.shape[1] // HEAD
    q_cols, kv_cols = q_heads * HEAD, kv_heads * HEAD
    qkv_cols = q_cols + 2 * kv_cols
    mp = lax.axis_size("mp")

    tok_own = reorder(tokens[0], q, quads)
    tok_all = lax.all_gather(tok_own, "mp", axis=0, tiled=True)

    def half_rows(value):
        mine = lax.dynamic_slice_in_dim(value, c * half_e, half_e, 1).reshape(rows, -1)
        give = lax.dynamic_slice_in_dim(value, (1 - c) * half_e, half_e, 1).reshape(rows, -1)
        return to_halves(mine, give, c), mine, give

    in_pair, in_kept, in_gave = half_rows(w_in)

    pad = jnp.zeros((rows, 128 - experts - 2), BF16)
    pack = jnp.concatenate(
        [w_query, key_weight, value_weight, router, attn_gain[:, None], moe_gain[:, None], pad], 1
    )
    pack_pair = to_halves(*column_halves(after(pack, in_gave, in_kept), c), c)
    pack_first = gather_first(*pack_pair, quads)
    pack_rest = gather_rest(*pack_pair, quads)
    pack_half = gather_join(
        *pack_pair, pack_first, pack_rest, gather_diagonal(pack_first, quads), quads
    )
    pack = jnp.concatenate(whole_columns(pack_half, c), 1)
    small_at = qkv_cols // 128
    gains = pack[:, qkv_cols + experts : qkv_cols + experts + 2].astype(F32)
    attn_g = gains[:, 0].reshape(1, width)
    moe_g = gains[:, 1].reshape(1, width)

    doc_row = segments
    doc_col = segments.reshape(length, 1)
    lane = jnp.arange(128, dtype=jnp.int32) % (HEAD // 2)
    freq = ROPE_BASE ** (-lane.astype(F32) * 2.0 / HEAD)
    angles = jnp.arange(length).astype(F32)[:, None] * freq[None, :]
    cosine = jnp.cos(angles)
    upper = (jnp.arange(128, dtype=jnp.int32) % HEAD) < (HEAD // 2)
    sine = jnp.where(upper[None, :], -jnp.sin(angles), jnp.sin(angles))

    out_pair, _, _ = half_rows(after(w_out, *pack_pair))
    in_src = in_pair
    in_got = gather_first(*in_src, quads)
    in_rest = gather_rest(*in_src, quads)

    normed_a, q_r, k_r, v_r, attended, lse = attn_fwd(
        tok_all, attn_g, pack, cosine, sine, doc_col, doc_row, q_heads, kv_heads
    )

    wo_pad = jnp.concatenate([w_output, jnp.zeros((rows, 5 * 64), BF16)], 1)
    wo_cols = lax.all_gather(after(wo_pad, pack), "mp", axis=0, tiled=False)
    wo_cols = jnp.concatenate([wo_cols[j, :, :q_cols] for j in range(mp)], 1)
    wo_pair = to_halves(*column_halves(after(wo_cols, attended), c), c)
    in_diag = gather_diagonal(in_got, quads)
    wo_src = all_after(wo_pair, *in_diag)
    wo_got, wo_rest = gather_first(*wo_src, quads), gather_rest(*wo_src, quads)
    out_src = all_after(out_pair, *wo_got, *wo_rest)
    out_got, out_rest = gather_first(*out_src, quads), gather_rest(*out_src, quads)
    wo_half = gather_join(*wo_src, wo_got, wo_rest, gather_diagonal(wo_got, quads), quads)
    step = width // 4
    wo_other = jnp.concatenate(
        [swap(wo_half[k * step : (k + 1) * step], "c", 1, 2) for k in range(4)], 0
    )
    wo_rows = jnp.concatenate(in_order(*lax.optimization_barrier((wo_half, wo_other)), c), 1)
    join = (*in_src, *in_got, *in_rest, *in_diag)
    join = all_after(join, *wo_got)
    in_full = gather_join(
        *join[:2], join[2 : 2 + len(in_got)], join[2 + len(in_got) : 2 + len(in_got) + len(in_rest)],
        join[2 + len(in_got) + len(in_rest) :], quads,
    )

    att_all = lax.all_gather(after(attended, *in_got, *in_rest, *out_pair), "mp", axis=0, tiled=False)
    middle, normed_m, gates, att_flat = mid_fwd(
        after(att_all, in_full, *out_got), wo_rows, tok_all, moe_g, pack, small_at, routes[0]
    )

    cot_own = lax.optimization_barrier(reorder(cotangent[0], q, quads))
    moe_grad = (RESID * cot_own.astype(F32)).astype(BF16)
    grad_all = lax.all_gather(after(moe_grad, attended), "mp", axis=0, tiled=True)

    x_own = normed_m
    x_other = swap(normed_m, "c", 1, 2)
    gates_other = swap(gates, "c", 1, 2)
    base = (c * half_e).astype(jnp.int32).reshape(1)
    hid_own, gact_own = moe_fwd(
        base, x_own, in_full, gates, length, 100
    )
    x_other = after(x_other, gact_own, *out_rest)
    out_diag = all_after(gather_diagonal(out_got, quads), gact_own)
    out_full = gather_pieces(*out_src, out_got, out_rest, out_diag, quads)
    hid_other, gact_other = moe_fwd(base, x_other, in_full, gates_other, length, 1)
    comb_give = combine(gact_other, out_full, length // 2)
    comb_recv = swap(comb_give, "c", 1, 2)
    comb_own = combine(after(gact_own, comb_give, grad_all), out_full, length // 2)
    combined = (comb_own.astype(F32) + comb_recv.astype(F32)).astype(BF16)
    moe_branch = lax.psum_scatter(combined, "mp", scatter_dimension=0, tiled=True).astype(F32)

    g_other = swap(after(grad_all, comb_give), "c", 1, 2)
    gacts = all_after((gact_own, gact_other), comb_own)
    if quads == 4:
        out_send = weight_grad(
            grad_all, g_other, *gacts, (SEND_LEFT, SEND_RIGHT, KEEP_LEFT, KEEP_RIGHT)
        )
        out_keep = out_send[2:]
        out_move = scatter_first(*out_send[:2])
    else:
        g2, gact2 = jnp.concatenate([grad_all, g_other], 0), jnp.concatenate(gacts, 0)
        out_move = out_keep = (tn(g2, gact2).astype(BF16),)
    gug_own, choice_own = moe_bwd(
        base, grad_all, out_full, gates, after(hid_own, *out_keep), length
    )
    gug_other, choice_other = moe_bwd(base, g_other, out_full, gates_other, after(hid_other, gug_own), length)
    choice = choice_own + swap(choice_other, "c", 1, 2)
    back_give = nt(after(gug_other, *out_move), in_full).astype(BF16)
    back_recv = swap(back_give, "c", 1, 2)
    gug_late = after(gug_own, back_give)
    back_own = nt(gug_late, in_full).astype(BF16)
    gates_c = gates * choice
    logit_grad = (gates_c - gates * jnp.sum(gates_c, -1, keepdims=True)).astype(BF16)
    def middle_back(*arrived):
        return back_mid(
            m.astype(jnp.int32).reshape(1), back_own, back_recv, logit_grad, pack, small_at,
            after(middle, moe_branch, *arrived), moe_g, cot_own, wo_rows, mp,
        )

    made = []

    def tie(left, right):
        made.extend(middle_back(left, right))
        return (made[0],)

    if quads == 4:
        out_sum = scatter_second(*out_keep, *out_move, tie)
    else:
        out_sum = scatter_plain(*out_keep)
        made.extend(middle_back())
    ag, p_part = made
    attended_grad = lax.psum_scatter(p_part, "mp", scatter_dimension=0, tiled=False)

    gugs = all_after((gug_own, gug_other), ag)
    if quads == 4:
        in_send = weight_grad(x_own, x_other, *gugs, (SEND_LEFT, SEND_RIGHT))
        in_move = scatter_first(*in_send)
        in_keep = weight_grad(
            x_own, x_other, *all_after(gugs, *in_send), (KEEP_LEFT, KEEP_RIGHT)
        )
    else:
        in_move = in_keep = (tn(jnp.concatenate([x_own, x_other], 0), jnp.concatenate(gugs, 0)).astype(BF16),)
    att_late = after(att_flat, *in_send) if quads == 4 else att_flat
    half_cols = att_flat.shape[1] // 2
    low_att, high_att = att_late[:, :half_cols], att_late[:, half_cols:]
    wo_give = tn(ag, jnp.where(c == 0, high_att, low_att)).astype(BF16)
    wo_mine = tn(ag, after(jnp.where(c == 0, low_att, high_att), wo_give)).astype(BF16)
    wo_part = (wo_mine.astype(F32) + swap(wo_give, "c", 1, 2).astype(F32)).astype(BF16)
    if quads == 4:
        wo_keep = (cut(wo_part, KEEP_LEFT), cut(wo_part, KEEP_RIGHT))
        wo_move = scatter_first(cut(wo_part, SEND_LEFT), cut(wo_part, SEND_RIGHT))
    layer_out = (
        lax.dynamic_slice_in_dim(middle, m * (length // mp), length // mp, 0) + RESID * after(moe_branch, ag)
    ).astype(BF16)

    dq, dkv = attn_bwd(
        attended_grad, q_r, k_r, v_r, attended, lse, cosine, sine, doc_col, doc_row
    )
    end_part = back_end(dq, dkv, pack, tok_all, attn_g, ag)
    grad_tokens = lax.psum_scatter(end_part, "mp", scatter_dimension=0, tiled=True).astype(F32)

    dq_late, dkv_late = after(dq, end_part), after(dkv, end_part)
    part = jnp.concatenate(
        [tn(normed_a, dq_late), tn(normed_a, dkv_late), tn(normed_m, logit_grad)], 1
    ).astype(BF16)
    mine, give = column_halves(part, c)
    pair = (mine.astype(F32) + swap(give, "c", 1, 2).astype(F32)).astype(BF16)
    if quads == 4:
        in_sum = scatter_second(*in_keep, *all_after(in_move, end_part))
        wo_sum = scatter_second(*wo_keep, *all_after(wo_move, end_part))
        pair_keep = (cut(pair, KEEP_LEFT), cut(pair, KEEP_RIGHT))
        pair_move = scatter_first(cut(pair, SEND_LEFT), cut(pair, SEND_RIGHT))
        *pair_move, in_left, in_right = lax.optimization_barrier((*pair_move, *in_sum))
        in_sum = (in_left, in_right)
        pair_sum = scatter_second(*pair_keep, *pair_move)
        late_sum = (*wo_sum, *pair_sum)
    else:
        in_sum, wo_sum, pair_sum = (scatter_plain(v) for v in (in_keep[0], wo_part, pair))
        late_sum = (*wo_sum, *pair_sum)
    late_mine, late_other = from_halves(late_sum, rows, c)
    wo_cols_here = wo_part.shape[1]
    wo_own_rows = jnp.concatenate(
        in_order(late_mine[:, :wo_cols_here], late_other[:, :wo_cols_here], c), 1
    )
    sums = jnp.concatenate(
        in_order(late_mine[:, wo_cols_here:], late_other[:, wo_cols_here:], c), 1
    ).astype(F32)
    grad_query = sums[:, :q_cols]
    grad_key = sums[:, q_cols : q_cols + kv_cols]
    grad_value = sums[:, q_cols + kv_cols : qkv_cols]
    router_part = sums[:, qkv_cols : qkv_cols + experts]

    in_mine, in_other = from_halves(in_sum, rows, c)
    out_mine, out_other = from_halves(all_after(out_sum, ag), rows, c)
    grad_in = jnp.concatenate(in_order(in_mine, in_other, c), 1).astype(F32)
    grad_out = jnp.concatenate(in_order(out_mine, out_other, c), 1).astype(F32)

    attn_gain_part = (
        jnp.sum(grad_query * w_query.astype(F32), 1)
        + jnp.sum(grad_key * key_weight.astype(F32), 1)
        + jnp.sum(grad_value * value_weight.astype(F32), 1)
    ) / attn_gain.astype(F32)
    moe_gain_part = (
        jnp.sum(in_mine.astype(F32) * in_kept.astype(F32), 1)
        + jnp.sum(in_other.astype(F32) * in_gave.astype(F32), 1)
        + jnp.sum(router_part * router.astype(F32), 1)
    ) / moe_gain.astype(F32)
    total = jnp.concatenate(
        [router_part, attn_gain_part[:, None], moe_gain_part[:, None], jnp.zeros((rows, 128 - experts - 2), F32)], 1
    )
    tiny = total.astype(BF16)
    grad_output = lax.dynamic_slice_in_dim(wo_own_rows, m * q_cols, q_cols, 1).astype(F32)
    for k in range(1, mp):
        send = lax.dynamic_slice_in_dim(wo_own_rows, ((m + k) % mp) * q_cols, q_cols, 1)
        got = lax.ppermute(
            jnp.concatenate([send, tiny], 1), "mp", [(i, (i + k) % mp) for i in range(mp)]
        ).astype(F32)
        grad_output = grad_output + got[:, :q_cols]
        total = total + got[:, q_cols:]

    return (
        restore(layer_out, q, quads)[None],
        restore(grad_tokens, q, quads)[None],
        total[:, experts],
        grad_query,
        grad_key,
        grad_value,
        grad_output,
        total[:, :experts],
        total[:, experts + 1],
        grad_in.reshape(w_in.shape),
        grad_out.reshape(w_out.shape),
    )


def solution(mesh):
    dp, mp = mesh.shape["dp"], mesh.shape["mp"]
    quads = dp // 2
    split = Mesh(mesh.devices.reshape(quads, 2, mp), ("q", "c", "mp"))
    d = ("q", "c")
    placed = (
        P(d, "mp", None),
        P(d),
        P(d, "mp"),
        P(d, "mp"),
        P(d, "mp"),
        P(d, "mp"),
        P(d, None),
        P(d),
        P(d, None, None, "mp"),
        P(d, None, "mp"),
        P(d, None),
        P(d, None, None),
        P(d, "mp", None),
    )
    return jax.shard_map(
        functools.partial(body, quads=quads),
        mesh=split,
        in_specs=placed,
        out_specs=(
            P(d, "mp", None),
            P(d, "mp", None),
            P(d),
            P(d, "mp"),
            P(d, "mp"),
            P(d, "mp"),
            P(d, "mp"),
            P(d, None),
            P(d),
            P(d, None, None, "mp"),
            P(d, None, "mp"),
        ),
        check_vma=False,
    )
```

```python
import functools

import jax
import jax.numpy as jnp
from jax import lax
from jax.experimental import pallas as pl
from jax.experimental.pallas import tpu as pltpu
from jax.sharding import Mesh
from jax.sharding import PartitionSpec as P

HEAD = 64
RESID = 0.22
ATTN_MULT = 0.015625
EPS = 1e-06
ROPE_BASE = 10000.0
NEG = -1e30
F32 = jnp.float32
BF16 = jnp.bfloat16
BLK = 256
VMEM_CAP = 60 * 1024 * 1024


def nt(left, right):
    return lax.dot_general(left, right, (((1,), (1,)), ((), ())), preferred_element_type=F32)


def tn(left, right):
    return lax.dot_general(left, right, (((0,), (0,)), ((), ())), preferred_element_type=F32)


def nn(left, right):
    return jnp.dot(left, right, preferred_element_type=F32)


def cost(flops, transcendentals, bytes_accessed, scale=1):
    return pl.CostEstimate(
        flops=flops // scale,
        transcendentals=transcendentals // scale,
        bytes_accessed=bytes_accessed // scale,
    )


def rope_cols(values, cosine, sine):
    lane = lax.broadcasted_iota(jnp.int32, cosine.shape, 1)
    low = (lane % HEAD) < (HEAD // 2)
    pieces = []
    for start in range(0, values.shape[1], 128):
        piece = values[:, start : start + 128]
        turned = jnp.where(low, pltpu.roll(piece, 96, 1), pltpu.roll(piece, 32, 1))
        pieces.append(piece * cosine + turned * sine)
    return pieces[0] if len(pieces) == 1 else jnp.concatenate(pieces, 1)


def seen(kc, i, kdoc_ref, qdoc, group):
    kdoc = kdoc_ref[pl.ds(pl.multiple_of(kc * BLK, BLK), BLK), :]
    kpos = kc * BLK + lax.broadcasted_iota(jnp.int32, (BLK, 1), 0)
    qpos = i * BLK + lax.broadcasted_iota(jnp.int32, (1, BLK), 1)
    visible = (kpos <= qpos) & (kdoc == qdoc)
    return jnp.where(visible, 0.0, NEG)


def attn_fwd_kernel(
    tok_ref, gain_ref, w_ref, cos_ref, sin_ref, kdoc_ref, qdoc_ref,
    na_ref, q_ref, k_ref, v_ref, att_ref, lse_ref, s_scr, *, q_heads, kv_heads,
):
    i = pl.program_id(0)
    group = q_heads // kv_heads
    tok = tok_ref[...].astype(F32)
    inv = lax.rsqrt(jnp.mean(tok * tok, -1, keepdims=True) + EPS)
    na = (tok * inv * gain_ref[...]).astype(BF16)
    na_ref[...] = na
    qkv = nn(na, w_ref[...])
    qk_cols = (q_heads + kv_heads) * HEAD
    roped = rope_cols(qkv[:, :qk_cols], cos_ref[...], sin_ref[...]).astype(BF16)
    vals = qkv[:, qk_cols:].astype(BF16)
    rows = pl.ds(pl.multiple_of(i * BLK, BLK), BLK)
    heads = [roped[:, h * HEAD : (h + 1) * HEAD] for h in range(q_heads + kv_heads)]
    for h in range(q_heads):
        q_ref[h] = heads[h]
    for g in range(kv_heads):
        k_ref[g, rows, :] = heads[q_heads + g]
        v_ref[g, rows, :] = vals[:, g * HEAD : (g + 1) * HEAD]
    lo = jnp.maximum(i - 2, 0)
    qdoc = qdoc_ref[...]
    groups = range(kv_heads)
    queries = [jnp.concatenate(heads[g * group : (g + 1) * group], 0) for g in groups]

    def scores(kc, tops):
        bias = seen(kc, i, kdoc_ref, qdoc, group)
        bias = jnp.concatenate([bias] * group, 1)
        rows = pl.ds(pl.multiple_of(kc * BLK, BLK), BLK)
        out = []
        for g in groups:
            s = nt(k_ref[g, rows, :], queries[g]) * ATTN_MULT + bias
            s_scr[g, kc - lo] = s
            out.append(jnp.maximum(tops[g], jnp.max(s, 0, keepdims=True)))
        return tuple(out)

    start = tuple(jnp.full((1, group * BLK), NEG, F32) for _ in groups)
    tops = lax.fori_loop(lo, i + 1, scores, start)

    def mix(kc, carry):
        rows = pl.ds(pl.multiple_of(kc * BLK, BLK), BLK)
        out = []
        for g in groups:
            total, mixed = carry[g]
            e = jnp.exp(s_scr[g, kc - lo] - tops[g])
            out.append(
                (
                    total + jnp.sum(e, 0, keepdims=True),
                    mixed + tn(v_ref[g, rows, :], e.astype(BF16)),
                )
            )
        return tuple(out)

    zero = (jnp.zeros((1, group * BLK), F32), jnp.zeros((HEAD, group * BLK), F32))
    sums = lax.fori_loop(lo, i + 1, mix, tuple(zero for _ in groups))
    for g in groups:
        total, out = sums[g]
        out = out / total
        lse_ref[0, g : g + 1, :] = tops[g] + jnp.log(total)
        for j in range(group):
            h = g * group + j
            att_ref[:, h * HEAD : (h + 1) * HEAD] = out[:, j * BLK : (j + 1) * BLK].T.astype(BF16)


def attn_fwd(tokens, gain, pack, cosine, sine, kdoc, qdoc, q_heads, kv_heads):
    length, width = tokens.shape
    blocks = length // BLK
    cols = (q_heads + 2 * kv_heads) * HEAD
    group = q_heads // kv_heads
    fixed = lambda i: (0, 0)
    fixed3 = lambda i: (0, 0, 0)
    row = lambda i: (i, 0)
    return pl.pallas_call(
        functools.partial(attn_fwd_kernel, q_heads=q_heads, kv_heads=kv_heads),
        grid=(blocks,),
        in_specs=[
            pl.BlockSpec((BLK, width), row),
            pl.BlockSpec((1, width), fixed),
            pl.BlockSpec((width, cols), fixed),
            pl.BlockSpec((BLK, 128), row),
            pl.BlockSpec((BLK, 128), row),
            pl.BlockSpec((length, 1), fixed),
            pl.BlockSpec((1, BLK), lambda i: (0, i)),
        ],
        out_specs=[
            pl.BlockSpec((BLK, width), row),
            pl.BlockSpec((q_heads, BLK, HEAD), lambda i: (0, i, 0)),
            pl.BlockSpec((kv_heads, length, HEAD), fixed3),
            pl.BlockSpec((kv_heads, length, HEAD), fixed3),
            pl.BlockSpec((BLK, q_heads * HEAD), row),
            pl.BlockSpec((1, kv_heads, group * BLK), lambda i: (i, 0, 0)),
        ],
        out_shape=[
            jax.ShapeDtypeStruct((length, width), BF16),
            jax.ShapeDtypeStruct((q_heads, length, HEAD), BF16),
            jax.ShapeDtypeStruct((kv_heads, length, HEAD), BF16),
            jax.ShapeDtypeStruct((kv_heads, length, HEAD), BF16),
            jax.ShapeDtypeStruct((length, q_heads * HEAD), BF16),
            jax.ShapeDtypeStruct((blocks, kv_heads, group * BLK), F32),
        ],
        scratch_shapes=[pltpu.VMEM((kv_heads, 3, BLK, group * BLK), F32)],
        compiler_params=pltpu.CompilerParams(
            dimension_semantics=("arbitrary",), vmem_limit_bytes=VMEM_CAP
        ),
        cost_estimate=cost(
            flops=2 * length * width * cols + 8 * length * 768 * q_heads * HEAD,
            transcendentals=length * 640 * q_heads,
            bytes_accessed=4 * length * width + 2 * width * cols,
            scale=100,
        ),
        name="attn_fwd",
    )(tokens, gain, pack, cosine, sine, kdoc, qdoc)


def attn_bwd_kernel(
    do_ref, q_ref, k_ref, v_ref, att_ref, lse_ref, cos_ref, sin_ref, kdoc_ref, qdoc_ref,
    dq_ref, dkv_ref, dk_scr, dv_scr, *, q_heads, kv_heads,
):
    i = pl.program_id(0)
    group = q_heads // kv_heads

    @pl.when(i == 0)
    def _():
        dk_scr[...] = jnp.zeros_like(dk_scr)
        dv_scr[...] = jnp.zeros_like(dv_scr)

    do = do_ref[...]
    lo = jnp.maximum(i - 2, 0)
    qdoc = qdoc_ref[...]
    att = att_ref[...]
    groups = range(kv_heads)
    queries, gives, dot_rows, lses = [], [], [], []
    for g in groups:
        span = range(g * group, (g + 1) * group)
        queries.append(jnp.concatenate([q_ref[h] for h in span], 0))
        gives.append(jnp.concatenate([do[:, h * HEAD : (h + 1) * HEAD] for h in span], 0))
        outs = jnp.concatenate([att[:, h * HEAD : (h + 1) * HEAD] for h in span], 0)
        dot_rows.append(
            jnp.sum((gives[g].astype(F32) * outs.astype(F32)).T, 0, keepdims=True)
        )
        lses.append(lse_ref[0, g : g + 1, :])

    def chunk(kc, dqs):
        rows = pl.ds(pl.multiple_of(kc * BLK, BLK), BLK)
        bias = seen(kc, i, kdoc_ref, qdoc, group)
        bias = jnp.concatenate([bias] * group, 1)
        out = []
        for g in groups:
            keys = k_ref[g, rows, :]
            prob = jnp.exp(nt(keys, queries[g]) * ATTN_MULT + bias - lses[g])
            dprob = nt(v_ref[g, rows, :], gives[g])
            ds = (prob * (dprob - dot_rows[g])).astype(BF16)
            dv_scr[g, rows, :] += nn(prob.astype(BF16), gives[g])
            dk_scr[g, rows, :] += nn(ds, queries[g])
            out.append(dqs[g] + tn(keys, ds))
        return tuple(out)

    zero = jnp.zeros((HEAD, group * BLK), F32)
    dqs = lax.fori_loop(lo, i + 1, chunk, tuple(zero for _ in groups))
    dq_heads = [dqs[g][:, j * BLK : (j + 1) * BLK].T for g in groups for j in range(group)]
    rows = pl.ds(pl.multiple_of(i * BLK, BLK), BLK)
    dq_all = jnp.concatenate(dq_heads, 1) * ATTN_MULT
    dq_ref[...] = rope_cols(dq_all, cos_ref[rows, :], -sin_ref[rows, :]).astype(BF16)

    @pl.when(i == pl.num_programs(0) - 1)
    def _():
        dk = jnp.concatenate([dk_scr[g] for g in range(kv_heads)], 1) * ATTN_MULT
        kcols = kv_heads * HEAD
        dkv_ref[:, :kcols] = rope_cols(dk, cos_ref[...], -sin_ref[...]).astype(BF16)
        dkv_ref[:, kcols:] = jnp.concatenate([dv_scr[g] for g in range(kv_heads)], 1).astype(BF16)


def attn_bwd(do, q, k, v, att, lse, cosine, sine, kdoc, qdoc):
    length = do.shape[0]
    q_heads, kv_heads = q.shape[0], k.shape[0]
    blocks = length // BLK
    group = q_heads // kv_heads
    fixed = lambda i: (0, 0)
    fixed3 = lambda i: (0, 0, 0)
    row = lambda i: (i, 0)
    return pl.pallas_call(
        functools.partial(attn_bwd_kernel, q_heads=q_heads, kv_heads=kv_heads),
        grid=(blocks,),
        in_specs=[
            pl.BlockSpec((BLK, q_heads * HEAD), row),
            pl.BlockSpec((q_heads, BLK, HEAD), lambda i: (0, i, 0)),
            pl.BlockSpec((kv_heads, length, HEAD), fixed3),
            pl.BlockSpec((kv_heads, length, HEAD), fixed3),
            pl.BlockSpec((BLK, q_heads * HEAD), row),
            pl.BlockSpec((1, kv_heads, group * BLK), lambda i: (i, 0, 0)),
            pl.BlockSpec((length, 128), fixed),
            pl.BlockSpec((length, 128), fixed),
            pl.BlockSpec((length, 1), fixed),
            pl.BlockSpec((1, BLK), lambda i: (0, i)),
        ],
        out_specs=[
            pl.BlockSpec((BLK, q_heads * HEAD), row),
            pl.BlockSpec((length, 2 * kv_heads * HEAD), fixed),
        ],
        out_shape=[
            jax.ShapeDtypeStruct((length, q_heads * HEAD), BF16),
            jax.ShapeDtypeStruct((length, 2 * kv_heads * HEAD), BF16),
        ],
        scratch_shapes=[
            pltpu.VMEM((kv_heads, length, HEAD), F32),
            pltpu.VMEM((kv_heads, length, HEAD), F32),
        ],
        compiler_params=pltpu.CompilerParams(
            dimension_semantics=("arbitrary",), vmem_limit_bytes=VMEM_CAP
        ),
        cost_estimate=cost(
            flops=20 * length * 768 * q_heads * HEAD,
            transcendentals=length * 640 * q_heads,
            bytes_accessed=8 * length * q_heads * HEAD,
        ),
        name="attn_bwd",
    )(do, q, k, v, att, lse, cosine, sine, kdoc, qdoc)


def mid_kernel(
    att_ref, wo_ref, tok_ref, gain_ref, small_ref, routes_ref, mid_ref, nm_ref, gate_ref, flat_ref
):
    att = jnp.concatenate([att_ref[k] for k in range(att_ref.shape[0])], 1)
    flat_ref[...] = att
    branch = nt(att, wo_ref[...])
    middle = tok_ref[...].astype(F32) + RESID * branch
    mid_ref[...] = middle
    inv = lax.rsqrt(jnp.mean(middle * middle, -1, keepdims=True) + EPS)
    nm = (middle * inv * gain_ref[...]).astype(BF16)
    nm_ref[...] = nm
    logits = nn(nm, small_ref[...])
    lane = lax.broadcasted_iota(jnp.int32, logits.shape, 1)
    chosen = lane == routes_ref[:, 0:1]
    for c in range(1, routes_ref.shape[1]):
        chosen = chosen | (lane == routes_ref[:, c : c + 1])
    logits = jnp.where(chosen, logits, NEG)
    e = jnp.exp(logits - jnp.max(logits, -1, keepdims=True))
    gate_ref[...] = e / jnp.sum(e, -1, keepdims=True)


def mid_fwd(att_all, wo_rows, tokens, gain, pack, small_at, routes):
    length, width = tokens.shape
    parts, _, cols = att_all.shape
    blocks = length // BLK
    fixed = lambda i: (0, 0)
    row = lambda i: (i, 0)
    return pl.pallas_call(
        mid_kernel,
        grid=(blocks,),
        in_specs=[
            pl.BlockSpec((parts, BLK, cols), lambda i: (0, i, 0)),
            pl.BlockSpec((width, parts * cols), fixed),
            pl.BlockSpec((BLK, width), row),
            pl.BlockSpec((1, width), fixed),
            pl.BlockSpec((width, 128), lambda i: (0, small_at)),
            pl.BlockSpec((BLK, routes.shape[1]), row),
        ],
        out_specs=[
            pl.BlockSpec((BLK, width), row),
            pl.BlockSpec((BLK, width), row),
            pl.BlockSpec((BLK, 128), row),
            pl.BlockSpec((BLK, parts * cols), row),
        ],
        out_shape=[
            jax.ShapeDtypeStruct((length, width), F32),
            jax.ShapeDtypeStruct((length, width), BF16),
            jax.ShapeDtypeStruct((length, 128), F32),
            jax.ShapeDtypeStruct((length, parts * cols), BF16),
        ],
        compiler_params=pltpu.CompilerParams(
            dimension_semantics=("arbitrary",), vmem_limit_bytes=VMEM_CAP
        ),
        cost_estimate=cost(
            flops=2 * length * width * cols * parts,
            transcendentals=length * 128,
            bytes_accessed=10 * length * width + 2 * width * cols * parts,
        ),
        name="mid_fwd",
    )(att_all, wo_rows, tokens, gain, pack, routes)


def norm_back(n_grad, values, gain):
    inv = lax.rsqrt(jnp.mean(values * values, -1, keepdims=True) + EPS)
    scaled = n_grad * gain
    return inv * (scaled - values * (inv * inv) * jnp.mean(scaled * values, -1, keepdims=True))


def back_mid_kernel(
    own_ref, back_ref, recv_ref, lg_ref, small_ref, mid_ref, gain_ref, cot_ref, wo_ref, ag_ref, p_ref
):
    n_grad = back_ref[...].astype(F32) + recv_ref[...].astype(F32) + nt(lg_ref[...], small_ref[...])
    grad = norm_back(n_grad, mid_ref[...], gain_ref[...])
    own = (pl.program_id(0) == own_ref[0]).astype(F32)
    ag = (RESID * (grad + own * cot_ref[...].astype(F32))).astype(BF16)
    ag_ref[...] = ag
    out = nn(ag, wo_ref[...]).astype(BF16)
    cols = p_ref.shape[2]
    for k in range(p_ref.shape[0]):
        p_ref[k] = out[:, k * cols : (k + 1) * cols]


def back_mid(own, back, recv, logit_grad, pack, small_at, middle, gain, cot, wo_rows, parts):
    length, width = middle.shape
    blocks = length // BLK
    cols = wo_rows.shape[1] // parts
    fixed = lambda i, o: (0, 0)
    row = lambda i, o: (i, 0)
    return pl.pallas_call(
        back_mid_kernel,
        grid_spec=pltpu.PrefetchScalarGridSpec(
            num_scalar_prefetch=1,
            grid=(blocks,),
            in_specs=[
                pl.BlockSpec((BLK, width), row),
                pl.BlockSpec((BLK, width), row),
                pl.BlockSpec((BLK, 128), row),
                pl.BlockSpec((width, 128), lambda i, o: (0, small_at)),
                pl.BlockSpec((BLK, width), row),
                pl.BlockSpec((1, width), fixed),
                pl.BlockSpec((BLK, width), fixed),
                pl.BlockSpec((width, parts * cols), fixed),
            ],
            out_specs=[
                pl.BlockSpec((BLK, width), row),
                pl.BlockSpec((parts, BLK, cols), lambda i, o: (0, i, 0)),
            ],
        ),
        out_shape=[
            jax.ShapeDtypeStruct((length, width), BF16),
            jax.ShapeDtypeStruct((parts, length, cols), BF16),
        ],
        compiler_params=pltpu.CompilerParams(
            dimension_semantics=("arbitrary",), vmem_limit_bytes=VMEM_CAP
        ),
        cost_estimate=cost(
            flops=2 * length * width * cols * parts,
            transcendentals=0,
            bytes_accessed=12 * length * width + 2 * width * cols * parts,
        ),
        name="back_mid",
    )(own, back, recv, logit_grad, pack, middle, gain, cot, wo_rows)


def back_end_kernel(dq_ref, dkv_ref, w_ref, tok_ref, gain_ref, ag_ref, out_ref):
    d_all = jnp.concatenate([dq_ref[...], dkv_ref[...]], 1)
    n_grad = nt(d_all, w_ref[...])
    grad = norm_back(n_grad, tok_ref[...].astype(F32), gain_ref[...])
    out_ref[...] = (grad + ag_ref[...].astype(F32) * (1.0 / RESID)).astype(BF16)


def back_end(dq, dkv, pack, tokens, gain, ag):
    length, width = tokens.shape
    cols = dq.shape[1] + dkv.shape[1]
    fixed = lambda i: (0, 0)
    row = lambda i: (i, 0)
    return pl.pallas_call(
        back_end_kernel,
        grid=(length // BLK,),
        in_specs=[
            pl.BlockSpec((BLK, dq.shape[1]), row),
            pl.BlockSpec((BLK, dkv.shape[1]), row),
            pl.BlockSpec((width, cols), fixed),
            pl.BlockSpec((BLK, width), row),
            pl.BlockSpec((1, width), fixed),
            pl.BlockSpec((BLK, width), row),
        ],
        out_specs=pl.BlockSpec((BLK, width), row),
        out_shape=jax.ShapeDtypeStruct((length, width), BF16),
        compiler_params=pltpu.CompilerParams(
            dimension_semantics=("arbitrary",), vmem_limit_bytes=VMEM_CAP
        ),
        cost_estimate=cost(
            flops=2 * length * width * cols,
            transcendentals=0,
            bytes_accessed=6 * length * width + 2 * width * cols,
        ),
        name="back_end",
    )(dq, dkv, pack, tokens, gain, ag)


def sigmoid(value):
    return 0.5 * jnp.tanh(0.5 * value) + 0.5


def gate_cols(gates, first):
    lane = lax.broadcasted_iota(jnp.int32, gates.shape, 1)
    return [
        jnp.sum(jnp.where(lane == first + k, gates, 0.0), -1, keepdims=True) for k in range(2)
    ]


def moe_fwd_kernel(base_ref, x_ref, w_ref, gate_ref, h_ref, gact_ref):
    p = pl.program_id(1)
    h = nn(x_ref[...], w_ref[...])
    h_ref[...] = h.astype(BF16)
    cols = gate_cols(gate_ref[...], base_ref[0] + 2 * p)
    for k in range(2):
        gate = h[:, 256 * k : 256 * k + 128]
        up = h[:, 256 * k + 128 : 256 * k + 256]
        act = gate * sigmoid(gate) * up
        gact_ref[:, 128 * k : 128 * k + 128] = (cols[k] * act).astype(BF16)


def moe_fwd(base, x, w_in, gates, rows, scale):
    length, width = x.shape
    cols = w_in.shape[1]
    return pl.pallas_call(
        moe_fwd_kernel,
        grid_spec=pltpu.PrefetchScalarGridSpec(
            num_scalar_prefetch=1,
            grid=(length // rows, cols // 512),
            in_specs=[
                pl.BlockSpec((rows, width), lambda i, p, b: (i, 0)),
                pl.BlockSpec((width, 512), lambda i, p, b: (0, p)),
                pl.BlockSpec((rows, 128), lambda i, p, b: (i, 0)),
            ],
            out_specs=[
                pl.BlockSpec((rows, 512), lambda i, p, b: (i, p)),
                pl.BlockSpec((rows, 256), lambda i, p, b: (i, p)),
            ],
        ),
        out_shape=[
            jax.ShapeDtypeStruct((length, cols), BF16),
            jax.ShapeDtypeStruct((length, cols // 2), BF16),
        ],
        compiler_params=pltpu.CompilerParams(
            dimension_semantics=("arbitrary", "arbitrary"), vmem_limit_bytes=VMEM_CAP
        ),
        cost_estimate=cost(
            flops=2 * length * width * cols,
            transcendentals=length * cols // 2,
            bytes_accessed=2 * length * (width + cols + cols // 2) + 4 * width * cols,
            scale=scale,
        ),
        name="moe_fwd",
    )(base, x, w_in, gates)


def combine_kernel(*refs):
    gact_ref, pieces, out_ref, w_scr = refs[0], refs[1:-2], refs[-2], refs[-1]

    @pl.when(pl.program_id(0) == 0)
    def _():
        at = 0
        for piece in pieces:
            w_scr[at : at + piece.shape[0], :] = piece[...]
            at += piece.shape[0]

    out_ref[...] = nt(gact_ref[...], w_scr[...]).astype(BF16)


def combine(gact, pieces, rows):
    length, cols = gact.shape
    width = sum(p.shape[0] for p in pieces)
    return pl.pallas_call(
        combine_kernel,
        grid=(length // rows,),
        in_specs=[pl.BlockSpec((rows, cols), lambda i: (i, 0))]
        + [pl.BlockSpec(p.shape, lambda i: (0, 0)) for p in pieces],
        out_specs=pl.BlockSpec((rows, width), lambda i: (i, 0)),
        out_shape=jax.ShapeDtypeStruct((length, width), BF16),
        scratch_shapes=[pltpu.VMEM((width, cols), BF16)],
        compiler_params=pltpu.CompilerParams(
            dimension_semantics=("arbitrary",), vmem_limit_bytes=VMEM_CAP
        ),
        cost_estimate=cost(
            flops=2 * length * width * cols,
            transcendentals=0,
            bytes_accessed=2 * (length * width + length * cols + width * cols),
        ),
        name="combine",
    )(gact, *pieces)


def moe_bwd_kernel(*refs):
    base_ref, g_ref, gate_ref, h_ref = refs[:4]
    pieces, gug_ref, choice_ref, plain_scr = refs[4:-3], refs[-3], refs[-2], refs[-1]
    p = pl.program_id(1)
    first = base_ref[0] + 2 * (p - 1)
    plain = plain_scr[1 - p % 2]
    cols = gate_cols(gate_ref[...], first)
    lane = lax.broadcasted_iota(jnp.int32, choice_ref.shape, 1)
    add = jnp.zeros(choice_ref.shape, F32)
    for k in range(2):
        gate = h_ref[:, 256 * k : 256 * k + 128].astype(F32)
        up = h_ref[:, 256 * k + 128 : 256 * k + 256].astype(F32)
        part = plain[:, 128 * k : 128 * k + 128]
        sig = sigmoid(gate)
        silu = gate * sig
        add = jnp.where(lane == first + k, jnp.sum(silu * up * part, -1, keepdims=True), add)
        act_grad = cols[k] * part
        gug_ref[:, 256 * k : 256 * k + 128] = (act_grad * up * (sig + silu * (1.0 - sig))).astype(
            BF16
        )
        gug_ref[:, 256 * k + 128 : 256 * k + 256] = (act_grad * silu).astype(BF16)
    choice_ref[...] = jnp.where(p > 1, choice_ref[...], 0.0) + jnp.where(p > 0, add, 0.0)
    weights = [piece[...] for piece in pieces]
    plain_scr[p % 2] = nn(g_ref[...], weights[0] if len(weights) == 1 else jnp.concatenate(weights, 0))


def moe_bwd(base, g, pieces, gates, h, rows):
    length, width = g.shape
    cols = h.shape[1]
    steps = cols // 512
    behind = lambda i, p, b: (i, jnp.maximum(p - 1, 0))
    return pl.pallas_call(
        moe_bwd_kernel,
        grid_spec=pltpu.PrefetchScalarGridSpec(
            num_scalar_prefetch=1,
            grid=(length // rows, steps + 1),
            in_specs=[
                pl.BlockSpec((rows, width), lambda i, p, b: (i, 0)),
                pl.BlockSpec((rows, 128), lambda i, p, b: (i, 0)),
                pl.BlockSpec((rows, 512), behind),
            ]
            + [
                pl.BlockSpec((w.shape[0], 256), lambda i, p, b: (0, jnp.minimum(p, steps - 1)))
                for w in pieces
            ],
            out_specs=[
                pl.BlockSpec((rows, 512), behind),
                pl.BlockSpec((rows, 128), lambda i, p, b: (i, 0)),
            ],
            scratch_shapes=[pltpu.VMEM((2, rows, 256), F32)],
        ),
        out_shape=[
            jax.ShapeDtypeStruct((length, cols), BF16),
            jax.ShapeDtypeStruct((length, 128), F32),
        ],
        compiler_params=pltpu.CompilerParams(
            dimension_semantics=("arbitrary", "arbitrary"), vmem_limit_bytes=VMEM_CAP
        ),
        cost_estimate=cost(
            flops=length * width * cols,
            transcendentals=length * cols // 2,
            bytes_accessed=2 * length * (width + 2 * cols) + 2 * width * cols,
        ),
        name="moe_bwd",
    )(base, g, gates, h, *pieces)


def segment_kernel(*refs, count):
    lefts, rights, outs = refs[:4], refs[4:6], refs[6:]
    first = tn(jnp.concatenate([lefts[0][...], lefts[1][...]], 1), rights[0][...])
    second = tn(jnp.concatenate([lefts[2][...], lefts[3][...]], 1), rights[1][...])
    value = (first + second).astype(BF16)
    for k in range(count):

        @pl.when(pl.program_id(0) == k)
        def _(k=k):
            outs[k][...] = value


def pick(s, values):
    out = values[0]
    for k in range(1, len(values)):
        out = jnp.where(s == k, values[k], out)
    return out


def weight_grad(left, left2, right, right2, segments):
    length, width = left.shape
    cols = right.shape[1] // 2
    quarter = width // 4
    wide = min(cols, 768)
    steps = cols // wide
    count = len(segments)
    firsts, seconds, halves = zip(*segments, strict=True)
    one = pl.BlockSpec((length, quarter), lambda s, j: (0, pick(s, firsts)))
    two = pl.BlockSpec((length, quarter), lambda s, j: (0, pick(s, seconds)))
    side = pl.BlockSpec((length, wide), lambda s, j: (0, pick(s, halves) * steps + j))

    def place(k):
        return pl.BlockSpec(
            (2 * quarter, wide),
            lambda s, j: (0, jnp.where(s == k, j, jnp.where(s < k, 0, steps - 1))),
        )

    return pl.pallas_call(
        functools.partial(segment_kernel, count=count),
        grid=(count, steps),
        in_specs=[one, two, one, two, side, side],
        out_specs=[place(k) for k in range(count)],
        out_shape=[jax.ShapeDtypeStruct((2 * quarter, cols), BF16)] * count,
        compiler_params=pltpu.CompilerParams(
            dimension_semantics=("arbitrary", "arbitrary"), vmem_limit_bytes=VMEM_CAP
        ),
        cost_estimate=cost(
            flops=2 * count * length * width * cols,
            transcendentals=0,
            bytes_accessed=4 * length * (width + 2 * cols),
            scale=100,
        ),
        name="weight_grad",
    )(left, left, left2, left2, right, right2)


def swap(value, axis, bit, size):
    return lax.ppermute(value, axis, [(i, i ^ bit) for i in range(size)])


def reorder(value, q, quads):
    if quads != 4:
        return value
    n = value.shape[-1] // 4
    b = [value[..., k * n : (k + 1) * n] for k in (0, 1, 3, 2)]
    odd = (q & 1) == 1
    far = (q & 2) == 2
    c = [jnp.where(odd, b[k], b[j]) for j, k in ((0, 1), (1, 0), (2, 3), (3, 2))]
    return jnp.concatenate([jnp.where(far, c[k], c[j]) for j, k in ((0, 3), (1, 2), (2, 1), (3, 0))], -1)


def restore(value, q, quads):
    if quads != 4:
        return value
    n = value.shape[-1] // 4
    b = [value[..., k * n : (k + 1) * n] for k in (0, 1, 3, 2)]
    odd = (q & 1) == 1
    far = (q & 2) == 2
    c = [jnp.where(odd, b[k ^ 1], b[k]) for k in range(4)]
    return jnp.concatenate([jnp.where(far, c[k ^ 2], c[k]) for k in range(4)], -1)


def gather_first(low, high, quads):
    if quads != 4:
        return (lax.all_gather(jnp.concatenate([low, high], 0), "q", axis=0, tiled=True),)
    return swap(low, "q", 1, 4), swap(high, "q", 2, 4)


def gather_rest(low, high, quads):
    if quads != 4:
        return ()
    return swap(high, "q", 1, 4), swap(low, "q", 2, 4)


def gather_diagonal(first, quads):
    if quads != 4:
        return ()
    return swap(first[0], "q", 2, 4), swap(first[1], "q", 1, 4)


def gather_join(low, high, first, rest, diagonal, quads):
    if quads != 4:
        return first[0]
    return jnp.concatenate(
        [low, high, first[0], rest[0], diagonal[0], diagonal[1], rest[1], first[1]], 0
    )


def gather_pieces(low, high, first, rest, diagonal, quads):
    if quads != 4:
        return first
    return (low, high, first[0], rest[0], diagonal[0], diagonal[1], rest[1], first[1])


def gather_rows(low, high, quads):
    first = gather_first(low, high, quads)
    rest = gather_rest(low, high, quads)
    return gather_join(low, high, first, rest, gather_diagonal(first, quads), quads)


SEND_LEFT, SEND_RIGHT, KEEP_LEFT, KEEP_RIGHT = (2, 3, 0), (2, 1, 1), (0, 1, 0), (0, 3, 1)


def cut(value, segment):
    n, half = value.shape[0] // 4, (value.shape[1] // 2 + 127) // 128 * 128
    side = value[:, half:] if segment[2] else value[:, :half]
    return jnp.concatenate([side[k * n : (k + 1) * n] for k in segment[:2]], 0)


def scatter_first(left, right):
    return swap(left, "q", 2, 4), swap(right, "q", 1, 4)


def scatter_second(keep_left, keep_right, from_y, from_x):
    n = keep_left.shape[0] // 2
    give_x = (keep_left[n:].astype(F32) + from_y[:n].astype(F32)).astype(BF16)
    give_y = (keep_right[n:].astype(F32) + from_x[:n].astype(F32)).astype(BF16)
    give_x, give_y = lax.optimization_barrier((give_x, give_y))
    arrived = swap(give_x, "q", 1, 4), swap(give_y, "q", 2, 4)
    return arrived, (give_x, give_y)


def scatter_last(keep_left, keep_right, from_y, from_x, arrived, *others):
    n = keep_left.shape[0] // 2
    keep_left, keep_right, from_y, from_x, left, right = all_after(
        (keep_left, keep_right, from_y, from_x, *arrived), *others
    )
    return (
        (keep_left[:n].astype(F32) + from_y[n:].astype(F32) + left.astype(F32)).astype(BF16),
        (keep_right[:n].astype(F32) + from_x[n:].astype(F32) + right.astype(F32)).astype(BF16),
    )


def scatter_plain(value):
    total = lax.psum_scatter(value, "q", scatter_dimension=0, tiled=True)
    half = total.shape[1] // 2
    return total[:, :half], total[:, half:]


def after(value, *others):
    return lax.optimization_barrier((value, *others))[0]


def all_after(values, *others):
    return lax.optimization_barrier((*values, *others))[: len(values)]


def to_halves(mine, give, c):
    other = swap(give, "c", 1, 2)
    first = c == 0
    return jnp.where(first, mine, other), jnp.where(first, other, mine)


def from_halves(totals, rows, c):
    def take(at):
        return jnp.concatenate([lax.dynamic_slice_in_dim(t, at * rows, rows, 0) for t in totals], 1)

    return take(c), swap(take(1 - c), "c", 1, 2)


def in_order(mine, other, c):
    return jnp.where(c == 0, mine, other), jnp.where(c == 0, other, mine)


def column_halves(value, c):
    n = value.shape[1] // 2
    mine = jnp.where(c == 0, value[:, :n], value[:, n:])
    give = jnp.where(c == 0, value[:, n:], value[:, :n])
    return mine, give


def whole_columns(half, c):
    other = swap(half, "c", 1, 2)
    return jnp.where(c == 0, half, other), jnp.where(c == 0, other, half)


def body(
    tokens, attn_gain, w_query, key_weight, value_weight, w_output, router, moe_gain, w_in, w_out,
    segments, routes, cotangent, *, quads,
):
    q = lax.axis_index("q")
    c = lax.axis_index("c")
    m = lax.axis_index("mp")
    length = segments.shape[1]
    width = tokens.shape[2]
    rows = w_query.shape[0]
    experts = router.shape[1]
    half_e = experts // 2
    ff = w_out.shape[2]
    q_heads = w_query.shape[1] // HEAD
    kv_heads = key_weight.shape[1] // HEAD
    q_cols, kv_cols = q_heads * HEAD, kv_heads * HEAD
    qkv_cols = q_cols + 2 * kv_cols
    mp = lax.axis_size("mp")

    tok_own = reorder(tokens[0], q, quads)
    tok_all = lax.all_gather(tok_own, "mp", axis=0, tiled=True)

    def half_rows(value):
        mine = lax.dynamic_slice_in_dim(value, c * half_e, half_e, 1).reshape(rows, -1)
        give = lax.dynamic_slice_in_dim(value, (1 - c) * half_e, half_e, 1).reshape(rows, -1)
        return to_halves(mine, give, c), mine, give

    in_pair, in_kept, in_gave = half_rows(w_in)

    pad = jnp.zeros((rows, 128 - experts - 2), BF16)
    pack = jnp.concatenate(
        [w_query, key_weight, value_weight, router, attn_gain[:, None], moe_gain[:, None], pad], 1
    )
    pack_pair = to_halves(*column_halves(after(pack, in_gave, in_kept), c), c)
    pack_pair = all_after(pack_pair, *in_pair)
    pack_first = gather_first(*pack_pair, quads)
    pack_rest = gather_rest(*pack_pair, quads)
    pack_half = gather_join(
        *pack_pair, pack_first, pack_rest, gather_diagonal(pack_first, quads), quads
    )
    pack = jnp.concatenate(whole_columns(pack_half, c), 1)
    small_at = qkv_cols // 128
    gains = pack[:, qkv_cols + experts : qkv_cols + experts + 2].astype(F32)
    attn_g = gains[:, 0].reshape(1, width)
    moe_g = gains[:, 1].reshape(1, width)

    doc_row = segments
    doc_col = segments.reshape(length, 1)
    lane = jnp.arange(128, dtype=jnp.int32) % (HEAD // 2)
    freq = ROPE_BASE ** (-lane.astype(F32) * 2.0 / HEAD)
    angles = jnp.arange(length).astype(F32)[:, None] * freq[None, :]
    cosine = jnp.cos(angles)
    upper = (jnp.arange(128, dtype=jnp.int32) % HEAD) < (HEAD // 2)
    sine = jnp.where(upper[None, :], -jnp.sin(angles), jnp.sin(angles))

    out_pair, _, _ = half_rows(after(w_out, *pack_pair))
    in_src = in_pair
    in_got = gather_first(*in_src, quads)
    in_rest = gather_rest(*in_src, quads)

    normed_a, q_r, k_r, v_r, attended, lse = attn_fwd(
        tok_all, attn_g, pack, cosine, sine, doc_col, doc_row, q_heads, kv_heads
    )

    wo_pad = jnp.concatenate([w_output, jnp.zeros((rows, 5 * 64), BF16)], 1)
    wo_cols = lax.all_gather(after(wo_pad, pack), "mp", axis=0, tiled=False)
    wo_cols = jnp.concatenate([wo_cols[j, :, :q_cols] for j in range(mp)], 1)
    wo_pair = to_halves(*column_halves(after(wo_cols, attended), c), c)
    in_diag = gather_diagonal(in_got, quads)
    wo_src = all_after(wo_pair, *in_diag)
    wo_got, wo_rest = gather_first(*wo_src, quads), gather_rest(*wo_src, quads)
    out_src = all_after(out_pair, *wo_got, *wo_rest)
    out_got, out_rest = gather_first(*out_src, quads), gather_rest(*out_src, quads)
    wo_half = gather_join(*wo_src, wo_got, wo_rest, gather_diagonal(wo_got, quads), quads)
    step = width // 4
    wo_other = jnp.concatenate(
        [swap(wo_half[k * step : (k + 1) * step], "c", 1, 2) for k in range(4)], 0
    )
    wo_rows = jnp.concatenate(in_order(*lax.optimization_barrier((wo_half, wo_other)), c), 1)
    join = (*in_src, *in_got, *in_rest, *in_diag)
    join = all_after(join, *wo_got)
    in_full = gather_join(
        *join[:2], join[2 : 2 + len(in_got)], join[2 + len(in_got) : 2 + len(in_got) + len(in_rest)],
        join[2 + len(in_got) + len(in_rest) :], quads,
    )

    att_all = lax.all_gather(after(attended, *in_got, *in_rest, *out_pair), "mp", axis=0, tiled=False)
    middle, normed_m, gates, att_flat = mid_fwd(
        after(att_all, in_full, *out_got), wo_rows, tok_all, moe_g, pack, small_at, routes[0]
    )

    cot_own = lax.optimization_barrier(reorder(cotangent[0], q, quads))
    moe_grad = (RESID * cot_own.astype(F32)).astype(BF16)
    grad_all = lax.all_gather(after(moe_grad, attended), "mp", axis=0, tiled=True)

    x_own = normed_m
    x_other = swap(normed_m, "c", 1, 2)
    gates_other = swap(gates, "c", 1, 2)
    base = (c * half_e).astype(jnp.int32).reshape(1)
    hid_own, gact_own = moe_fwd(
        base, x_own, in_full, gates, length, 100
    )
    x_other = after(x_other, gact_own, *out_rest)
    out_diag = gather_diagonal(all_after(out_got, gact_own), quads)
    out_full = gather_pieces(*out_src, out_got, out_rest, out_diag, quads)
    hid_other, gact_other = moe_fwd(base, x_other, in_full, gates_other, length, 1)
    comb_give = combine(gact_other, out_full, length // 2)
    comb_recv = swap(comb_give, "c", 1, 2)
    comb_own = combine(after(gact_own, comb_give, grad_all), out_full, length // 2)
    combined = (comb_own.astype(F32) + comb_recv.astype(F32)).astype(BF16)
    moe_branch = lax.psum_scatter(combined, "mp", scatter_dimension=0, tiled=True).astype(F32)

    g_other = swap(after(grad_all, comb_give), "c", 1, 2)
    gacts = all_after((gact_own, gact_other), comb_own)
    if quads == 4:
        out_send = weight_grad(
            grad_all, g_other, *gacts, (SEND_LEFT, SEND_RIGHT, KEEP_LEFT, KEEP_RIGHT)
        )
        out_keep = out_send[2:]
        out_move = scatter_first(*out_send[:2])
    else:
        g2, gact2 = jnp.concatenate([grad_all, g_other], 0), jnp.concatenate(gacts, 0)
        out_move = out_keep = (tn(g2, gact2).astype(BF16),)
    gug_own, choice_own = moe_bwd(
        base, grad_all, out_full, gates, after(hid_own, *out_keep), length
    )
    gug_other, choice_other = moe_bwd(base, g_other, out_full, gates_other, after(hid_other, gug_own), length)
    choice = choice_own + swap(choice_other, "c", 1, 2)
    back_give = nt(after(gug_other, *out_move), in_full).astype(BF16)
    back_recv = swap(back_give, "c", 1, 2)
    gug_late = after(gug_own, back_give)
    back_own = nt(gug_late, in_full).astype(BF16)
    gates_c = gates * choice
    logit_grad = (gates_c - gates * jnp.sum(gates_c, -1, keepdims=True)).astype(BF16)
    out_late = scatter_second(*out_keep, *out_move)[0] if quads == 4 else ()
    ag, p_part = back_mid(
        m.astype(jnp.int32).reshape(1), back_own, back_recv, logit_grad, pack, small_at,
        after(middle, moe_branch, *out_late), moe_g, cot_own, wo_rows, mp,
    )
    attended_grad = lax.psum_scatter(p_part, "mp", scatter_dimension=0, tiled=False)

    gugs = all_after((gug_own, gug_other), ag)
    if quads == 4:
        in_send = weight_grad(x_own, x_other, *gugs, (SEND_LEFT, SEND_RIGHT))
        in_move = scatter_first(*in_send)
        in_keep = weight_grad(
            x_own, x_other, *all_after(gugs, *in_send), (KEEP_LEFT, KEEP_RIGHT)
        )
    else:
        in_move = in_keep = (tn(jnp.concatenate([x_own, x_other], 0), jnp.concatenate(gugs, 0)).astype(BF16),)
    att_late = after(att_flat, *in_send) if quads == 4 else att_flat
    half_cols = att_flat.shape[1] // 2
    low_att, high_att = att_late[:, :half_cols], att_late[:, half_cols:]
    wo_give = tn(ag, jnp.where(c == 0, high_att, low_att)).astype(BF16)
    wo_mine = tn(ag, after(jnp.where(c == 0, low_att, high_att), wo_give)).astype(BF16)
    wo_part = (wo_mine.astype(F32) + swap(wo_give, "c", 1, 2).astype(F32)).astype(BF16)
    if quads == 4:
        wo_keep = (cut(wo_part, KEEP_LEFT), cut(wo_part, KEEP_RIGHT))
        wo_move = scatter_first(cut(wo_part, SEND_LEFT), cut(wo_part, SEND_RIGHT))
    dq, dkv = attn_bwd(
        attended_grad, q_r, k_r, v_r, attended, lse, cosine, sine, doc_col, doc_row
    )
    end_part = back_end(dq, dkv, pack, tok_all, attn_g, ag)
    grad_tokens = lax.psum_scatter(end_part, "mp", scatter_dimension=0, tiled=True).astype(F32)

    layer_out = (
        lax.dynamic_slice_in_dim(middle, m * (length // mp), length // mp, 0) + RESID * after(moe_branch, end_part)
    ).astype(BF16)

    given = (end_part,)
    if quads == 4:
        in_move = all_after(in_move, end_part)
        in_late, given = scatter_second(*in_keep, *in_move)
        wo_move = all_after(wo_move, *given)
        wo_late, _ = scatter_second(*wo_keep, *wo_move)
    dq_late, dkv_late = after(dq, *given), after(dkv, *given)
    part = jnp.concatenate(
        [tn(normed_a, dq_late), tn(normed_a, dkv_late), tn(normed_m, after(logit_grad, *given))], 1
    ).astype(BF16)
    mine, give = column_halves(part, c)
    pair = (mine.astype(F32) + swap(give, "c", 1, 2).astype(F32)).astype(BF16)
    if quads == 4:
        pair_keep = (cut(pair, KEEP_LEFT), cut(pair, KEEP_RIGHT))
        pair_move = scatter_first(cut(pair, SEND_LEFT), cut(pair, SEND_RIGHT))
        *pair_move, in_left, in_right = lax.optimization_barrier((*pair_move, *in_late))
        in_late = (in_left, in_right)
        pair_late, _ = scatter_second(*pair_keep, *pair_move)
        in_sum = scatter_last(*in_keep, *in_move, in_late)
        wo_sum = scatter_last(*wo_keep, *wo_move, wo_late)
        pair_sum = scatter_last(*pair_keep, *pair_move, pair_late)
        out_sum = scatter_last(*out_keep, *out_move, out_late, end_part)
    else:
        in_sum, wo_sum, pair_sum, out_sum = (
            scatter_plain(v) for v in (in_keep[0], wo_part, pair, out_keep[0])
        )
    late_sum = (*wo_sum, *pair_sum)
    late_mine, late_other = from_halves(late_sum, rows, c)
    wo_cols_here = wo_part.shape[1]
    wo_own_rows = jnp.concatenate(
        in_order(late_mine[:, :wo_cols_here], late_other[:, :wo_cols_here], c), 1
    )
    sums = jnp.concatenate(
        in_order(late_mine[:, wo_cols_here:], late_other[:, wo_cols_here:], c), 1
    ).astype(F32)
    grad_query = sums[:, :q_cols]
    grad_key = sums[:, q_cols : q_cols + kv_cols]
    grad_value = sums[:, q_cols + kv_cols : qkv_cols]
    router_part = sums[:, qkv_cols : qkv_cols + experts]

    in_mine, in_other = from_halves(in_sum, rows, c)
    out_mine, out_other = from_halves(out_sum, rows, c)
    grad_in = jnp.concatenate(in_order(in_mine, in_other, c), 1).astype(F32)
    grad_out = jnp.concatenate(in_order(out_mine, out_other, c), 1).astype(F32)

    attn_gain_part = (
        jnp.sum(grad_query * w_query.astype(F32), 1)
        + jnp.sum(grad_key * key_weight.astype(F32), 1)
        + jnp.sum(grad_value * value_weight.astype(F32), 1)
    ) / attn_gain.astype(F32)
    moe_gain_part = (
        jnp.sum(in_mine.astype(F32) * in_kept.astype(F32), 1)
        + jnp.sum(in_other.astype(F32) * in_gave.astype(F32), 1)
        + jnp.sum(router_part * router.astype(F32), 1)
    ) / moe_gain.astype(F32)
    total = jnp.concatenate(
        [router_part, attn_gain_part[:, None], moe_gain_part[:, None], jnp.zeros((rows, 128 - experts - 2), F32)], 1
    )
    tiny = total.astype(BF16)
    grad_output = lax.dynamic_slice_in_dim(wo_own_rows, m * q_cols, q_cols, 1).astype(F32)
    for k in range(1, mp):
        send = lax.dynamic_slice_in_dim(wo_own_rows, ((m + k) % mp) * q_cols, q_cols, 1)
        got = lax.ppermute(
            jnp.concatenate([send, tiny], 1), "mp", [(i, (i + k) % mp) for i in range(mp)]
        ).astype(F32)
        grad_output = grad_output + got[:, :q_cols]
        total = total + got[:, q_cols:]

    return (
        restore(layer_out, q, quads)[None],
        restore(grad_tokens, q, quads)[None],
        total[:, experts],
        grad_query,
        grad_key,
        grad_value,
        grad_output,
        total[:, :experts],
        total[:, experts + 1],
        grad_in.reshape(w_in.shape),
        grad_out.reshape(w_out.shape),
    )


def solution(mesh):
    dp, mp = mesh.shape["dp"], mesh.shape["mp"]
    quads = dp // 2
    split = Mesh(mesh.devices.reshape(quads, 2, mp), ("q", "c", "mp"))
    d = ("q", "c")
    placed = (
        P(d, "mp", None),
        P(d),
        P(d, "mp"),
        P(d, "mp"),
        P(d, "mp"),
        P(d, "mp"),
        P(d, None),
        P(d),
        P(d, None, None, "mp"),
        P(d, None, "mp"),
        P(d, None),
        P(d, None, None),
        P(d, "mp", None),
    )
    return jax.shard_map(
        functools.partial(body, quads=quads),
        mesh=split,
        in_specs=placed,
        out_specs=(
            P(d, "mp", None),
            P(d, "mp", None),
            P(d),
            P(d, "mp"),
            P(d, "mp"),
            P(d, "mp"),
            P(d, "mp"),
            P(d, None),
            P(d),
            P(d, None, None, "mp"),
            P(d, None, "mp"),
        ),
        check_vma=False,
    )
```

```python
import functools

import jax
import jax.numpy as jnp
from jax import lax
from jax.experimental import pallas as pl
from jax.experimental.pallas import tpu as pltpu
from jax.sharding import Mesh
from jax.sharding import PartitionSpec as P

HEAD = 64
RESID = 0.22
ATTN_MULT = 0.015625
EPS = 1e-06
ROPE_BASE = 10000.0
NEG = -1e30
F32 = jnp.float32
BF16 = jnp.bfloat16
BLK = 256
VMEM_CAP = 60 * 1024 * 1024


def nt(left, right):
    return lax.dot_general(left, right, (((1,), (1,)), ((), ())), preferred_element_type=F32)


def tn(left, right):
    return lax.dot_general(left, right, (((0,), (0,)), ((), ())), preferred_element_type=F32)


def nn(left, right):
    return jnp.dot(left, right, preferred_element_type=F32)


def cost(flops, transcendentals, bytes_accessed, scale=1):
    return pl.CostEstimate(
        flops=flops // scale,
        transcendentals=transcendentals // scale,
        bytes_accessed=bytes_accessed // scale,
    )


def rope_cols(values, cosine, sine):
    lane = lax.broadcasted_iota(jnp.int32, cosine.shape, 1)
    low = (lane % HEAD) < (HEAD // 2)
    pieces = []
    for start in range(0, values.shape[1], 128):
        piece = values[:, start : start + 128]
        turned = jnp.where(low, pltpu.roll(piece, 96, 1), pltpu.roll(piece, 32, 1))
        pieces.append(piece * cosine + turned * sine)
    return pieces[0] if len(pieces) == 1 else jnp.concatenate(pieces, 1)


def seen(kc, i, kdoc_ref, qdoc, group):
    kdoc = kdoc_ref[pl.ds(pl.multiple_of(kc * BLK, BLK), BLK), :]
    kpos = kc * BLK + lax.broadcasted_iota(jnp.int32, (BLK, 1), 0)
    qpos = i * BLK + lax.broadcasted_iota(jnp.int32, (1, BLK), 1)
    visible = (kpos <= qpos) & (kdoc == qdoc)
    return jnp.where(visible, 0.0, NEG)


def attn_fwd_kernel(
    tok_ref, gain_ref, w_ref, cos_ref, sin_ref, kdoc_ref, qdoc_ref,
    na_ref, q_ref, k_ref, v_ref, att_ref, lse_ref, s_scr, *, q_heads, kv_heads,
):
    i = pl.program_id(0)
    group = q_heads // kv_heads
    tok = tok_ref[...].astype(F32)
    inv = lax.rsqrt(jnp.mean(tok * tok, -1, keepdims=True) + EPS)
    na = (tok * inv * gain_ref[...]).astype(BF16)
    na_ref[...] = na
    qkv = nn(na, w_ref[...])
    qk_cols = (q_heads + kv_heads) * HEAD
    roped = rope_cols(qkv[:, :qk_cols], cos_ref[...], sin_ref[...]).astype(BF16)
    vals = qkv[:, qk_cols:].astype(BF16)
    rows = pl.ds(pl.multiple_of(i * BLK, BLK), BLK)
    heads = [roped[:, h * HEAD : (h + 1) * HEAD] for h in range(q_heads + kv_heads)]
    for h in range(q_heads):
        q_ref[h] = heads[h]
    for g in range(kv_heads):
        k_ref[g, rows, :] = heads[q_heads + g]
        v_ref[g, rows, :] = vals[:, g * HEAD : (g + 1) * HEAD]
    lo = jnp.maximum(i - 2, 0)
    qdoc = qdoc_ref[...]
    groups = range(kv_heads)
    queries = [jnp.concatenate(heads[g * group : (g + 1) * group], 0) for g in groups]

    def scores(kc, tops):
        bias = seen(kc, i, kdoc_ref, qdoc, group)
        bias = jnp.concatenate([bias] * group, 1)
        rows = pl.ds(pl.multiple_of(kc * BLK, BLK), BLK)
        out = []
        for g in groups:
            s = nt(k_ref[g, rows, :], queries[g]) * ATTN_MULT + bias
            s_scr[g, kc - lo] = s
            out.append(jnp.maximum(tops[g], jnp.max(s, 0, keepdims=True)))
        return tuple(out)

    start = tuple(jnp.full((1, group * BLK), NEG, F32) for _ in groups)
    tops = lax.fori_loop(lo, i + 1, scores, start)

    def mix(kc, carry):
        rows = pl.ds(pl.multiple_of(kc * BLK, BLK), BLK)
        out = []
        for g in groups:
            total, mixed = carry[g]
            e = jnp.exp(s_scr[g, kc - lo] - tops[g])
            out.append(
                (
                    total + jnp.sum(e, 0, keepdims=True),
                    mixed + tn(v_ref[g, rows, :], e.astype(BF16)),
                )
            )
        return tuple(out)

    zero = (jnp.zeros((1, group * BLK), F32), jnp.zeros((HEAD, group * BLK), F32))
    sums = lax.fori_loop(lo, i + 1, mix, tuple(zero for _ in groups))
    for g in groups:
        total, out = sums[g]
        out = out / total
        lse_ref[0, g : g + 1, :] = tops[g] + jnp.log(total)
        for j in range(group):
            h = g * group + j
            att_ref[:, h * HEAD : (h + 1) * HEAD] = out[:, j * BLK : (j + 1) * BLK].T.astype(BF16)


def attn_fwd(tokens, gain, pack, cosine, sine, kdoc, qdoc, q_heads, kv_heads):
    length, width = tokens.shape
    blocks = length // BLK
    cols = (q_heads + 2 * kv_heads) * HEAD
    group = q_heads // kv_heads
    fixed = lambda i: (0, 0)
    fixed3 = lambda i: (0, 0, 0)
    row = lambda i: (i, 0)
    return pl.pallas_call(
        functools.partial(attn_fwd_kernel, q_heads=q_heads, kv_heads=kv_heads),
        grid=(blocks,),
        in_specs=[
            pl.BlockSpec((BLK, width), row),
            pl.BlockSpec((1, width), fixed),
            pl.BlockSpec((width, cols), fixed),
            pl.BlockSpec((BLK, 128), row),
            pl.BlockSpec((BLK, 128), row),
            pl.BlockSpec((length, 1), fixed),
            pl.BlockSpec((1, BLK), lambda i: (0, i)),
        ],
        out_specs=[
            pl.BlockSpec((BLK, width), row),
            pl.BlockSpec((q_heads, BLK, HEAD), lambda i: (0, i, 0)),
            pl.BlockSpec((kv_heads, length, HEAD), fixed3),
            pl.BlockSpec((kv_heads, length, HEAD), fixed3),
            pl.BlockSpec((BLK, q_heads * HEAD), row),
            pl.BlockSpec((1, kv_heads, group * BLK), lambda i: (i, 0, 0)),
        ],
        out_shape=[
            jax.ShapeDtypeStruct((length, width), BF16),
            jax.ShapeDtypeStruct((q_heads, length, HEAD), BF16),
            jax.ShapeDtypeStruct((kv_heads, length, HEAD), BF16),
            jax.ShapeDtypeStruct((kv_heads, length, HEAD), BF16),
            jax.ShapeDtypeStruct((length, q_heads * HEAD), BF16),
            jax.ShapeDtypeStruct((blocks, kv_heads, group * BLK), F32),
        ],
        scratch_shapes=[pltpu.VMEM((kv_heads, 3, BLK, group * BLK), F32)],
        compiler_params=pltpu.CompilerParams(
            dimension_semantics=("arbitrary",), vmem_limit_bytes=VMEM_CAP
        ),
        cost_estimate=cost(
            flops=2 * length * width * cols + 8 * length * 768 * q_heads * HEAD,
            transcendentals=length * 640 * q_heads,
            bytes_accessed=4 * length * width + 2 * width * cols,
            scale=100,
        ),
        name="attn_fwd",
    )(tokens, gain, pack, cosine, sine, kdoc, qdoc)


def attn_bwd_kernel(
    do_ref, q_ref, k_ref, v_ref, att_ref, lse_ref, cos_ref, sin_ref, kdoc_ref, qdoc_ref,
    dq_ref, dkv_ref, dk_scr, dv_scr, *, q_heads, kv_heads,
):
    i = pl.program_id(0)
    group = q_heads // kv_heads

    @pl.when(i == 0)
    def _():
        dk_scr[...] = jnp.zeros_like(dk_scr)
        dv_scr[...] = jnp.zeros_like(dv_scr)

    do = do_ref[...]
    lo = jnp.maximum(i - 2, 0)
    qdoc = qdoc_ref[...]
    att = att_ref[...]
    groups = range(kv_heads)
    queries, gives, dot_rows, lses = [], [], [], []
    for g in groups:
        span = range(g * group, (g + 1) * group)
        queries.append(jnp.concatenate([q_ref[h] for h in span], 0))
        gives.append(jnp.concatenate([do[:, h * HEAD : (h + 1) * HEAD] for h in span], 0))
        outs = jnp.concatenate([att[:, h * HEAD : (h + 1) * HEAD] for h in span], 0)
        dot_rows.append(
            jnp.sum((gives[g].astype(F32) * outs.astype(F32)).T, 0, keepdims=True)
        )
        lses.append(lse_ref[0, g : g + 1, :])

    def chunk(kc, dqs):
        rows = pl.ds(pl.multiple_of(kc * BLK, BLK), BLK)
        bias = seen(kc, i, kdoc_ref, qdoc, group)
        bias = jnp.concatenate([bias] * group, 1)
        out = []
        for g in groups:
            keys = k_ref[g, rows, :]
            prob = jnp.exp(nt(keys, queries[g]) * ATTN_MULT + bias - lses[g])
            dprob = nt(v_ref[g, rows, :], gives[g])
            ds = (prob * (dprob - dot_rows[g])).astype(BF16)
            dv_scr[g, rows, :] += nn(prob.astype(BF16), gives[g])
            dk_scr[g, rows, :] += nn(ds, queries[g])
            out.append(dqs[g] + tn(keys, ds))
        return tuple(out)

    zero = jnp.zeros((HEAD, group * BLK), F32)
    dqs = lax.fori_loop(lo, i + 1, chunk, tuple(zero for _ in groups))
    dq_heads = [dqs[g][:, j * BLK : (j + 1) * BLK].T for g in groups for j in range(group)]
    rows = pl.ds(pl.multiple_of(i * BLK, BLK), BLK)
    dq_all = jnp.concatenate(dq_heads, 1) * ATTN_MULT
    dq_ref[...] = rope_cols(dq_all, cos_ref[rows, :], -sin_ref[rows, :]).astype(BF16)

    @pl.when(i == pl.num_programs(0) - 1)
    def _():
        dk = jnp.concatenate([dk_scr[g] for g in range(kv_heads)], 1) * ATTN_MULT
        kcols = kv_heads * HEAD
        dkv_ref[:, :kcols] = rope_cols(dk, cos_ref[...], -sin_ref[...]).astype(BF16)
        dkv_ref[:, kcols:] = jnp.concatenate([dv_scr[g] for g in range(kv_heads)], 1).astype(BF16)


def attn_bwd(do, q, k, v, att, lse, cosine, sine, kdoc, qdoc):
    length = do.shape[0]
    q_heads, kv_heads = q.shape[0], k.shape[0]
    blocks = length // BLK
    group = q_heads // kv_heads
    fixed = lambda i: (0, 0)
    fixed3 = lambda i: (0, 0, 0)
    row = lambda i: (i, 0)
    return pl.pallas_call(
        functools.partial(attn_bwd_kernel, q_heads=q_heads, kv_heads=kv_heads),
        grid=(blocks,),
        in_specs=[
            pl.BlockSpec((BLK, q_heads * HEAD), row),
            pl.BlockSpec((q_heads, BLK, HEAD), lambda i: (0, i, 0)),
            pl.BlockSpec((kv_heads, length, HEAD), fixed3),
            pl.BlockSpec((kv_heads, length, HEAD), fixed3),
            pl.BlockSpec((BLK, q_heads * HEAD), row),
            pl.BlockSpec((1, kv_heads, group * BLK), lambda i: (i, 0, 0)),
            pl.BlockSpec((length, 128), fixed),
            pl.BlockSpec((length, 128), fixed),
            pl.BlockSpec((length, 1), fixed),
            pl.BlockSpec((1, BLK), lambda i: (0, i)),
        ],
        out_specs=[
            pl.BlockSpec((BLK, q_heads * HEAD), row),
            pl.BlockSpec((length, 2 * kv_heads * HEAD), fixed),
        ],
        out_shape=[
            jax.ShapeDtypeStruct((length, q_heads * HEAD), BF16),
            jax.ShapeDtypeStruct((length, 2 * kv_heads * HEAD), BF16),
        ],
        scratch_shapes=[
            pltpu.VMEM((kv_heads, length, HEAD), F32),
            pltpu.VMEM((kv_heads, length, HEAD), F32),
        ],
        compiler_params=pltpu.CompilerParams(
            dimension_semantics=("arbitrary",), vmem_limit_bytes=VMEM_CAP
        ),
        cost_estimate=cost(
            flops=20 * length * 768 * q_heads * HEAD,
            transcendentals=length * 640 * q_heads,
            bytes_accessed=8 * length * q_heads * HEAD,
        ),
        name="attn_bwd",
    )(do, q, k, v, att, lse, cosine, sine, kdoc, qdoc)


def mid_kernel(
    att_ref, wo_ref, tok_ref, gain_ref, small_ref, routes_ref, mid_ref, nm_ref, gate_ref, flat_ref
):
    att = jnp.concatenate([att_ref[k] for k in range(att_ref.shape[0])], 1)
    flat_ref[...] = att
    branch = nt(att, wo_ref[...])
    middle = tok_ref[...].astype(F32) + RESID * branch
    mid_ref[...] = middle
    inv = lax.rsqrt(jnp.mean(middle * middle, -1, keepdims=True) + EPS)
    nm = (middle * inv * gain_ref[...]).astype(BF16)
    nm_ref[...] = nm
    logits = nn(nm, small_ref[...])
    lane = lax.broadcasted_iota(jnp.int32, logits.shape, 1)
    chosen = lane == routes_ref[:, 0:1]
    for c in range(1, routes_ref.shape[1]):
        chosen = chosen | (lane == routes_ref[:, c : c + 1])
    logits = jnp.where(chosen, logits, NEG)
    e = jnp.exp(logits - jnp.max(logits, -1, keepdims=True))
    gate_ref[...] = e / jnp.sum(e, -1, keepdims=True)


def mid_fwd(att_all, wo_rows, tokens, gain, pack, small_at, routes):
    length, width = tokens.shape
    parts, _, cols = att_all.shape
    blocks = length // BLK
    fixed = lambda i: (0, 0)
    row = lambda i: (i, 0)
    return pl.pallas_call(
        mid_kernel,
        grid=(blocks,),
        in_specs=[
            pl.BlockSpec((parts, BLK, cols), lambda i: (0, i, 0)),
            pl.BlockSpec((width, parts * cols), fixed),
            pl.BlockSpec((BLK, width), row),
            pl.BlockSpec((1, width), fixed),
            pl.BlockSpec((width, 128), lambda i: (0, small_at)),
            pl.BlockSpec((BLK, routes.shape[1]), row),
        ],
        out_specs=[
            pl.BlockSpec((BLK, width), row),
            pl.BlockSpec((BLK, width), row),
            pl.BlockSpec((BLK, 128), row),
            pl.BlockSpec((BLK, parts * cols), row),
        ],
        out_shape=[
            jax.ShapeDtypeStruct((length, width), F32),
            jax.ShapeDtypeStruct((length, width), BF16),
            jax.ShapeDtypeStruct((length, 128), F32),
            jax.ShapeDtypeStruct((length, parts * cols), BF16),
        ],
        compiler_params=pltpu.CompilerParams(
            dimension_semantics=("arbitrary",), vmem_limit_bytes=VMEM_CAP
        ),
        cost_estimate=cost(
            flops=2 * length * width * cols * parts,
            transcendentals=length * 128,
            bytes_accessed=10 * length * width + 2 * width * cols * parts,
        ),
        name="mid_fwd",
    )(att_all, wo_rows, tokens, gain, pack, routes)


def norm_back(n_grad, values, gain):
    inv = lax.rsqrt(jnp.mean(values * values, -1, keepdims=True) + EPS)
    scaled = n_grad * gain
    return inv * (scaled - values * (inv * inv) * jnp.mean(scaled * values, -1, keepdims=True))


def back_mid_kernel(
    own_ref, back_ref, recv_ref, lg_ref, small_ref, mid_ref, gain_ref, cot_ref, wo_ref, ag_ref, p_ref
):
    n_grad = back_ref[...].astype(F32) + recv_ref[...].astype(F32) + nt(lg_ref[...], small_ref[...])
    grad = norm_back(n_grad, mid_ref[...], gain_ref[...])
    own = (pl.program_id(0) == own_ref[0]).astype(F32)
    ag = (RESID * (grad + own * cot_ref[...].astype(F32))).astype(BF16)
    ag_ref[...] = ag
    out = nn(ag, wo_ref[...]).astype(BF16)
    cols = p_ref.shape[2]
    for k in range(p_ref.shape[0]):
        p_ref[k] = out[:, k * cols : (k + 1) * cols]


def back_mid(own, back, recv, logit_grad, pack, small_at, middle, gain, cot, wo_rows, parts):
    length, width = middle.shape
    blocks = length // BLK
    cols = wo_rows.shape[1] // parts
    fixed = lambda i, o: (0, 0)
    row = lambda i, o: (i, 0)
    return pl.pallas_call(
        back_mid_kernel,
        grid_spec=pltpu.PrefetchScalarGridSpec(
            num_scalar_prefetch=1,
            grid=(blocks,),
            in_specs=[
                pl.BlockSpec((BLK, width), row),
                pl.BlockSpec((BLK, width), row),
                pl.BlockSpec((BLK, 128), row),
                pl.BlockSpec((width, 128), lambda i, o: (0, small_at)),
                pl.BlockSpec((BLK, width), row),
                pl.BlockSpec((1, width), fixed),
                pl.BlockSpec((BLK, width), fixed),
                pl.BlockSpec((width, parts * cols), fixed),
            ],
            out_specs=[
                pl.BlockSpec((BLK, width), row),
                pl.BlockSpec((parts, BLK, cols), lambda i, o: (0, i, 0)),
            ],
        ),
        out_shape=[
            jax.ShapeDtypeStruct((length, width), BF16),
            jax.ShapeDtypeStruct((parts, length, cols), BF16),
        ],
        compiler_params=pltpu.CompilerParams(
            dimension_semantics=("arbitrary",), vmem_limit_bytes=VMEM_CAP
        ),
        cost_estimate=cost(
            flops=2 * length * width * cols * parts,
            transcendentals=0,
            bytes_accessed=12 * length * width + 2 * width * cols * parts,
        ),
        name="back_mid",
    )(own, back, recv, logit_grad, pack, middle, gain, cot, wo_rows)


def back_end_kernel(dq_ref, dkv_ref, w_ref, tok_ref, gain_ref, ag_ref, out_ref):
    d_all = jnp.concatenate([dq_ref[...], dkv_ref[...]], 1)
    n_grad = nt(d_all, w_ref[...])
    grad = norm_back(n_grad, tok_ref[...].astype(F32), gain_ref[...])
    out_ref[...] = (grad + ag_ref[...].astype(F32) * (1.0 / RESID)).astype(BF16)


def back_end(dq, dkv, pack, tokens, gain, ag):
    length, width = tokens.shape
    cols = dq.shape[1] + dkv.shape[1]
    fixed = lambda i: (0, 0)
    row = lambda i: (i, 0)
    return pl.pallas_call(
        back_end_kernel,
        grid=(length // BLK,),
        in_specs=[
            pl.BlockSpec((BLK, dq.shape[1]), row),
            pl.BlockSpec((BLK, dkv.shape[1]), row),
            pl.BlockSpec((width, cols), fixed),
            pl.BlockSpec((BLK, width), row),
            pl.BlockSpec((1, width), fixed),
            pl.BlockSpec((BLK, width), row),
        ],
        out_specs=pl.BlockSpec((BLK, width), row),
        out_shape=jax.ShapeDtypeStruct((length, width), BF16),
        compiler_params=pltpu.CompilerParams(
            dimension_semantics=("arbitrary",), vmem_limit_bytes=VMEM_CAP
        ),
        cost_estimate=cost(
            flops=2 * length * width * cols,
            transcendentals=0,
            bytes_accessed=6 * length * width + 2 * width * cols,
        ),
        name="back_end",
    )(dq, dkv, pack, tokens, gain, ag)


def sigmoid(value):
    return 0.5 * jnp.tanh(0.5 * value) + 0.5


def gate_cols(gates, first):
    lane = lax.broadcasted_iota(jnp.int32, gates.shape, 1)
    return [
        jnp.sum(jnp.where(lane == first + k, gates, 0.0), -1, keepdims=True) for k in range(2)
    ]


def moe_fwd_kernel(base_ref, x_ref, w_ref, gate_ref, h_ref, gact_ref):
    p = pl.program_id(1)
    h = nn(x_ref[...], w_ref[...])
    h_ref[...] = h.astype(BF16)
    cols = gate_cols(gate_ref[...], base_ref[0] + 2 * p)
    for k in range(2):
        gate = h[:, 256 * k : 256 * k + 128]
        up = h[:, 256 * k + 128 : 256 * k + 256]
        act = gate * sigmoid(gate) * up
        gact_ref[:, 128 * k : 128 * k + 128] = (cols[k] * act).astype(BF16)


def moe_fwd(base, x, w_in, gates, rows, scale):
    length, width = x.shape
    cols = w_in.shape[1]
    return pl.pallas_call(
        moe_fwd_kernel,
        grid_spec=pltpu.PrefetchScalarGridSpec(
            num_scalar_prefetch=1,
            grid=(length // rows, cols // 512),
            in_specs=[
                pl.BlockSpec((rows, width), lambda i, p, b: (i, 0)),
                pl.BlockSpec((width, 512), lambda i, p, b: (0, p)),
                pl.BlockSpec((rows, 128), lambda i, p, b: (i, 0)),
            ],
            out_specs=[
                pl.BlockSpec((rows, 512), lambda i, p, b: (i, p)),
                pl.BlockSpec((rows, 256), lambda i, p, b: (i, p)),
            ],
        ),
        out_shape=[
            jax.ShapeDtypeStruct((length, cols), BF16),
            jax.ShapeDtypeStruct((length, cols // 2), BF16),
        ],
        compiler_params=pltpu.CompilerParams(
            dimension_semantics=("arbitrary", "arbitrary"), vmem_limit_bytes=VMEM_CAP
        ),
        cost_estimate=cost(
            flops=2 * length * width * cols,
            transcendentals=length * cols // 2,
            bytes_accessed=2 * length * (width + cols + cols // 2) + 4 * width * cols,
            scale=scale,
        ),
        name="moe_fwd",
    )(base, x, w_in, gates)


def combine_kernel(*refs):
    gact_ref, pieces, out_ref, w_scr = refs[0], refs[1:-2], refs[-2], refs[-1]

    @pl.when(pl.program_id(0) == 0)
    def _():
        at = 0
        for piece in pieces:
            w_scr[at : at + piece.shape[0], :] = piece[...]
            at += piece.shape[0]

    out_ref[...] = nt(gact_ref[...], w_scr[...]).astype(BF16)


def combine(gact, pieces, rows):
    length, cols = gact.shape
    width = sum(p.shape[0] for p in pieces)
    return pl.pallas_call(
        combine_kernel,
        grid=(length // rows,),
        in_specs=[pl.BlockSpec((rows, cols), lambda i: (i, 0))]
        + [pl.BlockSpec(p.shape, lambda i: (0, 0)) for p in pieces],
        out_specs=pl.BlockSpec((rows, width), lambda i: (i, 0)),
        out_shape=jax.ShapeDtypeStruct((length, width), BF16),
        scratch_shapes=[pltpu.VMEM((width, cols), BF16)],
        compiler_params=pltpu.CompilerParams(
            dimension_semantics=("arbitrary",), vmem_limit_bytes=VMEM_CAP
        ),
        cost_estimate=cost(
            flops=2 * length * width * cols,
            transcendentals=0,
            bytes_accessed=2 * (length * width + length * cols + width * cols),
        ),
        name="combine",
    )(gact, *pieces)


def moe_bwd_kernel(*refs):
    base_ref, g_ref, gate_ref, h_ref = refs[:4]
    pieces, gug_ref, choice_ref, plain_scr = refs[4:-3], refs[-3], refs[-2], refs[-1]
    p = pl.program_id(1)
    first = base_ref[0] + 2 * (p - 1)
    plain = plain_scr[1 - p % 2]
    cols = gate_cols(gate_ref[...], first)
    lane = lax.broadcasted_iota(jnp.int32, choice_ref.shape, 1)
    add = jnp.zeros(choice_ref.shape, F32)
    for k in range(2):
        gate = h_ref[:, 256 * k : 256 * k + 128].astype(F32)
        up = h_ref[:, 256 * k + 128 : 256 * k + 256].astype(F32)
        part = plain[:, 128 * k : 128 * k + 128]
        sig = sigmoid(gate)
        silu = gate * sig
        add = jnp.where(lane == first + k, jnp.sum(silu * up * part, -1, keepdims=True), add)
        act_grad = cols[k] * part
        gug_ref[:, 256 * k : 256 * k + 128] = (act_grad * up * (sig + silu * (1.0 - sig))).astype(
            BF16
        )
        gug_ref[:, 256 * k + 128 : 256 * k + 256] = (act_grad * silu).astype(BF16)
    choice_ref[...] = jnp.where(p > 1, choice_ref[...], 0.0) + jnp.where(p > 0, add, 0.0)
    weights = [piece[...] for piece in pieces]
    plain_scr[p % 2] = nn(g_ref[...], weights[0] if len(weights) == 1 else jnp.concatenate(weights, 0))


def moe_bwd(base, g, pieces, gates, h, rows):
    length, width = g.shape
    cols = h.shape[1]
    steps = cols // 512
    behind = lambda i, p, b: (i, jnp.maximum(p - 1, 0))
    return pl.pallas_call(
        moe_bwd_kernel,
        grid_spec=pltpu.PrefetchScalarGridSpec(
            num_scalar_prefetch=1,
            grid=(length // rows, steps + 1),
            in_specs=[
                pl.BlockSpec((rows, width), lambda i, p, b: (i, 0)),
                pl.BlockSpec((rows, 128), lambda i, p, b: (i, 0)),
                pl.BlockSpec((rows, 512), behind),
            ]
            + [
                pl.BlockSpec((w.shape[0], 256), lambda i, p, b: (0, jnp.minimum(p, steps - 1)))
                for w in pieces
            ],
            out_specs=[
                pl.BlockSpec((rows, 512), behind),
                pl.BlockSpec((rows, 128), lambda i, p, b: (i, 0)),
            ],
            scratch_shapes=[pltpu.VMEM((2, rows, 256), F32)],
        ),
        out_shape=[
            jax.ShapeDtypeStruct((length, cols), BF16),
            jax.ShapeDtypeStruct((length, 128), F32),
        ],
        compiler_params=pltpu.CompilerParams(
            dimension_semantics=("arbitrary", "arbitrary"), vmem_limit_bytes=VMEM_CAP
        ),
        cost_estimate=cost(
            flops=length * width * cols,
            transcendentals=length * cols // 2,
            bytes_accessed=2 * length * (width + 2 * cols) + 2 * width * cols,
        ),
        name="moe_bwd",
    )(base, g, gates, h, *pieces)


def segment_kernel(*refs, count):
    lefts, rights, outs = refs[:4], refs[4:6], refs[6:]
    first = tn(jnp.concatenate([lefts[0][...], lefts[1][...]], 1), rights[0][...])
    second = tn(jnp.concatenate([lefts[2][...], lefts[3][...]], 1), rights[1][...])
    value = (first + second).astype(BF16)
    for k in range(count):

        @pl.when(pl.program_id(0) == k)
        def _(k=k):
            outs[k][...] = value


def pick(s, values):
    out = values[0]
    for k in range(1, len(values)):
        out = jnp.where(s == k, values[k], out)
    return out


def weight_grad(left, left2, right, right2, segments):
    length, width = left.shape
    cols = right.shape[1] // 2
    quarter = width // 4
    wide = min(cols, 768)
    steps = cols // wide
    count = len(segments)
    firsts, seconds, halves = zip(*segments, strict=True)
    one = pl.BlockSpec((length, quarter), lambda s, j: (0, pick(s, firsts)))
    two = pl.BlockSpec((length, quarter), lambda s, j: (0, pick(s, seconds)))
    side = pl.BlockSpec((length, wide), lambda s, j: (0, pick(s, halves) * steps + j))

    def place(k):
        return pl.BlockSpec(
            (2 * quarter, wide),
            lambda s, j: (0, jnp.where(s == k, j, jnp.where(s < k, 0, steps - 1))),
        )

    return pl.pallas_call(
        functools.partial(segment_kernel, count=count),
        grid=(count, steps),
        in_specs=[one, two, one, two, side, side],
        out_specs=[place(k) for k in range(count)],
        out_shape=[jax.ShapeDtypeStruct((2 * quarter, cols), BF16)] * count,
        compiler_params=pltpu.CompilerParams(
            dimension_semantics=("arbitrary", "arbitrary"), vmem_limit_bytes=VMEM_CAP
        ),
        cost_estimate=cost(
            flops=2 * count * length * width * cols,
            transcendentals=0,
            bytes_accessed=4 * length * (width + 2 * cols),
            scale=100,
        ),
        name="weight_grad",
    )(left, left, left2, left2, right, right2)


def swap(value, axis, bit, size):
    return lax.ppermute(value, axis, [(i, i ^ bit) for i in range(size)])


def reorder(value, q, quads):
    if quads != 4:
        return value
    n = value.shape[-1] // 4
    b = [value[..., k * n : (k + 1) * n] for k in (0, 1, 3, 2)]
    odd = (q & 1) == 1
    far = (q & 2) == 2
    c = [jnp.where(odd, b[k], b[j]) for j, k in ((0, 1), (1, 0), (2, 3), (3, 2))]
    return jnp.concatenate([jnp.where(far, c[k], c[j]) for j, k in ((0, 3), (1, 2), (2, 1), (3, 0))], -1)


def restore(value, q, quads):
    if quads != 4:
        return value
    n = value.shape[-1] // 4
    b = [value[..., k * n : (k + 1) * n] for k in (0, 1, 3, 2)]
    odd = (q & 1) == 1
    far = (q & 2) == 2
    c = [jnp.where(odd, b[k ^ 1], b[k]) for k in range(4)]
    return jnp.concatenate([jnp.where(far, c[k ^ 2], c[k]) for k in range(4)], -1)


def gather_first(low, high, quads):
    if quads != 4:
        return (lax.all_gather(jnp.concatenate([low, high], 0), "q", axis=0, tiled=True),)
    return swap(low, "q", 1, 4), swap(high, "q", 2, 4)


def gather_rest(low, high, quads):
    if quads != 4:
        return ()
    return swap(high, "q", 1, 4), swap(low, "q", 2, 4)


def gather_diagonal(first, quads):
    if quads != 4:
        return ()
    return swap(first[0], "q", 2, 4), swap(first[1], "q", 1, 4)


def gather_join(low, high, first, rest, diagonal, quads):
    if quads != 4:
        return first[0]
    return jnp.concatenate(
        [low, high, first[0], rest[0], diagonal[0], diagonal[1], rest[1], first[1]], 0
    )


def gather_pieces(low, high, first, rest, diagonal, quads):
    if quads != 4:
        return first
    return (low, high, first[0], rest[0], diagonal[0], diagonal[1], rest[1], first[1])


def gather_rows(low, high, quads):
    first = gather_first(low, high, quads)
    rest = gather_rest(low, high, quads)
    return gather_join(low, high, first, rest, gather_diagonal(first, quads), quads)


SEND_LEFT, SEND_RIGHT, KEEP_LEFT, KEEP_RIGHT = (2, 3, 0), (2, 1, 1), (0, 1, 0), (0, 3, 1)


def cut(value, segment):
    n, half = value.shape[0] // 4, (value.shape[1] // 2 + 127) // 128 * 128
    side = value[:, half:] if segment[2] else value[:, :half]
    return jnp.concatenate([side[k * n : (k + 1) * n] for k in segment[:2]], 0)


def scatter_first(left, right):
    return swap(left, "q", 2, 4), swap(right, "q", 1, 4)


def scatter_second(keep_left, keep_right, from_y, from_x):
    n = keep_left.shape[0] // 2
    give_x = (keep_left[n:].astype(F32) + from_y[:n].astype(F32)).astype(BF16)
    give_y = (keep_right[n:].astype(F32) + from_x[:n].astype(F32)).astype(BF16)
    give_x, give_y = lax.optimization_barrier((give_x, give_y))
    arrived = swap(give_x, "q", 1, 4), swap(give_y, "q", 2, 4)
    return arrived, (give_x, give_y)


def scatter_last(keep_left, keep_right, from_y, from_x, arrived, *others):
    n = keep_left.shape[0] // 2
    keep_left, keep_right, from_y, from_x, left, right = all_after(
        (keep_left, keep_right, from_y, from_x, *arrived), *others
    )
    return (
        (keep_left[:n].astype(F32) + from_y[n:].astype(F32) + left.astype(F32)).astype(BF16),
        (keep_right[:n].astype(F32) + from_x[n:].astype(F32) + right.astype(F32)).astype(BF16),
    )


def small_first(value):
    n = value.shape[0] // 4
    return swap(value[n : 3 * n], "q", 1, 4)


def small_second(value, got):
    n = value.shape[0] // 4
    give = (value[3 * n :].astype(F32) + got[n:].astype(F32)).astype(BF16)
    return swap(lax.optimization_barrier(give), "q", 2, 4)


def small_last(value, got, late):
    n = value.shape[0] // 4
    value, got, late = lax.optimization_barrier((value, got, late))
    return (value[:n].astype(F32) + got[:n].astype(F32) + late.astype(F32)).astype(BF16)


def scatter_plain(value):
    total = lax.psum_scatter(value, "q", scatter_dimension=0, tiled=True)
    half = total.shape[1] // 2
    return total[:, :half], total[:, half:]


def after(value, *others):
    return lax.optimization_barrier((value, *others))[0]


def all_after(values, *others):
    return lax.optimization_barrier((*values, *others))[: len(values)]


def to_halves(mine, give, c):
    other = swap(give, "c", 1, 2)
    first = c == 0
    return jnp.where(first, mine, other), jnp.where(first, other, mine)


def part_halves(totals, rows, c):
    def take(at):
        return jnp.concatenate([lax.dynamic_slice_in_dim(t, at * rows, rows, 0) for t in totals], 1)

    return take(c), take(1 - c)


def from_halves(totals, rows, c):
    mine, give = part_halves(totals, rows, c)
    return mine, swap(give, "c", 1, 2)


def in_order(mine, other, c):
    return jnp.where(c == 0, mine, other), jnp.where(c == 0, other, mine)


def column_halves(value, c):
    n = value.shape[1] // 2
    mine = jnp.where(c == 0, value[:, :n], value[:, n:])
    give = jnp.where(c == 0, value[:, n:], value[:, :n])
    return mine, give


def whole_columns(half, c):
    other = swap(half, "c", 1, 2)
    return jnp.where(c == 0, half, other), jnp.where(c == 0, other, half)


def body(
    tokens, attn_gain, w_query, key_weight, value_weight, w_output, router, moe_gain, w_in, w_out,
    segments, routes, cotangent, *, quads,
):
    q = lax.axis_index("q")
    c = lax.axis_index("c")
    m = lax.axis_index("mp")
    length = segments.shape[1]
    width = tokens.shape[2]
    rows = w_query.shape[0]
    experts = router.shape[1]
    half_e = experts // 2
    ff = w_out.shape[2]
    q_heads = w_query.shape[1] // HEAD
    kv_heads = key_weight.shape[1] // HEAD
    q_cols, kv_cols = q_heads * HEAD, kv_heads * HEAD
    qkv_cols = q_cols + 2 * kv_cols
    mp = lax.axis_size("mp")

    tok_own = reorder(tokens[0], q, quads)
    tok_all = lax.all_gather(tok_own, "mp", axis=0, tiled=True)

    def half_rows(value):
        mine = lax.dynamic_slice_in_dim(value, c * half_e, half_e, 1).reshape(rows, -1)
        give = lax.dynamic_slice_in_dim(value, (1 - c) * half_e, half_e, 1).reshape(rows, -1)
        return to_halves(mine, give, c), mine, give

    in_pair, in_kept, in_gave = half_rows(w_in)

    pad = jnp.zeros((rows, 128 - experts - 2), BF16)
    pack = jnp.concatenate(
        [w_query, key_weight, value_weight, router, attn_gain[:, None], moe_gain[:, None], pad], 1
    )
    pack_pair = to_halves(*column_halves(after(pack, in_gave, in_kept), c), c)
    pack_pair = all_after(pack_pair, *in_pair)
    pack_first = gather_first(*pack_pair, quads)
    pack_rest = gather_rest(*pack_pair, quads)
    pack_half = gather_join(
        *pack_pair, pack_first, pack_rest, gather_diagonal(pack_first, quads), quads
    )
    pack = jnp.concatenate(whole_columns(pack_half, c), 1)
    small_at = qkv_cols // 128
    gains = pack[:, qkv_cols + experts : qkv_cols + experts + 2].astype(F32)
    attn_g = gains[:, 0].reshape(1, width)
    moe_g = gains[:, 1].reshape(1, width)

    doc_row = segments
    doc_col = segments.reshape(length, 1)
    lane = jnp.arange(128, dtype=jnp.int32) % (HEAD // 2)
    freq = ROPE_BASE ** (-lane.astype(F32) * 2.0 / HEAD)
    angles = jnp.arange(length).astype(F32)[:, None] * freq[None, :]
    cosine = jnp.cos(angles)
    upper = (jnp.arange(128, dtype=jnp.int32) % HEAD) < (HEAD // 2)
    sine = jnp.where(upper[None, :], -jnp.sin(angles), jnp.sin(angles))

    out_pair, _, _ = half_rows(after(w_out, *pack_pair))
    in_src = in_pair
    in_got = gather_first(*in_src, quads)
    in_rest = gather_rest(*in_src, quads)

    normed_a, q_r, k_r, v_r, attended, lse = attn_fwd(
        tok_all, attn_g, pack, cosine, sine, doc_col, doc_row, q_heads, kv_heads
    )

    wo_pad = jnp.concatenate([w_output, jnp.zeros((rows, 5 * 64), BF16)], 1)
    wo_cols = lax.all_gather(after(wo_pad, pack), "mp", axis=0, tiled=False)
    wo_cols = jnp.concatenate([wo_cols[j, :, :q_cols] for j in range(mp)], 1)
    wo_pair = to_halves(*column_halves(after(wo_cols, attended), c), c)
    in_diag = gather_diagonal(in_got, quads)
    wo_src = all_after(wo_pair, *in_diag)
    wo_got, wo_rest = gather_first(*wo_src, quads), gather_rest(*wo_src, quads)
    out_src = all_after(out_pair, *wo_got, *wo_rest)
    out_got, out_rest = gather_first(*out_src, quads), gather_rest(*out_src, quads)
    wo_half = gather_join(*wo_src, wo_got, wo_rest, gather_diagonal(wo_got, quads), quads)
    step = width // 4
    wo_other = jnp.concatenate(
        [swap(wo_half[k * step : (k + 1) * step], "c", 1, 2) for k in range(4)], 0
    )
    wo_rows = jnp.concatenate(in_order(*lax.optimization_barrier((wo_half, wo_other)), c), 1)
    join = (*in_src, *in_got, *in_rest, *in_diag)
    join = all_after(join, *wo_got)
    in_full = gather_join(
        *join[:2], join[2 : 2 + len(in_got)], join[2 + len(in_got) : 2 + len(in_got) + len(in_rest)],
        join[2 + len(in_got) + len(in_rest) :], quads,
    )

    att_all = lax.all_gather(after(attended, *in_got, *in_rest, *out_pair), "mp", axis=0, tiled=False)
    middle, normed_m, gates, att_flat = mid_fwd(
        after(att_all, in_full, *out_got), wo_rows, tok_all, moe_g, pack, small_at, routes[0]
    )

    cot_own = lax.optimization_barrier(reorder(cotangent[0], q, quads))
    moe_grad = (RESID * cot_own.astype(F32)).astype(BF16)
    grad_all = lax.all_gather(after(moe_grad, attended), "mp", axis=0, tiled=True)

    x_own = normed_m
    x_other = swap(normed_m, "c", 1, 2)
    gates_other = swap(gates, "c", 1, 2)
    base = (c * half_e).astype(jnp.int32).reshape(1)
    hid_own, gact_own = moe_fwd(
        base, x_own, in_full, gates, length, 100
    )
    x_other = after(x_other, gact_own, *out_rest)
    out_diag = gather_diagonal(all_after(out_got, gact_own), quads)
    out_full = gather_pieces(*out_src, out_got, out_rest, out_diag, quads)
    hid_other, gact_other = moe_fwd(base, x_other, in_full, gates_other, length, 1)
    comb_give = combine(gact_other, out_full, length // 2)
    comb_recv = swap(comb_give, "c", 1, 2)
    comb_own = combine(after(gact_own, comb_give, grad_all), out_full, length // 2)
    combined = (comb_own.astype(F32) + comb_recv.astype(F32)).astype(BF16)
    moe_low = lax.psum_scatter(combined, "mp", scatter_dimension=0, tiled=True)

    g_other = swap(after(grad_all, comb_give), "c", 1, 2)
    gacts = all_after((gact_own, gact_other), comb_own)
    if quads == 4:
        out_send = weight_grad(
            grad_all, g_other, *gacts, (SEND_LEFT, SEND_RIGHT, KEEP_LEFT, KEEP_RIGHT)
        )
        out_keep = out_send[2:]
        out_move = scatter_first(*out_send[:2])
    else:
        g2, gact2 = jnp.concatenate([grad_all, g_other], 0), jnp.concatenate(gacts, 0)
        out_move = out_keep = (tn(g2, gact2).astype(BF16),)
    gug_own, choice_own = moe_bwd(
        base, grad_all, out_full, gates, after(hid_own, *out_keep), length
    )
    gug_other, choice_other = moe_bwd(base, g_other, out_full, gates_other, after(hid_other, gug_own), length)
    choice = choice_own + swap(choice_other, "c", 1, 2)
    back_give = nt(after(gug_other, *out_move), in_full).astype(BF16)
    back_recv = swap(back_give, "c", 1, 2)
    gug_late = after(gug_own, back_give)
    back_own = nt(gug_late, in_full).astype(BF16)
    gates_c = gates * choice
    logit_grad = (gates_c - gates * jnp.sum(gates_c, -1, keepdims=True)).astype(BF16)
    out_late = scatter_second(*out_keep, *out_move)[0] if quads == 4 else ()
    ag, p_part = back_mid(
        m.astype(jnp.int32).reshape(1), back_own, back_recv, logit_grad, pack, small_at,
        after(middle, moe_low, *out_late), moe_g, cot_own, wo_rows, mp,
    )
    attended_grad = lax.psum_scatter(p_part, "mp", scatter_dimension=0, tiled=False)

    gugs = all_after((gug_own, gug_other), ag)
    if quads == 4:
        in_send = weight_grad(x_own, x_other, *gugs, (SEND_LEFT, SEND_RIGHT))
        in_move = scatter_first(*in_send)
        in_keep = weight_grad(
            x_own, x_other, *all_after(gugs, *in_send), (KEEP_LEFT, KEEP_RIGHT)
        )
    else:
        in_move = in_keep = (tn(jnp.concatenate([x_own, x_other], 0), jnp.concatenate(gugs, 0)).astype(BF16),)
    att_late = after(att_flat, *in_send) if quads == 4 else att_flat
    half_cols = att_flat.shape[1] // 2
    low_att, high_att = att_late[:, :half_cols], att_late[:, half_cols:]
    wo_give = tn(ag, jnp.where(c == 0, high_att, low_att)).astype(BF16)
    wo_mine = tn(ag, after(jnp.where(c == 0, low_att, high_att), wo_give)).astype(BF16)
    wo_part = (wo_mine.astype(F32) + swap(wo_give, "c", 1, 2).astype(F32)).astype(BF16)
    if quads == 4:
        wo_keep = (cut(wo_part, KEEP_LEFT), cut(wo_part, KEEP_RIGHT))
        wo_move = scatter_first(cut(wo_part, SEND_LEFT), cut(wo_part, SEND_RIGHT))
    dq, dkv = attn_bwd(
        attended_grad, q_r, k_r, v_r, attended, lse, cosine, sine, doc_col, doc_row
    )
    end_part = back_end(dq, dkv, pack, tok_all, attn_g, ag)
    grad_tokens = lax.psum_scatter(end_part, "mp", scatter_dimension=0, tiled=True).astype(F32)

    layer_out = (
        lax.dynamic_slice_in_dim(middle, m * (length // mp), length // mp, 0) + RESID * after(moe_low, end_part).astype(F32)
    ).astype(BF16)

    given = (end_part,)
    if quads == 4:
        in_move = all_after(in_move, end_part)
        in_late, given = scatter_second(*in_keep, *in_move)
        wo_move = all_after(wo_move, *given)
        wo_late, _ = scatter_second(*wo_keep, *wo_move)
    dq_late, dkv_late = after(dq, *given), after(dkv, *given)
    part = jnp.concatenate(
        [tn(normed_a, dq_late), tn(normed_a, dkv_late), tn(normed_m, after(logit_grad, *given))], 1
    ).astype(BF16)
    mine, give = column_halves(part, c)
    pair = (mine.astype(F32) + swap(give, "c", 1, 2).astype(F32)).astype(BF16)
    if quads == 4:
        pair_move = small_first(pair)
        in_sum = scatter_last(*in_keep, *in_move, in_late)
        in_mine, in_give = part_halves(in_sum, rows, c)
        pair_move, in_give = lax.optimization_barrier((pair_move, in_give))
        in_other = swap(in_give, "c", 1, 2)
        pair_late = small_second(pair, pair_move)
        wo_sum = scatter_last(*wo_keep, *wo_move, wo_late, pair_move)
        pair_sum = (small_last(pair, pair_move, pair_late),)
        out_sum = scatter_last(*out_keep, *out_move, out_late, end_part)
    else:
        in_sum, wo_sum, pair_sum, out_sum = (
            scatter_plain(v) for v in (in_keep[0], wo_part, pair, out_keep[0])
        )
        in_mine, in_other = from_halves(in_sum, rows, c)
    late_sum = (*wo_sum, *pair_sum)
    late_mine, late_other = from_halves(late_sum, rows, c)
    wo_cols_here = wo_part.shape[1]
    wo_own_rows = jnp.concatenate(
        in_order(late_mine[:, :wo_cols_here], late_other[:, :wo_cols_here], c), 1
    )
    sums = jnp.concatenate(
        in_order(late_mine[:, wo_cols_here:], late_other[:, wo_cols_here:], c), 1
    ).astype(F32)
    grad_query = sums[:, :q_cols]
    grad_key = sums[:, q_cols : q_cols + kv_cols]
    grad_value = sums[:, q_cols + kv_cols : qkv_cols]
    router_part = sums[:, qkv_cols : qkv_cols + experts]

    out_mine, out_other = from_halves(out_sum, rows, c)
    grad_in = jnp.concatenate(in_order(in_mine, in_other, c), 1).astype(F32)
    grad_out = jnp.concatenate(in_order(out_mine, out_other, c), 1).astype(F32)

    attn_gain_part = (
        jnp.sum(grad_query * w_query.astype(F32), 1)
        + jnp.sum(grad_key * key_weight.astype(F32), 1)
        + jnp.sum(grad_value * value_weight.astype(F32), 1)
    ) / attn_gain.astype(F32)
    moe_gain_part = (
        jnp.sum(in_mine.astype(F32) * in_kept.astype(F32), 1)
        + jnp.sum(in_other.astype(F32) * in_gave.astype(F32), 1)
        + jnp.sum(router_part * router.astype(F32), 1)
    ) / moe_gain.astype(F32)
    total = jnp.concatenate(
        [router_part, attn_gain_part[:, None], moe_gain_part[:, None], jnp.zeros((rows, 128 - experts - 2), F32)], 1
    )
    tiny = total.astype(BF16)
    grad_output = lax.dynamic_slice_in_dim(wo_own_rows, m * q_cols, q_cols, 1).astype(F32)
    for k in range(1, mp):
        send = lax.dynamic_slice_in_dim(wo_own_rows, ((m + k) % mp) * q_cols, q_cols, 1)
        got = lax.ppermute(
            jnp.concatenate([send, tiny], 1), "mp", [(i, (i + k) % mp) for i in range(mp)]
        ).astype(F32)
        grad_output = grad_output + got[:, :q_cols]
        total = total + got[:, q_cols:]

    return (
        restore(layer_out, q, quads)[None],
        restore(grad_tokens, q, quads)[None],
        total[:, experts],
        grad_query,
        grad_key,
        grad_value,
        grad_output,
        total[:, :experts],
        total[:, experts + 1],
        grad_in.reshape(w_in.shape),
        grad_out.reshape(w_out.shape),
    )


def solution(mesh):
    dp, mp = mesh.shape["dp"], mesh.shape["mp"]
    quads = dp // 2
    split = Mesh(mesh.devices.reshape(quads, 2, mp), ("q", "c", "mp"))
    d = ("q", "c")
    placed = (
        P(d, "mp", None),
        P(d),
        P(d, "mp"),
        P(d, "mp"),
        P(d, "mp"),
        P(d, "mp"),
        P(d, None),
        P(d),
        P(d, None, None, "mp"),
        P(d, None, "mp"),
        P(d, None),
        P(d, None, None),
        P(d, "mp", None),
    )
    return jax.shard_map(
        functools.partial(body, quads=quads),
        mesh=split,
        in_specs=placed,
        out_specs=(
            P(d, "mp", None),
            P(d, "mp", None),
            P(d),
            P(d, "mp"),
            P(d, "mp"),
            P(d, "mp"),
            P(d, "mp"),
            P(d, None),
            P(d),
            P(d, None, None, "mp"),
            P(d, None, "mp"),
        ),
        check_vma=False,
    )
```

```python
import functools

import jax
import jax.numpy as jnp
from jax import lax
from jax.experimental import pallas as pl
from jax.experimental.pallas import tpu as pltpu
from jax.sharding import Mesh
from jax.sharding import PartitionSpec as P

HEAD = 64
RESID = 0.22
ATTN_MULT = 0.015625
EPS = 1e-06
ROPE_BASE = 10000.0
NEG = -1e30
F32 = jnp.float32
BF16 = jnp.bfloat16
BLK = 256
VMEM_CAP = 60 * 1024 * 1024


def nt(left, right):
    return lax.dot_general(left, right, (((1,), (1,)), ((), ())), preferred_element_type=F32)


def tn(left, right):
    return lax.dot_general(left, right, (((0,), (0,)), ((), ())), preferred_element_type=F32)


def nn(left, right):
    return jnp.dot(left, right, preferred_element_type=F32)


def cost(flops, transcendentals, bytes_accessed, scale=1):
    return pl.CostEstimate(
        flops=flops // scale,
        transcendentals=transcendentals // scale,
        bytes_accessed=bytes_accessed // scale,
    )


def rope_cols(values, cosine, sine):
    lane = lax.broadcasted_iota(jnp.int32, cosine.shape, 1)
    low = (lane % HEAD) < (HEAD // 2)
    pieces = []
    for start in range(0, values.shape[1], 128):
        piece = values[:, start : start + 128]
        turned = jnp.where(low, pltpu.roll(piece, 96, 1), pltpu.roll(piece, 32, 1))
        pieces.append(piece * cosine + turned * sine)
    return pieces[0] if len(pieces) == 1 else jnp.concatenate(pieces, 1)


def seen(kc, i, kdoc_ref, qdoc, group):
    kdoc = kdoc_ref[pl.ds(pl.multiple_of(kc * BLK, BLK), BLK), :]
    kpos = kc * BLK + lax.broadcasted_iota(jnp.int32, (BLK, 1), 0)
    qpos = i * BLK + lax.broadcasted_iota(jnp.int32, (1, BLK), 1)
    visible = (kpos <= qpos) & (kdoc == qdoc)
    return jnp.where(visible, 0.0, NEG)


def attn_fwd_kernel(
    tok_ref, gain_ref, w_ref, cos_ref, sin_ref, kdoc_ref, qdoc_ref,
    na_ref, q_ref, k_ref, v_ref, att_ref, lse_ref, s_scr, *, q_heads, kv_heads,
):
    i = pl.program_id(0)
    group = q_heads // kv_heads
    tok = tok_ref[...].astype(F32)
    inv = lax.rsqrt(jnp.mean(tok * tok, -1, keepdims=True) + EPS)
    na = (tok * inv * gain_ref[...]).astype(BF16)
    na_ref[...] = na
    qkv = nn(na, w_ref[...])
    qk_cols = (q_heads + kv_heads) * HEAD
    roped = rope_cols(qkv[:, :qk_cols], cos_ref[...], sin_ref[...]).astype(BF16)
    vals = qkv[:, qk_cols:].astype(BF16)
    rows = pl.ds(pl.multiple_of(i * BLK, BLK), BLK)
    heads = [roped[:, h * HEAD : (h + 1) * HEAD] for h in range(q_heads + kv_heads)]
    for h in range(q_heads):
        q_ref[h] = heads[h]
    for g in range(kv_heads):
        k_ref[g, rows, :] = heads[q_heads + g]
        v_ref[g, rows, :] = vals[:, g * HEAD : (g + 1) * HEAD]
    lo = jnp.maximum(i - 2, 0)
    qdoc = qdoc_ref[...]
    groups = range(kv_heads)
    queries = [jnp.concatenate(heads[g * group : (g + 1) * group], 0) for g in groups]

    def scores(kc, tops):
        bias = seen(kc, i, kdoc_ref, qdoc, group)
        bias = jnp.concatenate([bias] * group, 1)
        rows = pl.ds(pl.multiple_of(kc * BLK, BLK), BLK)
        out = []
        for g in groups:
            s = nt(k_ref[g, rows, :], queries[g]) * ATTN_MULT + bias
            s_scr[g, kc - lo] = s
            out.append(jnp.maximum(tops[g], jnp.max(s, 0, keepdims=True)))
        return tuple(out)

    start = tuple(jnp.full((1, group * BLK), NEG, F32) for _ in groups)
    tops = lax.fori_loop(lo, i + 1, scores, start)

    def mix(kc, carry):
        rows = pl.ds(pl.multiple_of(kc * BLK, BLK), BLK)
        out = []
        for g in groups:
            total, mixed = carry[g]
            e = jnp.exp(s_scr[g, kc - lo] - tops[g])
            out.append(
                (
                    total + jnp.sum(e, 0, keepdims=True),
                    mixed + tn(v_ref[g, rows, :], e.astype(BF16)),
                )
            )
        return tuple(out)

    zero = (jnp.zeros((1, group * BLK), F32), jnp.zeros((HEAD, group * BLK), F32))
    sums = lax.fori_loop(lo, i + 1, mix, tuple(zero for _ in groups))
    for g in groups:
        total, out = sums[g]
        out = out / total
        lse_ref[0, g : g + 1, :] = tops[g] + jnp.log(total)
        for j in range(group):
            h = g * group + j
            att_ref[:, h * HEAD : (h + 1) * HEAD] = out[:, j * BLK : (j + 1) * BLK].T.astype(BF16)


def attn_fwd(tokens, gain, pack, cosine, sine, kdoc, qdoc, q_heads, kv_heads):
    length, width = tokens.shape
    blocks = length // BLK
    cols = (q_heads + 2 * kv_heads) * HEAD
    group = q_heads // kv_heads
    fixed = lambda i: (0, 0)
    fixed3 = lambda i: (0, 0, 0)
    row = lambda i: (i, 0)
    return pl.pallas_call(
        functools.partial(attn_fwd_kernel, q_heads=q_heads, kv_heads=kv_heads),
        grid=(blocks,),
        in_specs=[
            pl.BlockSpec((BLK, width), row),
            pl.BlockSpec((1, width), fixed),
            pl.BlockSpec((width, cols), fixed),
            pl.BlockSpec((BLK, 128), row),
            pl.BlockSpec((BLK, 128), row),
            pl.BlockSpec((length, 1), fixed),
            pl.BlockSpec((1, BLK), lambda i: (0, i)),
        ],
        out_specs=[
            pl.BlockSpec((BLK, width), row),
            pl.BlockSpec((q_heads, BLK, HEAD), lambda i: (0, i, 0)),
            pl.BlockSpec((kv_heads, length, HEAD), fixed3),
            pl.BlockSpec((kv_heads, length, HEAD), fixed3),
            pl.BlockSpec((BLK, q_heads * HEAD), row),
            pl.BlockSpec((1, kv_heads, group * BLK), lambda i: (i, 0, 0)),
        ],
        out_shape=[
            jax.ShapeDtypeStruct((length, width), BF16),
            jax.ShapeDtypeStruct((q_heads, length, HEAD), BF16),
            jax.ShapeDtypeStruct((kv_heads, length, HEAD), BF16),
            jax.ShapeDtypeStruct((kv_heads, length, HEAD), BF16),
            jax.ShapeDtypeStruct((length, q_heads * HEAD), BF16),
            jax.ShapeDtypeStruct((blocks, kv_heads, group * BLK), F32),
        ],
        scratch_shapes=[pltpu.VMEM((kv_heads, 3, BLK, group * BLK), F32)],
        compiler_params=pltpu.CompilerParams(
            dimension_semantics=("arbitrary",), vmem_limit_bytes=VMEM_CAP
        ),
        cost_estimate=cost(
            flops=2 * length * width * cols + 8 * length * 768 * q_heads * HEAD,
            transcendentals=length * 640 * q_heads,
            bytes_accessed=4 * length * width + 2 * width * cols,
            scale=100,
        ),
        name="attn_fwd",
    )(tokens, gain, pack, cosine, sine, kdoc, qdoc)


def attn_bwd_kernel(
    do_ref, q_ref, k_ref, v_ref, att_ref, lse_ref, cos_ref, sin_ref, kdoc_ref, qdoc_ref,
    dq_ref, dkv_ref, dk_scr, dv_scr, *, q_heads, kv_heads,
):
    i = pl.program_id(0)
    group = q_heads // kv_heads

    @pl.when(i == 0)
    def _():
        dk_scr[...] = jnp.zeros_like(dk_scr)
        dv_scr[...] = jnp.zeros_like(dv_scr)

    do = do_ref[...]
    lo = jnp.maximum(i - 2, 0)
    qdoc = qdoc_ref[...]
    att = att_ref[...]
    groups = range(kv_heads)
    queries, gives, dot_rows, lses = [], [], [], []
    for g in groups:
        span = range(g * group, (g + 1) * group)
        queries.append(jnp.concatenate([q_ref[h] for h in span], 0))
        gives.append(jnp.concatenate([do[:, h * HEAD : (h + 1) * HEAD] for h in span], 0))
        outs = jnp.concatenate([att[:, h * HEAD : (h + 1) * HEAD] for h in span], 0)
        dot_rows.append(
            jnp.sum((gives[g].astype(F32) * outs.astype(F32)).T, 0, keepdims=True)
        )
        lses.append(lse_ref[0, g : g + 1, :])

    def chunk(kc, dqs):
        rows = pl.ds(pl.multiple_of(kc * BLK, BLK), BLK)
        bias = seen(kc, i, kdoc_ref, qdoc, group)
        bias = jnp.concatenate([bias] * group, 1)
        out = []
        for g in groups:
            keys = k_ref[g, rows, :]
            prob = jnp.exp(nt(keys, queries[g]) * ATTN_MULT + bias - lses[g])
            dprob = nt(v_ref[g, rows, :], gives[g])
            ds = (prob * (dprob - dot_rows[g])).astype(BF16)
            dv_scr[g, rows, :] += nn(prob.astype(BF16), gives[g])
            dk_scr[g, rows, :] += nn(ds, queries[g])
            out.append(dqs[g] + tn(keys, ds))
        return tuple(out)

    zero = jnp.zeros((HEAD, group * BLK), F32)
    dqs = lax.fori_loop(lo, i + 1, chunk, tuple(zero for _ in groups))
    dq_heads = [dqs[g][:, j * BLK : (j + 1) * BLK].T for g in groups for j in range(group)]
    rows = pl.ds(pl.multiple_of(i * BLK, BLK), BLK)
    dq_all = jnp.concatenate(dq_heads, 1) * ATTN_MULT
    dq_ref[...] = rope_cols(dq_all, cos_ref[rows, :], -sin_ref[rows, :]).astype(BF16)

    @pl.when(i == pl.num_programs(0) - 1)
    def _():
        dk = jnp.concatenate([dk_scr[g] for g in range(kv_heads)], 1) * ATTN_MULT
        kcols = kv_heads * HEAD
        dkv_ref[:, :kcols] = rope_cols(dk, cos_ref[...], -sin_ref[...]).astype(BF16)
        dkv_ref[:, kcols:] = jnp.concatenate([dv_scr[g] for g in range(kv_heads)], 1).astype(BF16)


def attn_bwd(do, q, k, v, att, lse, cosine, sine, kdoc, qdoc):
    length = do.shape[0]
    q_heads, kv_heads = q.shape[0], k.shape[0]
    blocks = length // BLK
    group = q_heads // kv_heads
    fixed = lambda i: (0, 0)
    fixed3 = lambda i: (0, 0, 0)
    row = lambda i: (i, 0)
    return pl.pallas_call(
        functools.partial(attn_bwd_kernel, q_heads=q_heads, kv_heads=kv_heads),
        grid=(blocks,),
        in_specs=[
            pl.BlockSpec((BLK, q_heads * HEAD), row),
            pl.BlockSpec((q_heads, BLK, HEAD), lambda i: (0, i, 0)),
            pl.BlockSpec((kv_heads, length, HEAD), fixed3),
            pl.BlockSpec((kv_heads, length, HEAD), fixed3),
            pl.BlockSpec((BLK, q_heads * HEAD), row),
            pl.BlockSpec((1, kv_heads, group * BLK), lambda i: (i, 0, 0)),
            pl.BlockSpec((length, 128), fixed),
            pl.BlockSpec((length, 128), fixed),
            pl.BlockSpec((length, 1), fixed),
            pl.BlockSpec((1, BLK), lambda i: (0, i)),
        ],
        out_specs=[
            pl.BlockSpec((BLK, q_heads * HEAD), row),
            pl.BlockSpec((length, 2 * kv_heads * HEAD), fixed),
        ],
        out_shape=[
            jax.ShapeDtypeStruct((length, q_heads * HEAD), BF16),
            jax.ShapeDtypeStruct((length, 2 * kv_heads * HEAD), BF16),
        ],
        scratch_shapes=[
            pltpu.VMEM((kv_heads, length, HEAD), F32),
            pltpu.VMEM((kv_heads, length, HEAD), F32),
        ],
        compiler_params=pltpu.CompilerParams(
            dimension_semantics=("arbitrary",), vmem_limit_bytes=VMEM_CAP
        ),
        cost_estimate=cost(
            flops=20 * length * 768 * q_heads * HEAD,
            transcendentals=length * 640 * q_heads,
            bytes_accessed=8 * length * q_heads * HEAD,
        ),
        name="attn_bwd",
    )(do, q, k, v, att, lse, cosine, sine, kdoc, qdoc)


def mid_kernel(
    att_ref, wo_ref, tok_ref, gain_ref, small_ref, routes_ref, mid_ref, nm_ref, gate_ref, flat_ref
):
    att = jnp.concatenate([att_ref[k] for k in range(att_ref.shape[0])], 1)
    flat_ref[...] = att
    branch = nt(att, wo_ref[...])
    middle = tok_ref[...].astype(F32) + RESID * branch
    mid_ref[...] = middle
    inv = lax.rsqrt(jnp.mean(middle * middle, -1, keepdims=True) + EPS)
    nm = (middle * inv * gain_ref[...]).astype(BF16)
    nm_ref[...] = nm
    logits = nn(nm, small_ref[...])
    lane = lax.broadcasted_iota(jnp.int32, logits.shape, 1)
    chosen = lane == routes_ref[:, 0:1]
    for c in range(1, routes_ref.shape[1]):
        chosen = chosen | (lane == routes_ref[:, c : c + 1])
    logits = jnp.where(chosen, logits, NEG)
    e = jnp.exp(logits - jnp.max(logits, -1, keepdims=True))
    gate_ref[...] = e / jnp.sum(e, -1, keepdims=True)


def mid_fwd(att_all, wo_rows, tokens, gain, pack, small_at, routes):
    length, width = tokens.shape
    parts, _, cols = att_all.shape
    blocks = length // BLK
    fixed = lambda i: (0, 0)
    row = lambda i: (i, 0)
    return pl.pallas_call(
        mid_kernel,
        grid=(blocks,),
        in_specs=[
            pl.BlockSpec((parts, BLK, cols), lambda i: (0, i, 0)),
            pl.BlockSpec((width, parts * cols), fixed),
            pl.BlockSpec((BLK, width), row),
            pl.BlockSpec((1, width), fixed),
            pl.BlockSpec((width, 128), lambda i: (0, small_at)),
            pl.BlockSpec((BLK, routes.shape[1]), row),
        ],
        out_specs=[
            pl.BlockSpec((BLK, width), row),
            pl.BlockSpec((BLK, width), row),
            pl.BlockSpec((BLK, 128), row),
            pl.BlockSpec((BLK, parts * cols), row),
        ],
        out_shape=[
            jax.ShapeDtypeStruct((length, width), F32),
            jax.ShapeDtypeStruct((length, width), BF16),
            jax.ShapeDtypeStruct((length, 128), F32),
            jax.ShapeDtypeStruct((length, parts * cols), BF16),
        ],
        compiler_params=pltpu.CompilerParams(
            dimension_semantics=("arbitrary",), vmem_limit_bytes=VMEM_CAP
        ),
        cost_estimate=cost(
            flops=2 * length * width * cols * parts,
            transcendentals=length * 128,
            bytes_accessed=10 * length * width + 2 * width * cols * parts,
        ),
        name="mid_fwd",
    )(att_all, wo_rows, tokens, gain, pack, routes)


def norm_back(n_grad, values, gain):
    inv = lax.rsqrt(jnp.mean(values * values, -1, keepdims=True) + EPS)
    scaled = n_grad * gain
    return inv * (scaled - values * (inv * inv) * jnp.mean(scaled * values, -1, keepdims=True))


def back_mid_kernel(
    own_ref, back_ref, recv_ref, lg_ref, small_ref, mid_ref, gain_ref, cot_ref, wo_ref, ag_ref, p_ref
):
    n_grad = back_ref[...].astype(F32) + recv_ref[...].astype(F32) + nt(lg_ref[...], small_ref[...])
    grad = norm_back(n_grad, mid_ref[...], gain_ref[...])
    own = (pl.program_id(0) == own_ref[0]).astype(F32)
    ag = (RESID * (grad + own * cot_ref[...].astype(F32))).astype(BF16)
    ag_ref[...] = ag
    out = nn(ag, wo_ref[...]).astype(BF16)
    cols = p_ref.shape[2]
    for k in range(p_ref.shape[0]):
        p_ref[k] = out[:, k * cols : (k + 1) * cols]


def back_mid(own, back, recv, logit_grad, pack, small_at, middle, gain, cot, wo_rows, parts):
    length, width = middle.shape
    blocks = length // BLK
    cols = wo_rows.shape[1] // parts
    fixed = lambda i, o: (0, 0)
    row = lambda i, o: (i, 0)
    return pl.pallas_call(
        back_mid_kernel,
        grid_spec=pltpu.PrefetchScalarGridSpec(
            num_scalar_prefetch=1,
            grid=(blocks,),
            in_specs=[
                pl.BlockSpec((BLK, width), row),
                pl.BlockSpec((BLK, width), row),
                pl.BlockSpec((BLK, 128), row),
                pl.BlockSpec((width, 128), lambda i, o: (0, small_at)),
                pl.BlockSpec((BLK, width), row),
                pl.BlockSpec((1, width), fixed),
                pl.BlockSpec((BLK, width), fixed),
                pl.BlockSpec((width, parts * cols), fixed),
            ],
            out_specs=[
                pl.BlockSpec((BLK, width), row),
                pl.BlockSpec((parts, BLK, cols), lambda i, o: (0, i, 0)),
            ],
        ),
        out_shape=[
            jax.ShapeDtypeStruct((length, width), BF16),
            jax.ShapeDtypeStruct((parts, length, cols), BF16),
        ],
        compiler_params=pltpu.CompilerParams(
            dimension_semantics=("arbitrary",), vmem_limit_bytes=VMEM_CAP
        ),
        cost_estimate=cost(
            flops=2 * length * width * cols * parts,
            transcendentals=0,
            bytes_accessed=12 * length * width + 2 * width * cols * parts,
        ),
        name="back_mid",
    )(own, back, recv, logit_grad, pack, middle, gain, cot, wo_rows)


def back_end_kernel(dq_ref, dkv_ref, w_ref, tok_ref, gain_ref, ag_ref, out_ref):
    d_all = jnp.concatenate([dq_ref[...], dkv_ref[...]], 1)
    n_grad = nt(d_all, w_ref[...])
    grad = norm_back(n_grad, tok_ref[...].astype(F32), gain_ref[...])
    out_ref[...] = (grad + ag_ref[...].astype(F32) * (1.0 / RESID)).astype(BF16)


def back_end(dq, dkv, pack, tokens, gain, ag):
    length, width = tokens.shape
    cols = dq.shape[1] + dkv.shape[1]
    fixed = lambda i: (0, 0)
    row = lambda i: (i, 0)
    return pl.pallas_call(
        back_end_kernel,
        grid=(length // BLK,),
        in_specs=[
            pl.BlockSpec((BLK, dq.shape[1]), row),
            pl.BlockSpec((BLK, dkv.shape[1]), row),
            pl.BlockSpec((width, cols), fixed),
            pl.BlockSpec((BLK, width), row),
            pl.BlockSpec((1, width), fixed),
            pl.BlockSpec((BLK, width), row),
        ],
        out_specs=pl.BlockSpec((BLK, width), row),
        out_shape=jax.ShapeDtypeStruct((length, width), BF16),
        compiler_params=pltpu.CompilerParams(
            dimension_semantics=("arbitrary",), vmem_limit_bytes=VMEM_CAP
        ),
        cost_estimate=cost(
            flops=2 * length * width * cols,
            transcendentals=0,
            bytes_accessed=6 * length * width + 2 * width * cols,
        ),
        name="back_end",
    )(dq, dkv, pack, tokens, gain, ag)


def sigmoid(value):
    return 0.5 * jnp.tanh(0.5 * value) + 0.5


def gate_cols(gates, first):
    lane = lax.broadcasted_iota(jnp.int32, gates.shape, 1)
    return [
        jnp.sum(jnp.where(lane == first + k, gates, 0.0), -1, keepdims=True) for k in range(2)
    ]


def moe_fwd_kernel(base_ref, x_ref, w_ref, gate_ref, h_ref, gact_ref):
    p = pl.program_id(1)
    h = nn(x_ref[...], w_ref[...])
    h_ref[...] = h.astype(BF16)
    cols = gate_cols(gate_ref[...], base_ref[0] + 2 * p)
    for k in range(2):
        gate = h[:, 256 * k : 256 * k + 128]
        up = h[:, 256 * k + 128 : 256 * k + 256]
        act = gate * sigmoid(gate) * up
        gact_ref[:, 128 * k : 128 * k + 128] = (cols[k] * act).astype(BF16)


def moe_fwd(base, x, w_in, gates, rows, scale):
    length, width = x.shape
    cols = w_in.shape[1]
    return pl.pallas_call(
        moe_fwd_kernel,
        grid_spec=pltpu.PrefetchScalarGridSpec(
            num_scalar_prefetch=1,
            grid=(length // rows, cols // 512),
            in_specs=[
                pl.BlockSpec((rows, width), lambda i, p, b: (i, 0)),
                pl.BlockSpec((width, 512), lambda i, p, b: (0, p)),
                pl.BlockSpec((rows, 128), lambda i, p, b: (i, 0)),
            ],
            out_specs=[
                pl.BlockSpec((rows, 512), lambda i, p, b: (i, p)),
                pl.BlockSpec((rows, 256), lambda i, p, b: (i, p)),
            ],
        ),
        out_shape=[
            jax.ShapeDtypeStruct((length, cols), BF16),
            jax.ShapeDtypeStruct((length, cols // 2), BF16),
        ],
        compiler_params=pltpu.CompilerParams(
            dimension_semantics=("arbitrary", "arbitrary"), vmem_limit_bytes=VMEM_CAP
        ),
        cost_estimate=cost(
            flops=2 * length * width * cols,
            transcendentals=length * cols // 2,
            bytes_accessed=2 * length * (width + cols + cols // 2) + 4 * width * cols,
            scale=scale,
        ),
        name="moe_fwd",
    )(base, x, w_in, gates)


def combine_kernel(*refs):
    gact_ref, pieces, out_ref, w_scr = refs[0], refs[1:-2], refs[-2], refs[-1]

    @pl.when(pl.program_id(0) == 0)
    def _():
        at = 0
        for piece in pieces:
            w_scr[at : at + piece.shape[0], :] = piece[...]
            at += piece.shape[0]

    out_ref[...] = nt(gact_ref[...], w_scr[...]).astype(BF16)


def combine(gact, pieces, rows):
    length, cols = gact.shape
    width = sum(p.shape[0] for p in pieces)
    return pl.pallas_call(
        combine_kernel,
        grid=(length // rows,),
        in_specs=[pl.BlockSpec((rows, cols), lambda i: (i, 0))]
        + [pl.BlockSpec(p.shape, lambda i: (0, 0)) for p in pieces],
        out_specs=pl.BlockSpec((rows, width), lambda i: (i, 0)),
        out_shape=jax.ShapeDtypeStruct((length, width), BF16),
        scratch_shapes=[pltpu.VMEM((width, cols), BF16)],
        compiler_params=pltpu.CompilerParams(
            dimension_semantics=("arbitrary",), vmem_limit_bytes=VMEM_CAP
        ),
        cost_estimate=cost(
            flops=2 * length * width * cols,
            transcendentals=0,
            bytes_accessed=2 * (length * width + length * cols + width * cols),
        ),
        name="combine",
    )(gact, *pieces)


def moe_bwd_kernel(*refs):
    base_ref, g_ref, gate_ref, h_ref = refs[:4]
    pieces, gug_ref, choice_ref, plain_scr = refs[4:-3], refs[-3], refs[-2], refs[-1]
    p = pl.program_id(1)
    first = base_ref[0] + 2 * (p - 1)
    plain = plain_scr[1 - p % 2]
    cols = gate_cols(gate_ref[...], first)
    lane = lax.broadcasted_iota(jnp.int32, choice_ref.shape, 1)
    add = jnp.zeros(choice_ref.shape, F32)
    for k in range(2):
        gate = h_ref[:, 256 * k : 256 * k + 128].astype(F32)
        up = h_ref[:, 256 * k + 128 : 256 * k + 256].astype(F32)
        part = plain[:, 128 * k : 128 * k + 128]
        sig = sigmoid(gate)
        silu = gate * sig
        add = jnp.where(lane == first + k, jnp.sum(silu * up * part, -1, keepdims=True), add)
        act_grad = cols[k] * part
        gug_ref[:, 256 * k : 256 * k + 128] = (act_grad * up * (sig + silu * (1.0 - sig))).astype(
            BF16
        )
        gug_ref[:, 256 * k + 128 : 256 * k + 256] = (act_grad * silu).astype(BF16)
    choice_ref[...] = jnp.where(p > 1, choice_ref[...], 0.0) + jnp.where(p > 0, add, 0.0)
    weights = [piece[...] for piece in pieces]
    plain_scr[p % 2] = nn(g_ref[...], weights[0] if len(weights) == 1 else jnp.concatenate(weights, 0))


def moe_bwd(base, g, pieces, gates, h, rows):
    length, width = g.shape
    cols = h.shape[1]
    steps = cols // 512
    behind = lambda i, p, b: (i, jnp.maximum(p - 1, 0))
    return pl.pallas_call(
        moe_bwd_kernel,
        grid_spec=pltpu.PrefetchScalarGridSpec(
            num_scalar_prefetch=1,
            grid=(length // rows, steps + 1),
            in_specs=[
                pl.BlockSpec((rows, width), lambda i, p, b: (i, 0)),
                pl.BlockSpec((rows, 128), lambda i, p, b: (i, 0)),
                pl.BlockSpec((rows, 512), behind),
            ]
            + [
                pl.BlockSpec((w.shape[0], 256), lambda i, p, b: (0, jnp.minimum(p, steps - 1)))
                for w in pieces
            ],
            out_specs=[
                pl.BlockSpec((rows, 512), behind),
                pl.BlockSpec((rows, 128), lambda i, p, b: (i, 0)),
            ],
            scratch_shapes=[pltpu.VMEM((2, rows, 256), F32)],
        ),
        out_shape=[
            jax.ShapeDtypeStruct((length, cols), BF16),
            jax.ShapeDtypeStruct((length, 128), F32),
        ],
        compiler_params=pltpu.CompilerParams(
            dimension_semantics=("arbitrary", "arbitrary"), vmem_limit_bytes=VMEM_CAP
        ),
        cost_estimate=cost(
            flops=length * width * cols,
            transcendentals=length * cols // 2,
            bytes_accessed=2 * length * (width + 2 * cols) + 2 * width * cols,
        ),
        name="moe_bwd",
    )(base, g, gates, h, *pieces)


def segment_kernel(*refs, count):
    lefts, rights, outs = refs[:4], refs[4:6], refs[6:]
    first = tn(jnp.concatenate([lefts[0][...], lefts[1][...]], 1), rights[0][...])
    second = tn(jnp.concatenate([lefts[2][...], lefts[3][...]], 1), rights[1][...])
    value = (first + second).astype(BF16)
    for k in range(count):

        @pl.when(pl.program_id(0) == k)
        def _(k=k):
            outs[k][...] = value


def pick(s, values):
    out = values[0]
    for k in range(1, len(values)):
        out = jnp.where(s == k, values[k], out)
    return out


def weight_grad(left, left2, right, right2, segments):
    length, width = left.shape
    cols = right.shape[1] // 2
    quarter = width // 4
    wide = min(cols, 768)
    steps = cols // wide
    count = len(segments)
    firsts, seconds, halves = zip(*segments, strict=True)
    one = pl.BlockSpec((length, quarter), lambda s, j: (0, pick(s, firsts)))
    two = pl.BlockSpec((length, quarter), lambda s, j: (0, pick(s, seconds)))
    side = pl.BlockSpec((length, wide), lambda s, j: (0, pick(s, halves) * steps + j))

    def place(k):
        return pl.BlockSpec(
            (2 * quarter, wide),
            lambda s, j: (0, jnp.where(s == k, j, jnp.where(s < k, 0, steps - 1))),
        )

    return pl.pallas_call(
        functools.partial(segment_kernel, count=count),
        grid=(count, steps),
        in_specs=[one, two, one, two, side, side],
        out_specs=[place(k) for k in range(count)],
        out_shape=[jax.ShapeDtypeStruct((2 * quarter, cols), BF16)] * count,
        compiler_params=pltpu.CompilerParams(
            dimension_semantics=("arbitrary", "arbitrary"), vmem_limit_bytes=VMEM_CAP
        ),
        cost_estimate=cost(
            flops=2 * count * length * width * cols,
            transcendentals=0,
            bytes_accessed=4 * length * (width + 2 * cols),
            scale=100,
        ),
        name="weight_grad",
    )(left, left, left2, left2, right, right2)


def swap(value, axis, bit, size):
    return lax.ppermute(value, axis, [(i, i ^ bit) for i in range(size)])


def reorder(value, q, quads):
    if quads != 4:
        return value
    n = value.shape[-1] // 4
    b = [value[..., k * n : (k + 1) * n] for k in (0, 1, 3, 2)]
    odd = (q & 1) == 1
    far = (q & 2) == 2
    c = [jnp.where(odd, b[k], b[j]) for j, k in ((0, 1), (1, 0), (2, 3), (3, 2))]
    return jnp.concatenate([jnp.where(far, c[k], c[j]) for j, k in ((0, 3), (1, 2), (2, 1), (3, 0))], -1)


def restore(value, q, quads):
    if quads != 4:
        return value
    n = value.shape[-1] // 4
    b = [value[..., k * n : (k + 1) * n] for k in (0, 1, 3, 2)]
    odd = (q & 1) == 1
    far = (q & 2) == 2
    c = [jnp.where(odd, b[k ^ 1], b[k]) for k in range(4)]
    return jnp.concatenate([jnp.where(far, c[k ^ 2], c[k]) for k in range(4)], -1)


def gather_first(low, high, quads):
    if quads != 4:
        return (lax.all_gather(jnp.concatenate([low, high], 0), "q", axis=0, tiled=True),)
    return swap(low, "q", 1, 4), swap(high, "q", 2, 4)


def gather_rest(low, high, quads):
    if quads != 4:
        return ()
    return swap(high, "q", 1, 4), swap(low, "q", 2, 4)


def gather_diagonal(first, quads):
    if quads != 4:
        return ()
    return swap(first[0], "q", 2, 4), swap(first[1], "q", 1, 4)


def gather_join(low, high, first, rest, diagonal, quads):
    if quads != 4:
        return first[0]
    return jnp.concatenate(
        [low, high, first[0], rest[0], diagonal[0], diagonal[1], rest[1], first[1]], 0
    )


def gather_pieces(low, high, first, rest, diagonal, quads):
    if quads != 4:
        return first
    return (low, high, first[0], rest[0], diagonal[0], diagonal[1], rest[1], first[1])


def gather_rows(low, high, quads):
    first = gather_first(low, high, quads)
    rest = gather_rest(low, high, quads)
    return gather_join(low, high, first, rest, gather_diagonal(first, quads), quads)


SEND_LEFT, SEND_RIGHT, KEEP_LEFT, KEEP_RIGHT = (2, 3, 0), (2, 1, 1), (0, 1, 0), (0, 3, 1)


def cut(value, segment):
    n, half = value.shape[0] // 4, (value.shape[1] // 2 + 127) // 128 * 128
    side = value[:, half:] if segment[2] else value[:, :half]
    return jnp.concatenate([side[k * n : (k + 1) * n] for k in segment[:2]], 0)


def scatter_first(left, right):
    return swap(left, "q", 2, 4), swap(right, "q", 1, 4)


def scatter_second(keep_left, keep_right, from_y, from_x):
    n = keep_left.shape[0] // 2
    give_x = (keep_left[n:].astype(F32) + from_y[:n].astype(F32)).astype(BF16)
    give_y = (keep_right[n:].astype(F32) + from_x[:n].astype(F32)).astype(BF16)
    give_x, give_y = lax.optimization_barrier((give_x, give_y))
    arrived = swap(give_x, "q", 1, 4), swap(give_y, "q", 2, 4)
    return arrived, (give_x, give_y)


def scatter_last(keep_left, keep_right, from_y, from_x, arrived, *others):
    n = keep_left.shape[0] // 2
    keep_left, keep_right, from_y, from_x, left, right = all_after(
        (keep_left, keep_right, from_y, from_x, *arrived), *others
    )
    return (
        (keep_left[:n].astype(F32) + from_y[n:].astype(F32) + left.astype(F32)).astype(BF16),
        (keep_right[:n].astype(F32) + from_x[n:].astype(F32) + right.astype(F32)).astype(BF16),
    )


def small_first(value):
    n = value.shape[0] // 4
    return swap(value[n : 3 * n], "q", 1, 4)


def small_second(value, got):
    n = value.shape[0] // 4
    give = (value[3 * n :].astype(F32) + got[n:].astype(F32)).astype(BF16)
    return swap(lax.optimization_barrier(give), "q", 2, 4)


def small_last(value, got, late):
    n = value.shape[0] // 4
    value, got, late = lax.optimization_barrier((value, got, late))
    return (value[:n].astype(F32) + got[:n].astype(F32) + late.astype(F32)).astype(BF16)


def scatter_plain(value):
    total = lax.psum_scatter(value, "q", scatter_dimension=0, tiled=True)
    half = total.shape[1] // 2
    return total[:, :half], total[:, half:]


def after(value, *others):
    return lax.optimization_barrier((value, *others))[0]


def all_after(values, *others):
    return lax.optimization_barrier((*values, *others))[: len(values)]


def to_halves(mine, give, c):
    other = swap(give, "c", 1, 2)
    first = c == 0
    return jnp.where(first, mine, other), jnp.where(first, other, mine)


def part_halves(totals, rows, c):
    def take(at):
        return jnp.concatenate([lax.dynamic_slice_in_dim(t, at * rows, rows, 0) for t in totals], 1)

    return take(c), take(1 - c)


def from_halves(totals, rows, c):
    mine, give = part_halves(totals, rows, c)
    return mine, swap(give, "c", 1, 2)


def in_order(mine, other, c):
    return jnp.where(c == 0, mine, other), jnp.where(c == 0, other, mine)


def column_halves(value, c):
    n = value.shape[1] // 2
    mine = jnp.where(c == 0, value[:, :n], value[:, n:])
    give = jnp.where(c == 0, value[:, n:], value[:, :n])
    return mine, give


def whole_columns(half, c):
    other = swap(half, "c", 1, 2)
    return jnp.where(c == 0, half, other), jnp.where(c == 0, other, half)


def body(
    tokens, attn_gain, w_query, key_weight, value_weight, w_output, router, moe_gain, w_in, w_out,
    segments, routes, cotangent, *, quads,
):
    q = lax.axis_index("q")
    c = lax.axis_index("c")
    m = lax.axis_index("mp")
    length = segments.shape[1]
    width = tokens.shape[2]
    rows = w_query.shape[0]
    experts = router.shape[1]
    half_e = experts // 2
    ff = w_out.shape[2]
    q_heads = w_query.shape[1] // HEAD
    kv_heads = key_weight.shape[1] // HEAD
    q_cols, kv_cols = q_heads * HEAD, kv_heads * HEAD
    qkv_cols = q_cols + 2 * kv_cols
    mp = lax.axis_size("mp")

    tok_own = reorder(tokens[0], q, quads)
    tok_all = lax.all_gather(tok_own, "mp", axis=0, tiled=True)

    def half_rows(value):
        mine = lax.dynamic_slice_in_dim(value, c * half_e, half_e, 1).reshape(rows, -1)
        give = lax.dynamic_slice_in_dim(value, (1 - c) * half_e, half_e, 1).reshape(rows, -1)
        return to_halves(mine, give, c), mine, give

    in_pair, in_kept, in_gave = half_rows(w_in)

    pad = jnp.zeros((rows, 128 - experts - 2), BF16)
    pack = jnp.concatenate(
        [w_query, key_weight, value_weight, router, attn_gain[:, None], moe_gain[:, None], pad], 1
    )
    pack_pair = to_halves(*column_halves(after(pack, in_gave, in_kept), c), c)
    pack_pair = all_after(pack_pair, *in_pair)
    pack_first = gather_first(*pack_pair, quads)
    pack_rest = gather_rest(*pack_pair, quads)
    pack_half = gather_join(
        *pack_pair, pack_first, pack_rest, gather_diagonal(pack_first, quads), quads
    )
    pack = jnp.concatenate(whole_columns(pack_half, c), 1)
    small_at = qkv_cols // 128
    gains = pack[:, qkv_cols + experts : qkv_cols + experts + 2].astype(F32)
    attn_g = gains[:, 0].reshape(1, width)
    moe_g = gains[:, 1].reshape(1, width)

    doc_row = segments
    doc_col = segments.reshape(length, 1)
    lane = jnp.arange(128, dtype=jnp.int32) % (HEAD // 2)
    freq = ROPE_BASE ** (-lane.astype(F32) * 2.0 / HEAD)
    angles = jnp.arange(length).astype(F32)[:, None] * freq[None, :]
    cosine = jnp.cos(angles)
    upper = (jnp.arange(128, dtype=jnp.int32) % HEAD) < (HEAD // 2)
    sine = jnp.where(upper[None, :], -jnp.sin(angles), jnp.sin(angles))

    out_pair, _, _ = half_rows(after(w_out, *pack_pair))
    in_src = in_pair
    in_got = gather_first(*in_src, quads)
    in_rest = gather_rest(*in_src, quads)

    normed_a, q_r, k_r, v_r, attended, lse = attn_fwd(
        tok_all, attn_g, pack, cosine, sine, doc_col, doc_row, q_heads, kv_heads
    )

    wo_pad = jnp.concatenate([w_output, jnp.zeros((rows, 5 * 64), BF16)], 1)
    wo_cols = lax.all_gather(after(wo_pad, pack), "mp", axis=0, tiled=False)
    wo_cols = jnp.concatenate([wo_cols[j, :, :q_cols] for j in range(mp)], 1)
    wo_pair = to_halves(*column_halves(after(wo_cols, attended), c), c)
    in_diag = gather_diagonal(in_got, quads)
    wo_src = all_after(wo_pair, *in_diag)
    wo_got, wo_rest = gather_first(*wo_src, quads), gather_rest(*wo_src, quads)
    out_src = all_after(out_pair, *wo_got, *wo_rest)
    out_got, out_rest = gather_first(*out_src, quads), gather_rest(*out_src, quads)
    wo_half = gather_join(*wo_src, wo_got, wo_rest, gather_diagonal(wo_got, quads), quads)
    step = width // 4
    wo_other = jnp.concatenate(
        [swap(wo_half[k * step : (k + 1) * step], "c", 1, 2) for k in range(4)], 0
    )
    wo_rows = jnp.concatenate(in_order(*lax.optimization_barrier((wo_half, wo_other)), c), 1)
    join = (*in_src, *in_got, *in_rest, *in_diag)
    join = all_after(join, *wo_got)
    in_full = gather_join(
        *join[:2], join[2 : 2 + len(in_got)], join[2 + len(in_got) : 2 + len(in_got) + len(in_rest)],
        join[2 + len(in_got) + len(in_rest) :], quads,
    )

    att_all = lax.all_gather(after(attended, *in_got, *in_rest, *out_pair), "mp", axis=0, tiled=False)
    middle, normed_m, gates, att_flat = mid_fwd(
        after(att_all, in_full, out_got[0]), wo_rows, tok_all, moe_g, pack, small_at, routes[0]
    )

    cot_own = lax.optimization_barrier(reorder(cotangent[0], q, quads))
    moe_grad = (RESID * cot_own.astype(F32)).astype(BF16)
    grad_all = lax.all_gather(after(moe_grad, attended), "mp", axis=0, tiled=True)

    x_own = normed_m
    x_other = swap(normed_m, "c", 1, 2)
    gates_other = swap(gates, "c", 1, 2)
    base = (c * half_e).astype(jnp.int32).reshape(1)
    hid_own, gact_own = moe_fwd(
        base, x_own, in_full, gates, length, 100
    )
    x_other = after(x_other, gact_own, out_got[-1])
    out_diag = gather_diagonal(all_after(out_got, gact_own), quads)
    out_full = gather_pieces(*out_src, out_got, out_rest, out_diag, quads)
    hid_other, gact_other = moe_fwd(base, x_other, in_full, gates_other, length, 1)
    comb_give = combine(gact_other, out_full, length // 2)
    comb_recv = swap(comb_give, "c", 1, 2)
    comb_own = combine(after(gact_own, comb_give, grad_all), out_full, length // 2)
    combined = (comb_own.astype(F32) + comb_recv.astype(F32)).astype(BF16)
    moe_low = lax.psum_scatter(combined, "mp", scatter_dimension=0, tiled=True)

    g_other = swap(after(grad_all, comb_give), "c", 1, 2)
    gacts = all_after((gact_own, gact_other), comb_own)
    if quads == 4:
        out_send = weight_grad(
            grad_all, g_other, *gacts, (SEND_LEFT, SEND_RIGHT, KEEP_LEFT, KEEP_RIGHT)
        )
        out_keep = out_send[2:]
        out_move = scatter_first(*out_send[:2])
    else:
        g2, gact2 = jnp.concatenate([grad_all, g_other], 0), jnp.concatenate(gacts, 0)
        out_move = out_keep = (tn(g2, gact2).astype(BF16),)
    gug_own, choice_own = moe_bwd(
        base, grad_all, out_full, gates, after(hid_own, *out_keep), length
    )
    gug_other, choice_other = moe_bwd(base, g_other, out_full, gates_other, after(hid_other, gug_own), length)
    choice = choice_own + swap(choice_other, "c", 1, 2)
    back_give = nt(after(gug_other, *out_move), in_full).astype(BF16)
    back_recv = swap(back_give, "c", 1, 2)
    gug_late = after(gug_own, back_give)
    back_own = nt(gug_late, in_full).astype(BF16)
    gates_c = gates * choice
    logit_grad = (gates_c - gates * jnp.sum(gates_c, -1, keepdims=True)).astype(BF16)
    out_late = scatter_second(*out_keep, *out_move)[0] if quads == 4 else ()
    ag, p_part = back_mid(
        m.astype(jnp.int32).reshape(1), back_own, back_recv, logit_grad, pack, small_at,
        after(middle, moe_low, *out_late), moe_g, cot_own, wo_rows, mp,
    )
    attended_grad = lax.psum_scatter(p_part, "mp", scatter_dimension=0, tiled=False)

    gugs = all_after((gug_own, gug_other), ag)
    if quads == 4:
        in_send = weight_grad(x_own, x_other, *gugs, (SEND_LEFT, SEND_RIGHT))
        in_move = scatter_first(*in_send)
        in_keep = weight_grad(
            x_own, x_other, *all_after(gugs, *in_send), (KEEP_LEFT, KEEP_RIGHT)
        )
    else:
        in_move = in_keep = (tn(jnp.concatenate([x_own, x_other], 0), jnp.concatenate(gugs, 0)).astype(BF16),)
    att_late = after(att_flat, *in_send) if quads == 4 else att_flat
    half_cols = att_flat.shape[1] // 2
    low_att, high_att = att_late[:, :half_cols], att_late[:, half_cols:]
    wo_give = tn(ag, jnp.where(c == 0, high_att, low_att)).astype(BF16)
    wo_mine = tn(ag, after(jnp.where(c == 0, low_att, high_att), wo_give)).astype(BF16)
    wo_part = (wo_mine.astype(F32) + swap(wo_give, "c", 1, 2).astype(F32)).astype(BF16)
    if quads == 4:
        wo_keep = (cut(wo_part, KEEP_LEFT), cut(wo_part, KEEP_RIGHT))
        wo_move = scatter_first(cut(wo_part, SEND_LEFT), cut(wo_part, SEND_RIGHT))
    dq, dkv = attn_bwd(
        attended_grad, q_r, k_r, v_r, attended, lse, cosine, sine, doc_col, doc_row
    )
    end_part = back_end(dq, dkv, pack, tok_all, attn_g, ag)
    grad_tokens = lax.psum_scatter(end_part, "mp", scatter_dimension=0, tiled=True).astype(F32)

    layer_out = (
        lax.dynamic_slice_in_dim(middle, m * (length // mp), length // mp, 0) + RESID * after(moe_low, end_part).astype(F32)
    ).astype(BF16)

    given = (end_part,)
    if quads == 4:
        in_move = all_after(in_move, end_part)
        in_late, given = scatter_second(*in_keep, *in_move)
        wo_move = all_after(wo_move, *given)
        wo_late, _ = scatter_second(*wo_keep, *wo_move)
    dq_late, dkv_late = after(dq, *given), after(dkv, *given)
    part = jnp.concatenate(
        [tn(normed_a, dq_late), tn(normed_a, dkv_late), tn(normed_m, after(logit_grad, *given))], 1
    ).astype(BF16)
    mine, give = column_halves(part, c)
    pair = (mine.astype(F32) + swap(give, "c", 1, 2).astype(F32)).astype(BF16)
    if quads == 4:
        pair_move = small_first(pair)
        in_sum = scatter_last(*in_keep, *in_move, in_late)
        in_mine, in_give = part_halves(in_sum, rows, c)
        pair_move, in_give = lax.optimization_barrier((pair_move, in_give))
        in_other = swap(in_give, "c", 1, 2)
        pair_late = small_second(pair, pair_move)
        wo_sum = scatter_last(*wo_keep, *wo_move, wo_late, pair_move)
        pair_sum = (small_last(pair, pair_move, pair_late),)
        out_sum = scatter_last(*out_keep, *out_move, out_late, end_part)
    else:
        in_sum, wo_sum, pair_sum, out_sum = (
            scatter_plain(v) for v in (in_keep[0], wo_part, pair, out_keep[0])
        )
        in_mine, in_other = from_halves(in_sum, rows, c)
    late_sum = (*wo_sum, *pair_sum)
    late_mine, late_other = from_halves(late_sum, rows, c)
    wo_cols_here = wo_part.shape[1]
    wo_own_rows = jnp.concatenate(
        in_order(late_mine[:, :wo_cols_here], late_other[:, :wo_cols_here], c), 1
    )
    sums = jnp.concatenate(
        in_order(late_mine[:, wo_cols_here:], late_other[:, wo_cols_here:], c), 1
    ).astype(F32)
    grad_query = sums[:, :q_cols]
    grad_key = sums[:, q_cols : q_cols + kv_cols]
    grad_value = sums[:, q_cols + kv_cols : qkv_cols]
    router_part = sums[:, qkv_cols : qkv_cols + experts]

    out_mine, out_other = from_halves(out_sum, rows, c)
    grad_in = jnp.concatenate(in_order(in_mine, in_other, c), 1).astype(F32)
    grad_out = jnp.concatenate(in_order(out_mine, out_other, c), 1).astype(F32)

    attn_gain_part = (
        jnp.sum(grad_query * w_query.astype(F32), 1)
        + jnp.sum(grad_key * key_weight.astype(F32), 1)
        + jnp.sum(grad_value * value_weight.astype(F32), 1)
    ) / attn_gain.astype(F32)
    moe_gain_part = (
        jnp.sum(in_mine.astype(F32) * in_kept.astype(F32), 1)
        + jnp.sum(in_other.astype(F32) * in_gave.astype(F32), 1)
        + jnp.sum(router_part * router.astype(F32), 1)
    ) / moe_gain.astype(F32)
    total = jnp.concatenate(
        [router_part, attn_gain_part[:, None], moe_gain_part[:, None], jnp.zeros((rows, 128 - experts - 2), F32)], 1
    )
    tiny = total.astype(BF16)
    grad_output = lax.dynamic_slice_in_dim(wo_own_rows, m * q_cols, q_cols, 1).astype(F32)
    for k in range(1, mp):
        send = lax.dynamic_slice_in_dim(wo_own_rows, ((m + k) % mp) * q_cols, q_cols, 1)
        got = lax.ppermute(
            jnp.concatenate([send, tiny], 1), "mp", [(i, (i + k) % mp) for i in range(mp)]
        ).astype(F32)
        grad_output = grad_output + got[:, :q_cols]
        total = total + got[:, q_cols:]

    return (
        restore(layer_out, q, quads)[None],
        restore(grad_tokens, q, quads)[None],
        total[:, experts],
        grad_query,
        grad_key,
        grad_value,
        grad_output,
        total[:, :experts],
        total[:, experts + 1],
        grad_in.reshape(w_in.shape),
        grad_out.reshape(w_out.shape),
    )


def solution(mesh):
    dp, mp = mesh.shape["dp"], mesh.shape["mp"]
    quads = dp // 2
    split = Mesh(mesh.devices.reshape(quads, 2, mp), ("q", "c", "mp"))
    d = ("q", "c")
    placed = (
        P(d, "mp", None),
        P(d),
        P(d, "mp"),
        P(d, "mp"),
        P(d, "mp"),
        P(d, "mp"),
        P(d, None),
        P(d),
        P(d, None, None, "mp"),
        P(d, None, "mp"),
        P(d, None),
        P(d, None, None),
        P(d, "mp", None),
    )
    return jax.shard_map(
        functools.partial(body, quads=quads),
        mesh=split,
        in_specs=placed,
        out_specs=(
            P(d, "mp", None),
            P(d, "mp", None),
            P(d),
            P(d, "mp"),
            P(d, "mp"),
            P(d, "mp"),
            P(d, "mp"),
            P(d, None),
            P(d),
            P(d, None, None, "mp"),
            P(d, None, "mp"),
        ),
        check_vma=False,
    )
```
